32 devices in a mesh: sib: 2 (over core), row: 4 (over z), col: 4 (over y, x).
Axes of the slice: x: 2, y: 2, z: 4, core: 2. Of those that a mesh axis runs over, the one named last changes fastest.
Arguments:
- child_front: float32 [2, 2048, 2048], P('sib', 'row', 'col'), may hold values from -6 to 6
- child_panel: float32 [2, 2048, 1024], P('sib', ('row', 'col')), may hold values from -0.42 to 0.42
- block_map: int32 [2, 16], replicated, may hold values from 0 to 23, as said below
- parent_front: float32 [3072, 3072], P(('row', 'sib'), 'col'), may hold values from -6 to 6
- pivot_inverse: float32 [512, 512], replicated, may hold values from -0.03 to 0.1, as said below
Outputs:
- parent_out: float32 [3072, 3072], P(('row', 'sib'), 'col')
The draws below stay inside these ranges and needn't reach their ends.
Inputs may be any that keep to these rules, and one draw needn't show every extreme that they name: `block_map`: each row is strictly increasing. A child block i that lands in parent block g * 6 + k with 0 <= k < 6 satisfies g * 4 - 2 <= i < (g + 1) * 4; the lower end is met for g = 1 in every draw, and the last parent block is always named. `pivot_inverse`: lower triangular with diagonal entries from 0.05 to 0.1.
All inputs are finite; a program needn't handle non-finite values.
Results may differ from the reference program's by a relative error of at most 0.0001.
Values sent between devices are 32-bit elements; how exact they have to be, the bound alone decides.
No kernel may reach another device: no remote copies, remote signals or barrier semaphores. Data moves between devices by JAX's collectives and lax.ppermute only.
A program may use at most 64 MiB of HBM per device.

```python
import jax
import jax.numpy as jnp
from jax import lax

BLK = 128
CBD = 4
PIV = 4
KC = 1024
PBD = 6
HB = 2
NCB = 16
CHILD = 2048
PARENT = 3072
PANEL = 512


def sibling_map(key, groups):
    key_steps, key_slots = jax.random.split(key)
    group_index = jnp.arange(groups + 1, dtype=jnp.int32)
    raw_steps = jax.random.randint(key_steps, (groups + 1,), -HB, 1, dtype=jnp.int32)
    offsets = jnp.where((group_index == 0) | (group_index == groups), 0, jnp.where(group_index == 1, PBD - PIV - CBD, raw_steps))
    counts = CBD + offsets[1:] - offsets[:-1]
    slot_index = jnp.arange(PBD, dtype=jnp.int32)
    scores = jax.random.randint(key_slots, (groups, PBD), 0, 1 << 20, dtype=jnp.int32) * PBD + slot_index[None, :]
    row_group = jnp.arange(groups, dtype=jnp.int32)[:, None]
    forced = (row_group == groups - 1) & (slot_index[None, :] == PBD - 1)
    scores = jnp.where(forced, -1, scores)
    slot_ranks = jnp.argsort(jnp.argsort(scores, axis=1), axis=1)
    chosen_flat = (slot_ranks < counts[:, None]).reshape(-1)
    position = jnp.arange(groups * PBD, dtype=jnp.int32)
    sorted_slots = jnp.argsort(jnp.where(chosen_flat, position, position + groups * PBD))
    return sorted_slots[:NCB].astype(jnp.int32)


def draw_block_map(key, part):
    groups = NCB // CBD
    first_map = sibling_map(jax.random.fold_in(key, 11), groups)
    second_map = sibling_map(jax.random.fold_in(key, 12), groups)
    return jnp.stack([first_map, second_map])


def draw_pivot_inverse(key, part):
    key_diag, key_low = jax.random.split(jax.random.fold_in(key, 29))
    row_index = jnp.arange(PANEL)[:, None]
    col_index = jnp.arange(PANEL)[None, :]
    lower = 0.005 * jax.random.truncated_normal(key_low, -4.0, 4.0, (PANEL, PANEL), jnp.float32)
    diagonal = jax.random.uniform(key_diag, (PANEL,), jnp.float32, 0.05, 0.1)
    return jnp.where(row_index > col_index, lower, 0.0) + jnp.where(row_index == col_index, diagonal[:, None], 0.0)


def steps_of(key, extent, cuts, low, high):
    def one(dim, parts):
        draws = jax.random.uniform(jax.random.fold_in(jax.random.fold_in(key, 6), dim), (parts,), jnp.float32, low / len(cuts), high / len(cuts))
        return jnp.repeat(jnp.exp(draws), extent[dim] // parts).reshape((-1,) + (1,) * (len(extent) - dim - 1))

    gain = one(*cuts[0])
    for cut in cuts[1:]:
        gain = gain * one(*cut)
    return gain


def scatter_about(key, dims, scale, limit, shards=(), kind=jnp.bfloat16):
    drawn = scale * jax.random.normal(key, dims, jnp.float32)
    if shards:
        drawn = drawn * steps_of(key, dims, shards, -0.22, 0.18)
    return jnp.clip(drawn, -limit, limit).astype(kind)


def setup_inputs(seed: int = 0) -> dict:
    arg_keys = jax.random.split(jax.random.key(seed), 6)
    return {
        "child_front": scatter_about(arg_keys[0], (2, CHILD, CHILD), 1.0, 6.0, ((0, 2), (1, 4), (2, 4)), jnp.float32),
        "child_panel": scatter_about(arg_keys[1], (2, CHILD, KC), 0.07, 0.42, ((0, 2), (1, 16)), jnp.float32),
        "block_map": draw_block_map(jax.random.fold_in(arg_keys[5], 71), 0),
        "parent_front": scatter_about(arg_keys[3], (PARENT, PARENT), 1.0, 6.0, ((0, 8), (1, 4)), jnp.float32),
        "pivot_inverse": draw_pivot_inverse(jax.random.fold_in(arg_keys[5], 71), 0),
    }


def schur_child(front_block, panel_block):
    return front_block - jnp.dot(panel_block, panel_block.T, precision=lax.Precision.HIGHEST, preferred_element_type=jnp.float32)


def reference(child_front, child_panel, block_map, parent_front, pivot_inverse):
    child_order = child_front.shape[1]
    parent_order = parent_front.shape[0]
    child_blocks = child_order // BLK
    parent_blocks = parent_order // BLK
    assembled = parent_front.reshape(parent_blocks, BLK, parent_blocks, BLK).transpose(0, 2, 1, 3)
    for sibling in range(2):
        update = schur_child(child_front[sibling], child_panel[sibling])
        update_tiles = update.reshape(child_blocks, BLK, child_blocks, BLK).transpose(0, 2, 1, 3)
        rows_map = block_map[sibling].astype(jnp.int32)
        assembled = assembled.at[rows_map[:, None], rows_map[None, :]].add(update_tiles)
    assembled = assembled.transpose(0, 2, 1, 3).reshape(parent_order, parent_order)
    factor_rows = jnp.dot(assembled[:, :PANEL], pivot_inverse.T, precision=lax.Precision.HIGHEST, preferred_element_type=jnp.float32)
    lower_rows = factor_rows[PANEL:]
    trailing = assembled[PANEL:, PANEL:] - jnp.dot(lower_rows, lower_rows.T, precision=lax.Precision.HIGHEST, preferred_element_type=jnp.float32)
    result = assembled.at[PANEL:, PANEL:].set(trailing)
    return result.at[:, :PANEL].set(factor_rows)
```

```python
import jax
import jax.numpy as jnp
from jax import lax
from jax.experimental import pallas as pl
from jax.experimental.pallas import tpu as pltpu
from jax.sharding import PartitionSpec as P

BLK = 128
CBD = 4
PBD = 6
HB = 2
PIV = 4
PANEL = 512
HALF = PBD // 2
EDGE = HB * BLK


SMEM = pl.BlockSpec(memory_space=pltpu.SMEM)
VMEM = pl.BlockSpec(memory_space=pltpu.VMEM)
ANY = pl.BlockSpec(memory_space=pl.ANY)

ROW, COL, SIB = 0, 1, 2
OWN_ROWS, OTHER_ROWS, OWN_COLS, OTHER_COLS = 3, 9, 15, 21
OWN_PIVOT, OTHER_PIVOT = 27, 31


def f32(*shape):
    return jax.ShapeDtypeStruct(shape, jnp.float32)


def halves(value):
    high = value.astype(jnp.bfloat16)
    low = (value - high.astype(jnp.float32)).astype(jnp.bfloat16)
    return high, low


def times_transpose(left, right):
    def dot(x, y):
        return lax.dot_general(
            x, y, (((1,), (1,)), ((), ())), preferred_element_type=jnp.float32
        )

    return dot(left[0], right[0]) + (dot(left[0], right[1]) + dot(left[1], right[0]))


def rotated(value, axis, steps):
    count = lax.axis_size(axis)
    return lax.ppermute(value, axis, [(i, (i + steps) % count) for i in range(count)])


def swapped(value, axis, mask):
    count = lax.axis_size(axis)
    return lax.ppermute(value, axis, [(i, i ^ mask) for i in range(count)])


def shifted(value, axis):
    count = lax.axis_size(axis)
    return lax.ppermute(value, axis, [(i, i + 1) for i in range(count - 1)])


def shifted_both(value, count):
    pairs = [
        (r * count + c, (r + 1) * count + c + 1)
        for r in range(count - 1)
        for c in range(count - 1)
    ]
    return lax.ppermute(value, ("row", "col"), pairs)


def run_copies(copies):
    for copy in copies:
        copy.start()
    for copy in copies:
        copy.wait()


def span(index, size):
    return pl.ds(pl.multiple_of(index * size, size), size)


def gather_copies(table, pieces, target, sems, size, base=0):
    return [
        pltpu.make_async_copy(piece, target.at[span(table[COL] ^ k, size)], sems.at[base + k])
        for k, piece in enumerate(pieces)
    ]


def window_choice(block_row, group, parent_span):
    padded = jnp.concatenate([jnp.full((HB,), -1, jnp.int32), block_row])
    window = lax.dynamic_slice_in_dim(padded, group * CBD, CBD + HB)
    target = group * parent_span + jnp.arange(parent_span, dtype=jnp.int32)
    places = jnp.arange(1, CBD + HB + 1, dtype=jnp.int32)
    hit = window[None, :] == target[:, None]
    return jnp.sum(jnp.where(hit, places[None, :], 0), axis=1).astype(jnp.int32) - 1


def pivot_product(table, rows, col_pieces, front):
    count = len(rows)
    sub, depth = rows[0].shape
    width = front.shape[1]

    def body(*refs):
        sc = refs[0]
        row_refs = refs[1 : 1 + count]
        col_refs = refs[1 + count : 1 + 2 * count]
        front_ref, out, edge, row_buf, col_buf, sems = refs[1 + 2 * count :]
        for d in range(count):

            @pl.when(sc[ROW] == d)
            def _():
                pltpu.make_async_copy(col_refs[d], col_buf, sems.at[count]).start()

        run_copies(gather_copies(sc, row_refs, row_buf, sems, sub))
        pltpu.make_async_copy(col_refs[0], col_buf, sems.at[count]).wait()
        part = front_ref[...] - times_transpose(halves(row_buf[...]), halves(col_buf[...]))
        out[...] = part
        edge[...] = part[-EDGE:]

    return pl.pallas_call(
        body,
        in_specs=[SMEM] + [ANY] * (2 * count) + [VMEM],
        out_specs=[VMEM, VMEM],
        out_shape=[f32(count * sub, width), f32(EDGE, width)],
        scratch_shapes=[
            pltpu.VMEM((count * sub, depth), jnp.float32),
            pltpu.VMEM((sub, depth), jnp.float32),
            pltpu.SemaphoreType.DMA((count + 1,)),
        ],
        name="pivot_product",
    )(table, *rows, *col_pieces, front)


def update_product(table, rows, cols, front):
    count = len(rows)
    sub, depth = rows[0].shape
    size = count * sub

    def body(*refs):
        sc = refs[0]
        row_refs = refs[1 : 1 + count]
        col_refs = refs[1 + count : 1 + 2 * count]
        front_ref, out, right, up, corner, row_buf, col_buf, sems = refs[1 + 2 * count :]
        run_copies(
            gather_copies(sc, row_refs, row_buf, sems, sub)
            + gather_copies(sc, col_refs, col_buf, sems, sub, count)
        )
        part = front_ref[...] - times_transpose(halves(row_buf[...]), halves(col_buf[...]))
        out[...] = part
        right[...] = part[:, -EDGE:]
        up[...] = part[-EDGE:, :]
        corner[...] = part[-EDGE:, -EDGE:]

    return pl.pallas_call(
        body,
        in_specs=[SMEM] + [ANY] * (2 * count) + [VMEM],
        out_specs=[VMEM] * 4,
        out_shape=[f32(size, size), f32(size, EDGE), f32(EDGE, size), f32(EDGE, EDGE)],
        scratch_shapes=[
            pltpu.VMEM((size, depth), jnp.float32),
            pltpu.VMEM((size, depth), jnp.float32),
            pltpu.SemaphoreType.DMA((2 * count,)),
        ],
        name="update_product",
    )(table, *rows, *cols, front)


def pick_for_cols(table, pieces, own=None):
    count = len(pieces)
    shape = pieces[0].shape
    with_own = own is not None
    out_shape = (2,) + shape if with_own else shape

    def body(*refs):
        sc = refs[0]
        ins = refs[1 : 1 + count]
        own_ref = refs[1 + count] if with_own else None
        outs = refs[1 + count + with_own : 1 + 2 * count + with_own]
        sems = refs[-1]
        places = [out.at[1] if with_own else out for out in outs]
        fixed = []
        if with_own:
            fixed = [
                pltpu.make_async_copy(own_ref, out.at[0], sems.at[count + k])
                for k, out in enumerate(outs)
            ]
        for copy in fixed:
            copy.start()
        for k in range(count):
            wanted = lax.rem(sc[ROW] - (sc[COL] ^ k) + count, count)
            for d in range(count):

                @pl.when(wanted == d)
                def _():
                    pltpu.make_async_copy(ins[d], places[k], sems.at[k]).start()

        for k in range(count):
            pltpu.make_async_copy(ins[0], places[k], sems.at[k]).wait()
        for copy in fixed:
            copy.wait()

    extra = [own] if with_own else []
    return pl.pallas_call(
        body,
        in_specs=[SMEM] + [ANY] * (count + with_own),
        out_specs=[ANY] * count,
        out_shape=[f32(*out_shape)] * count,
        scratch_shapes=[pltpu.SemaphoreType.DMA((2 * count,))],
        name="pick_for_cols",
    )(table, *pieces, *extra)


def place_rows(table, part, edge):
    size, width = part.shape
    rows = HALF * BLK

    def body(sc, part_ref, edge_ref, keep, send, window):
        window[:EDGE] = edge_ref[...]
        window[EDGE:] = part_ref[...]
        for target, half in ((keep, sc[SIB]), (send, 1 - sc[SIB])):
            for slot in range(HALF):
                place = sc[OWN_ROWS + half * HALF + slot]
                block = window[span(jnp.maximum(place, 0), BLK), :]
                target[slot * BLK : (slot + 1) * BLK, :] = jnp.where(place >= 0, block, 0.0)

    return pl.pallas_call(
        body,
        in_specs=[SMEM, VMEM, VMEM],
        out_specs=[VMEM, VMEM],
        out_shape=[f32(rows, width), f32(rows, width)],
        scratch_shapes=[pltpu.VMEM((size + EDGE, width), jnp.float32)],
        name="place_rows",
    )(table, part, edge)


def factor_slice(table, dealt, parent_slice, pivot_inverse):
    count = len(dealt)
    _, rows, sub = dealt[0].shape

    def body(*refs):
        sc = refs[0]
        pieces = refs[1 : 1 + count]
        parent_ref, inverse_ref, out, order, sums, ordered, sems = refs[1 + count :]
        copies = [
            pltpu.make_async_copy(piece, order.at[sc[COL] ^ k], sems.at[k])
            for k, piece in enumerate(pieces)
        ]
        run_copies(copies)
        sums[...] = parent_ref[...]
        for sibling, base in ((0, OWN_PIVOT), (1, OTHER_PIVOT)):
            for j in range(count):
                ordered[:, j * sub : (j + 1) * sub] = order[j, sibling]
            for child in range(PIV):
                block = ordered[:, child * BLK : (child + 1) * BLK]
                for parent in range(PIV):
                    cols = slice(parent * BLK, (parent + 1) * BLK)
                    sums[:, cols] += jnp.where(sc[base + child] == parent, block, 0.0)
        out[...] = times_transpose(halves(sums[...]), halves(inverse_ref[...]))

    return pl.pallas_call(
        body,
        in_specs=[SMEM] + [ANY] * count + [VMEM, VMEM],
        out_specs=VMEM,
        out_shape=f32(rows, PANEL),
        scratch_shapes=[
            pltpu.VMEM((count, 2, rows, sub), jnp.float32),
            pltpu.VMEM((rows, PANEL), jnp.float32),
            pltpu.VMEM((rows, PANEL), jnp.float32),
            pltpu.SemaphoreType.DMA((count,)),
        ],
        name="factor_slice",
    )(table, *dealt, parent_slice, pivot_inverse)


def lay_col_factor(table, pieces):
    count = len(pieces)
    _, rows, width = pieces[0].shape

    def body(*refs):
        sc = refs[0]
        ins = [ref.at[1] for ref in refs[1 : 1 + count]]
        out, sems = refs[1 + count :]
        run_copies(gather_copies(sc, ins, out, sems, rows))

    return pl.pallas_call(
        body,
        in_specs=[SMEM] + [ANY] * count,
        out_specs=ANY,
        out_shape=f32(count * rows, width),
        scratch_shapes=[pltpu.SemaphoreType.DMA((count,))],
        name="lay_col_factor",
    )(table, *pieces)


def finish(table, parent, own, other, pieces, col_own, col_other):
    count = len(pieces)
    rows, width = parent.shape
    piece_rows = pieces[0].shape[1]
    size = own[0].shape[0]

    def body(*refs):
        sc, parent_ref = refs[:2]
        own_refs, other_refs = refs[2:6], refs[6:10]
        ins = [ref.at[0] for ref in refs[10 : 10 + count]]
        col_own_ref, col_other_ref = refs[10 + count : 12 + count]
        out = refs[12 + count]
        own_win, other_win, row_factor, col_factor, sems = refs[13 + count :]
        low, high = slice(0, EDGE), slice(EDGE, EDGE + size)
        copies = gather_copies(sc, ins, row_factor, sems, piece_rows)
        copies += [
            pltpu.make_async_copy(
                col_own_ref, col_factor.at[span(sc[SIB], rows)], sems.at[count]
            ),
            pltpu.make_async_copy(
                col_other_ref, col_factor.at[span(1 - sc[SIB], rows)], sems.at[count + 1]
            ),
        ]
        place = count + 2
        for refs_in, window in ((own_refs, own_win), (other_refs, other_win)):
            spots = ((high, high), (high, low), (low, high), (low, low))
            for ref, (down, across) in zip(refs_in, spots):
                copies.append(
                    pltpu.make_async_copy(ref, window.at[down, across], sems.at[place])
                )
                place += 1
        run_copies(copies)
        first_row = (sc[ROW] * 2 + sc[SIB]) * HALF
        first_col = sc[COL] * PBD
        left = halves(row_factor[...])
        for q in range(PBD):
            cols = slice(q * BLK, (q + 1) * BLK)
            product = times_transpose(left, halves(col_factor[cols, :]))
            col_inside = first_col + q >= PIV
            for p in range(HALF):
                lines = slice(p * BLK, (p + 1) * BLK)
                total = parent_ref[lines, cols]
                for window, row_base, col_base in (
                    (own_win, OWN_ROWS, OWN_COLS),
                    (other_win, OTHER_ROWS, OTHER_COLS),
                ):
                    down = sc[row_base + sc[SIB] * HALF + p]
                    across = sc[col_base + q]
                    block = window[
                        span(jnp.maximum(down, 0), BLK), span(jnp.maximum(across, 0), BLK)
                    ]
                    total += jnp.where((down >= 0) & (across >= 0), block, 0.0)
                inside = col_inside & (first_row + p >= PIV)
                total = jnp.where(inside, total - product[lines, :], total)
                if q < PIV:
                    total = jnp.where(sc[COL] == 0, row_factor[lines, cols], total)
                out[lines, cols] = total

    return pl.pallas_call(
        body,
        in_specs=[SMEM, VMEM] + [ANY] * (8 + count + 2),
        out_specs=VMEM,
        out_shape=f32(rows, width),
        scratch_shapes=[
            pltpu.VMEM((size + EDGE, size + EDGE), jnp.float32),
            pltpu.VMEM((size + EDGE, size + EDGE), jnp.float32),
            pltpu.VMEM((rows, PANEL), jnp.float32),
            pltpu.VMEM((2 * rows, PANEL), jnp.float32),
            pltpu.SemaphoreType.DMA((count + 10,)),
        ],
        name="finish",
    )(table, parent, *own, *other, *pieces, col_own, col_other)


def shards(child_front, child_panel, block_map, parent_front, pivot_inverse):
    front_index = lax.axis_index("sib")
    row_index = lax.axis_index("row")
    col_index = lax.axis_index("col")
    count = lax.axis_size("col")
    front = child_front[0]
    panel = child_panel[0]
    sub = panel.shape[0]
    parent_rows, parent_cols = parent_front.shape
    parent_span = parent_cols // BLK
    deal = parent_rows // count

    own_map = lax.dynamic_index_in_dim(block_map, front_index, 0, keepdims=False)
    other_map = lax.dynamic_index_in_dim(block_map, 1 - front_index, 0, keepdims=False)
    table = jnp.concatenate(
        [
            jnp.stack([row_index, col_index, front_index]).astype(jnp.int32),
            window_choice(own_map, row_index, parent_span),
            window_choice(other_map, row_index, parent_span),
            window_choice(own_map, col_index, parent_span),
            window_choice(other_map, col_index, parent_span),
            own_map[:PIV],
            other_map[:PIV],
        ]
    )

    rows = [panel] + [swapped(panel, "col", k) for k in range(1, count)]
    turned = [panel] + [rotated(panel, "row", d) for d in range(1, count)]

    front_slice = front[:, :sub]
    parent_slice = parent_front[:deal, :PANEL]
    for j in range(1, count):
        sent_front = lax.ppermute(front[:, j * sub : (j + 1) * sub], "col", [(0, j)])
        sent_parent = lax.ppermute(
            parent_front[j * deal : (j + 1) * deal, :PANEL], "col", [(0, j)]
        )
        mine = col_index == j
        front_slice = jnp.where(mine, sent_front, front_slice)
        parent_slice = jnp.where(mine, sent_parent, parent_slice)

    part, edge = pivot_product(table, rows, turned, front_slice)
    keep, send = place_rows(table, part, shifted(edge, "row"))
    both = jnp.stack([keep, swapped(send, "sib", 1)])
    dealt = []
    for k in range(count):
        piece = lax.dynamic_slice_in_dim(both, (col_index ^ k) * deal, deal, axis=1)
        dealt.append(swapped(piece, "col", k) if k else piece)
    factor = factor_slice(table, dealt, parent_slice, pivot_inverse)
    factors = [factor] + [rotated(factor, "row", d) for d in range(1, count)]
    factor_pairs = pick_for_cols(table, factors, factor)
    factor_pairs = [factor_pairs[0]] + [
        swapped(factor_pairs[k], "col", k) for k in range(1, count)
    ]
    col_own = lay_col_factor(table, factor_pairs)
    col_other = swapped(col_own, "sib", 1)

    picked = pick_for_cols(table, turned)
    cols = [picked[0]] + [swapped(picked[k], "col", k) for k in range(1, count)]
    update, right, up, corner = update_product(table, rows, cols, front)
    own = [update, shifted(right, "col"), shifted(up, "row"), shifted_both(corner, count)]
    other = [swapped(value, "sib", 1) for value in own]
    return finish(table, parent_front, own, other, factor_pairs, col_own, col_other)


def solution(mesh):
    in_specs = (
        P("sib", "row", "col"),
        P("sib", ("row", "col"), None),
        P(),
        P(("row", "sib"), "col"),
        P(),
    )
    out_specs = P(("row", "sib"), "col")
    return jax.shard_map(shards, mesh=mesh, in_specs=in_specs, out_specs=out_specs, check_vma=False)
```

```python
import jax
import jax.numpy as jnp
from jax import lax
from jax.experimental import pallas as pl
from jax.experimental.pallas import tpu as pltpu
from jax.sharding import PartitionSpec as P

BLK = 128
CBD = 4
PBD = 6
HB = 2
PIV = 4
PANEL = 512
HALF = PBD // 2
EDGE = HB * BLK


SMEM = pl.BlockSpec(memory_space=pltpu.SMEM)
VMEM = pl.BlockSpec(memory_space=pltpu.VMEM)
ANY = pl.BlockSpec(memory_space=pl.ANY)

ROW, COL, SIB = 0, 1, 2
OWN_ROWS, OTHER_ROWS, OWN_COLS, OTHER_COLS = 3, 9, 15, 21
OWN_PIVOT, OTHER_PIVOT = 27, 31


def f32(*shape):
    return jax.ShapeDtypeStruct(shape, jnp.float32)


def halves(value):
    high = value.astype(jnp.bfloat16)
    low = (value - high.astype(jnp.float32)).astype(jnp.bfloat16)
    return high, low


def times_transpose(left, right):
    def dot(x, y):
        return lax.dot_general(
            x, y, (((1,), (1,)), ((), ())), preferred_element_type=jnp.float32
        )

    return dot(left[0], right[0]) + (dot(left[0], right[1]) + dot(left[1], right[0]))


def rotated(value, axis, steps):
    count = lax.axis_size(axis)
    return lax.ppermute(value, axis, [(i, (i + steps) % count) for i in range(count)])


def swapped(value, axis, mask):
    count = lax.axis_size(axis)
    return lax.ppermute(value, axis, [(i, i ^ mask) for i in range(count)])


def shifted(value, axis):
    count = lax.axis_size(axis)
    return lax.ppermute(value, axis, [(i, i + 1) for i in range(count - 1)])


def shifted_both(value, count):
    pairs = [
        (r * count + c, (r + 1) * count + c + 1)
        for r in range(count - 1)
        for c in range(count - 1)
    ]
    return lax.ppermute(value, ("row", "col"), pairs)


def run_copies(copies):
    for copy in copies:
        copy.start()
    for copy in copies:
        copy.wait()


def span(index, size):
    return pl.ds(pl.multiple_of(index * size, size), size)


def gather_copies(table, pieces, target, sems, size, base=0):
    return [
        pltpu.make_async_copy(piece, target.at[span(table[COL] ^ k, size)], sems.at[base + k])
        for k, piece in enumerate(pieces)
    ]


def window_choice(block_row, group, parent_span):
    padded = jnp.concatenate([jnp.full((HB,), -1, jnp.int32), block_row])
    window = lax.dynamic_slice_in_dim(padded, group * CBD, CBD + HB)
    target = group * parent_span + jnp.arange(parent_span, dtype=jnp.int32)
    places = jnp.arange(1, CBD + HB + 1, dtype=jnp.int32)
    hit = window[None, :] == target[:, None]
    return jnp.sum(jnp.where(hit, places[None, :], 0), axis=1).astype(jnp.int32) - 1


def pivot_product(table, rows, col_pieces, front):
    count = len(rows)
    sub, depth = rows[0].shape
    width = front.shape[1]

    def body(*refs):
        sc = refs[0]
        row_refs = refs[1 : 1 + count]
        col_refs = refs[1 + count : 1 + 2 * count]
        front_ref, out, edge, row_buf, col_buf, sems = refs[1 + 2 * count :]
        for d in range(count):

            @pl.when(sc[ROW] == d)
            def _():
                pltpu.make_async_copy(col_refs[d], col_buf, sems.at[count]).start()

        run_copies(gather_copies(sc, row_refs, row_buf, sems, sub))
        pltpu.make_async_copy(col_refs[0], col_buf, sems.at[count]).wait()
        part = front_ref[...] - times_transpose(halves(row_buf[...]), halves(col_buf[...]))
        out[...] = part
        edge[...] = part[-EDGE:]

    return pl.pallas_call(
        body,
        in_specs=[SMEM] + [ANY] * (2 * count) + [VMEM],
        out_specs=[VMEM, VMEM],
        out_shape=[f32(count * sub, width), f32(EDGE, width)],
        scratch_shapes=[
            pltpu.VMEM((count * sub, depth), jnp.float32),
            pltpu.VMEM((sub, depth), jnp.float32),
            pltpu.SemaphoreType.DMA((count + 1,)),
        ],
        name="pivot_product",
    )(table, *rows, *col_pieces, front)


def update_product(table, rows, cols, front):
    count = len(rows)
    sub, depth = rows[0].shape
    size = count * sub

    def body(*refs):
        sc = refs[0]
        row_refs = refs[1 : 1 + count]
        col_refs = refs[1 + count : 1 + 2 * count]
        front_ref, out, right, up, corner, row_buf, col_buf, sems = refs[1 + 2 * count :]
        run_copies(
            gather_copies(sc, row_refs, row_buf, sems, sub)
            + gather_copies(sc, col_refs, col_buf, sems, sub, count)
        )
        part = front_ref[...] - times_transpose(halves(row_buf[...]), halves(col_buf[...]))
        out[...] = part
        right[...] = part[:, -EDGE:]
        up[...] = part[-EDGE:, :]
        corner[...] = part[-EDGE:, -EDGE:]

    return pl.pallas_call(
        body,
        in_specs=[SMEM] + [ANY] * (2 * count) + [VMEM],
        out_specs=[VMEM] * 4,
        out_shape=[f32(size, size), f32(size, EDGE), f32(EDGE, size), f32(EDGE, EDGE)],
        scratch_shapes=[
            pltpu.VMEM((size, depth), jnp.float32),
            pltpu.VMEM((size, depth), jnp.float32),
            pltpu.SemaphoreType.DMA((2 * count,)),
        ],
        name="update_product",
    )(table, *rows, *cols, front)


def pick_for_cols(table, pieces, own=None):
    count = len(pieces)
    shape = pieces[0].shape
    with_own = own is not None
    out_shape = (2,) + shape if with_own else shape

    def body(*refs):
        sc = refs[0]
        ins = refs[1 : 1 + count]
        own_ref = refs[1 + count] if with_own else None
        outs = refs[1 + count + with_own : 1 + 2 * count + with_own]
        sems = refs[-1]
        places = [out.at[1] if with_own else out for out in outs]
        fixed = []
        if with_own:
            fixed = [
                pltpu.make_async_copy(own_ref, out.at[0], sems.at[count + k])
                for k, out in enumerate(outs)
            ]
        for copy in fixed:
            copy.start()
        for k in range(count):
            wanted = lax.rem(sc[ROW] - (sc[COL] ^ k) + count, count)
            for d in range(count):

                @pl.when(wanted == d)
                def _():
                    pltpu.make_async_copy(ins[d], places[k], sems.at[k]).start()

        for k in range(count):
            pltpu.make_async_copy(ins[0], places[k], sems.at[k]).wait()
        for copy in fixed:
            copy.wait()

    extra = [own] if with_own else []
    return pl.pallas_call(
        body,
        in_specs=[SMEM] + [ANY] * (count + with_own),
        out_specs=[VMEM] * count,
        out_shape=[f32(*out_shape)] * count,
        scratch_shapes=[pltpu.SemaphoreType.DMA((2 * count,))],
        name="pick_for_cols",
    )(table, *pieces, *extra)


def place_rows(table, part, edge):
    size, width = part.shape
    rows = HALF * BLK

    def body(sc, part_ref, edge_ref, keep, send, window):
        window[:EDGE] = edge_ref[...]
        window[EDGE:] = part_ref[...]
        for target, half in ((keep, sc[SIB]), (send, 1 - sc[SIB])):
            for slot in range(HALF):
                place = sc[OWN_ROWS + half * HALF + slot]
                block = window[span(jnp.maximum(place, 0), BLK), :]
                target[slot * BLK : (slot + 1) * BLK, :] = jnp.where(place >= 0, block, 0.0)

    return pl.pallas_call(
        body,
        in_specs=[SMEM, VMEM, VMEM],
        out_specs=[VMEM, VMEM],
        out_shape=[f32(rows, width), f32(rows, width)],
        scratch_shapes=[pltpu.VMEM((size + EDGE, width), jnp.float32)],
        name="place_rows",
    )(table, part, edge)


def factor_slice(table, dealt, parent_slice, pivot_inverse):
    count = len(dealt)
    _, rows, sub = dealt[0].shape

    def body(*refs):
        sc = refs[0]
        pieces = refs[1 : 1 + count]
        parent_ref, inverse_ref, out, order, sums, ordered, sems = refs[1 + count :]
        copies = [
            pltpu.make_async_copy(piece, order.at[sc[COL] ^ k], sems.at[k])
            for k, piece in enumerate(pieces)
        ]
        run_copies(copies)
        sums[...] = parent_ref[...]
        for sibling, base in ((0, OWN_PIVOT), (1, OTHER_PIVOT)):
            for j in range(count):
                ordered[:, j * sub : (j + 1) * sub] = order[j, sibling]
            for child in range(PIV):
                block = ordered[:, child * BLK : (child + 1) * BLK]
                for parent in range(PIV):
                    cols = slice(parent * BLK, (parent + 1) * BLK)
                    sums[:, cols] += jnp.where(sc[base + child] == parent, block, 0.0)
        out[...] = times_transpose(halves(sums[...]), halves(inverse_ref[...]))

    return pl.pallas_call(
        body,
        in_specs=[SMEM] + [ANY] * count + [VMEM, VMEM],
        out_specs=VMEM,
        out_shape=f32(rows, PANEL),
        scratch_shapes=[
            pltpu.VMEM((count, 2, rows, sub), jnp.float32),
            pltpu.VMEM((rows, PANEL), jnp.float32),
            pltpu.VMEM((rows, PANEL), jnp.float32),
            pltpu.SemaphoreType.DMA((count,)),
        ],
        name="factor_slice",
    )(table, *dealt, parent_slice, pivot_inverse)


def lay_col_factor(table, pieces):
    count = len(pieces)
    _, rows, width = pieces[0].shape

    def body(*refs):
        sc = refs[0]
        ins = [ref.at[1] for ref in refs[1 : 1 + count]]
        out, sems = refs[1 + count :]
        run_copies(gather_copies(sc, ins, out, sems, rows))

    return pl.pallas_call(
        body,
        in_specs=[SMEM] + [ANY] * count,
        out_specs=VMEM,
        out_shape=f32(count * rows, width),
        scratch_shapes=[pltpu.SemaphoreType.DMA((count,))],
        name="lay_col_factor",
    )(table, *pieces)


def finish(table, parent, own, other, pieces, col_own, col_other):
    count = len(pieces)
    rows, width = parent.shape
    piece_rows = pieces[0].shape[1]
    size = own[0].shape[0]

    def body(*refs):
        sc, parent_ref = refs[:2]
        own_refs, other_refs = refs[2:6], refs[6:10]
        ins = [ref.at[0] for ref in refs[10 : 10 + count]]
        col_own_ref, col_other_ref = refs[10 + count : 12 + count]
        out = refs[12 + count]
        own_win, other_win, row_factor, col_factor, sems = refs[13 + count :]
        low, high = slice(0, EDGE), slice(EDGE, EDGE + size)
        copies = gather_copies(sc, ins, row_factor, sems, piece_rows)
        copies += [
            pltpu.make_async_copy(
                col_own_ref, col_factor.at[span(sc[SIB], rows)], sems.at[count]
            ),
            pltpu.make_async_copy(
                col_other_ref, col_factor.at[span(1 - sc[SIB], rows)], sems.at[count + 1]
            ),
        ]
        place = count + 2
        for refs_in, window in ((own_refs, own_win), (other_refs, other_win)):
            spots = ((high, high), (high, low), (low, high), (low, low))
            for ref, (down, across) in zip(refs_in, spots):
                copies.append(
                    pltpu.make_async_copy(ref, window.at[down, across], sems.at[place])
                )
                place += 1
        run_copies(copies)
        first_row = (sc[ROW] * 2 + sc[SIB]) * HALF
        first_col = sc[COL] * PBD
        left = halves(row_factor[...])
        for q in range(PBD):
            cols = slice(q * BLK, (q + 1) * BLK)
            product = times_transpose(left, halves(col_factor[cols, :]))
            col_inside = first_col + q >= PIV
            for p in range(HALF):
                lines = slice(p * BLK, (p + 1) * BLK)
                total = parent_ref[lines, cols]
                for window, row_base, col_base in (
                    (own_win, OWN_ROWS, OWN_COLS),
                    (other_win, OTHER_ROWS, OTHER_COLS),
                ):
                    down = sc[row_base + sc[SIB] * HALF + p]
                    across = sc[col_base + q]
                    block = window[
                        span(jnp.maximum(down, 0), BLK), span(jnp.maximum(across, 0), BLK)
                    ]
                    total += jnp.where((down >= 0) & (across >= 0), block, 0.0)
                inside = col_inside & (first_row + p >= PIV)
                total = jnp.where(inside, total - product[lines, :], total)
                if q < PIV:
                    total = jnp.where(sc[COL] == 0, row_factor[lines, cols], total)
                out[lines, cols] = total

    return pl.pallas_call(
        body,
        in_specs=[SMEM, VMEM] + [ANY] * (8 + count + 2),
        out_specs=VMEM,
        out_shape=f32(rows, width),
        scratch_shapes=[
            pltpu.VMEM((size + EDGE, size + EDGE), jnp.float32),
            pltpu.VMEM((size + EDGE, size + EDGE), jnp.float32),
            pltpu.VMEM((rows, PANEL), jnp.float32),
            pltpu.VMEM((2 * rows, PANEL), jnp.float32),
            pltpu.SemaphoreType.DMA((count + 10,)),
        ],
        name="finish",
    )(table, parent, *own, *other, *pieces, col_own, col_other)


def shards(child_front, child_panel, block_map, parent_front, pivot_inverse):
    front_index = lax.axis_index("sib")
    row_index = lax.axis_index("row")
    col_index = lax.axis_index("col")
    count = lax.axis_size("col")
    front = child_front[0]
    panel = child_panel[0]
    sub = panel.shape[0]
    parent_rows, parent_cols = parent_front.shape
    parent_span = parent_cols // BLK
    deal = parent_rows // count

    own_map = lax.dynamic_index_in_dim(block_map, front_index, 0, keepdims=False)
    other_map = lax.dynamic_index_in_dim(block_map, 1 - front_index, 0, keepdims=False)
    table = jnp.concatenate(
        [
            jnp.stack([row_index, col_index, front_index]).astype(jnp.int32),
            window_choice(own_map, row_index, parent_span),
            window_choice(other_map, row_index, parent_span),
            window_choice(own_map, col_index, parent_span),
            window_choice(other_map, col_index, parent_span),
            own_map[:PIV],
            other_map[:PIV],
        ]
    )

    rows = [panel] + [swapped(panel, "col", k) for k in range(1, count)]
    turned = [panel] + [rotated(panel, "row", d) for d in range(1, count)]

    front_slice = front[:, :sub]
    parent_slice = parent_front[:deal, :PANEL]
    for j in range(1, count):
        sent_front = lax.ppermute(front[:, j * sub : (j + 1) * sub], "col", [(0, j)])
        sent_parent = lax.ppermute(
            parent_front[j * deal : (j + 1) * deal, :PANEL], "col", [(0, j)]
        )
        mine = col_index == j
        front_slice = jnp.where(mine, sent_front, front_slice)
        parent_slice = jnp.where(mine, sent_parent, parent_slice)

    part, edge = pivot_product(table, rows, turned, front_slice)
    keep, send = place_rows(table, part, shifted(edge, "row"))
    both = jnp.stack([keep, swapped(send, "sib", 1)])
    dealt = []
    for k in range(count):
        piece = lax.dynamic_slice_in_dim(both, (col_index ^ k) * deal, deal, axis=1)
        dealt.append(swapped(piece, "col", k) if k else piece)
    factor = factor_slice(table, dealt, parent_slice, pivot_inverse)
    factors = [factor] + [rotated(factor, "row", d) for d in range(1, count)]
    factor_pairs = pick_for_cols(table, factors, factor)
    factor_pairs = [factor_pairs[0]] + [
        swapped(factor_pairs[k], "col", k) for k in range(1, count)
    ]
    col_own = lay_col_factor(table, factor_pairs)
    col_other = swapped(col_own, "sib", 1)

    picked = pick_for_cols(table, turned)
    cols = [picked[0]] + [swapped(picked[k], "col", k) for k in range(1, count)]
    update, right, up, corner = update_product(table, rows, cols, front)
    own = [update, shifted(right, "col"), shifted(up, "row"), shifted_both(corner, count)]
    other = [swapped(value, "sib", 1) for value in own]
    return finish(table, parent_front, own, other, factor_pairs, col_own, col_other)


def solution(mesh):
    in_specs = (
        P("sib", "row", "col"),
        P("sib", ("row", "col"), None),
        P(),
        P(("row", "sib"), "col"),
        P(),
    )
    out_specs = P(("row", "sib"), "col")
    return jax.shard_map(shards, mesh=mesh, in_specs=in_specs, out_specs=out_specs, check_vma=False)
```

```python
import jax
import jax.numpy as jnp
from jax import lax
from jax.experimental import pallas as pl
from jax.experimental.pallas import tpu as pltpu
from jax.sharding import PartitionSpec as P


BLK = 128
CBD = 4
PBD = 6
HB = 2
PIV = 4
PANEL = 512
HALF = PBD // 2
EDGE = HB * BLK


SMEM = pl.BlockSpec(memory_space=pltpu.SMEM)
VMEM = pl.BlockSpec(memory_space=pltpu.VMEM)
ANY = pl.BlockSpec(memory_space=pl.ANY)

ROW, COL, SIB = 0, 1, 2
OWN_ROWS, OTHER_ROWS, OWN_COLS, OTHER_COLS = 3, 9, 15, 21
OWN_PIVOT, OTHER_PIVOT = 27, 31


def f32(*shape):
    return jax.ShapeDtypeStruct(shape, jnp.float32)


def halves(value):
    high = value.astype(jnp.bfloat16)
    low = (value - high.astype(jnp.float32)).astype(jnp.bfloat16)
    return high, low


def times_transpose(left, right):
    def dot(x, y):
        return lax.dot_general(
            x, y, (((1,), (1,)), ((), ())), preferred_element_type=jnp.float32
        )

    return dot(left[0], right[0]) + (dot(left[0], right[1]) + dot(left[1], right[0]))


def rotated(value, axis, steps):
    count = lax.axis_size(axis)
    return lax.ppermute(value, axis, [(i, (i + steps) % count) for i in range(count)])


def swapped(value, axis, mask):
    count = lax.axis_size(axis)
    return lax.ppermute(value, axis, [(i, i ^ mask) for i in range(count)])


def shifted(value, axis):
    count = lax.axis_size(axis)
    return lax.ppermute(value, axis, [(i, i + 1) for i in range(count - 1)])


def shifted_both(value, count):
    pairs = [
        (r * count + c, (r + 1) * count + c + 1)
        for r in range(count - 1)
        for c in range(count - 1)
    ]
    return lax.ppermute(value, ("row", "col"), pairs)


def run_copies(copies):
    for copy in copies:
        copy.start()
    for copy in copies:
        copy.wait()


def span(index, size):
    return pl.ds(pl.multiple_of(index * size, size), size)


def gather_copies(table, pieces, target, sems, size, base=0):
    return [
        pltpu.make_async_copy(piece, target.at[span(table[COL] ^ k, size)], sems.at[base + k])
        for k, piece in enumerate(pieces)
    ]


def window_choice(block_row, group, parent_span):
    padded = jnp.concatenate([jnp.full((HB,), -1, jnp.int32), block_row])
    window = lax.dynamic_slice_in_dim(padded, group * CBD, CBD + HB)
    target = group * parent_span + jnp.arange(parent_span, dtype=jnp.int32)
    places = jnp.arange(1, CBD + HB + 1, dtype=jnp.int32)
    hit = window[None, :] == target[:, None]
    return jnp.sum(jnp.where(hit, places[None, :], 0), axis=1).astype(jnp.int32) - 1


def start_chosen(chosen, choices, target, sem):
    for d, choice in enumerate(choices):

        @pl.when(chosen == d)
        def _():
            pltpu.make_async_copy(choice, target, sem).start()


def turn_of(sc, mask, count):
    return lax.rem(sc[ROW] - (sc[COL] ^ mask) + count, count)


def pivot_product(table, rows, turned, dealt):
    count = len(rows)
    sub, depth = rows[0].shape
    size = count * sub

    def body(*refs):
        sc = refs[0]
        row_refs = refs[1 : 1 + count]
        col_refs = refs[1 + count : 1 + 2 * count]
        deal_refs = refs[1 + 2 * count : 1 + 3 * count]
        out, edge, row_buf, col_buf, front, sems = refs[1 + 3 * count :]
        start_chosen(sc[ROW], col_refs, col_buf, sems.at[count])
        front_parts = [ref.at[pl.ds(0, size)] for ref in deal_refs]
        start_chosen(sc[COL], front_parts, front, sems.at[count + 1])
        run_copies(gather_copies(sc, row_refs, row_buf, sems, sub))
        pltpu.make_async_copy(col_refs[0], col_buf, sems.at[count]).wait()
        pltpu.make_async_copy(front_parts[0], front, sems.at[count + 1]).wait()
        part = front[...] - times_transpose(halves(row_buf[...]), halves(col_buf[...]))
        out[...] = part
        edge[...] = part[-EDGE:]

    return pl.pallas_call(
        body,
        in_specs=[SMEM] + [ANY] * (3 * count),
        out_specs=[VMEM, VMEM],
        out_shape=[f32(size, sub), f32(EDGE, sub)],
        scratch_shapes=[
            pltpu.VMEM((size, depth), jnp.float32),
            pltpu.VMEM((sub, depth), jnp.float32),
            pltpu.VMEM((size, sub), jnp.float32),
            pltpu.SemaphoreType.DMA((count + 2,)),
        ],
        name="pivot_product",
    )(table, *rows, *turned, *dealt)


def update_product(table, rows, turned, cols, front):
    count = len(rows)
    sub, depth = rows[0].shape
    size = count * sub

    def body(*refs):
        sc = refs[0]
        row_refs = refs[1 : 1 + count]
        turn_refs = refs[1 + count : 1 + 2 * count]
        col_refs = refs[1 + 2 * count : 3 * count]
        front_ref, out, right, up, corner, row_buf, col_buf, sems = refs[3 * count :]
        home = col_buf.at[span(sc[COL], sub)]
        start_chosen(turn_of(sc, 0, count), turn_refs, home, sems.at[count])
        copies = gather_copies(sc, row_refs, row_buf, sems, sub)
        copies += [
            pltpu.make_async_copy(
                ref, col_buf.at[span(sc[COL] ^ (k + 1), sub)], sems.at[count + 1 + k]
            )
            for k, ref in enumerate(col_refs)
        ]
        run_copies(copies)
        pltpu.make_async_copy(turn_refs[0], home, sems.at[count]).wait()
        part = front_ref[...] - times_transpose(halves(row_buf[...]), halves(col_buf[...]))
        out[...] = part
        right[...] = part[:, -EDGE:]
        up[...] = part[-EDGE:, :]
        corner[...] = part[-EDGE:, -EDGE:]

    return pl.pallas_call(
        body,
        in_specs=[SMEM] + [ANY] * (3 * count - 1) + [VMEM],
        out_specs=[VMEM] * 4,
        out_shape=[f32(size, size), f32(size, EDGE), f32(EDGE, size), f32(EDGE, EDGE)],
        scratch_shapes=[
            pltpu.VMEM((size, depth), jnp.float32),
            pltpu.VMEM((size, depth), jnp.float32),
            pltpu.SemaphoreType.DMA((2 * count,)),
        ],
        name="update_product",
    )(table, *rows, *turned, *cols, front)


def pick_for_cols(table, pieces, masks):
    count = len(pieces)

    def body(*refs):
        sc = refs[0]
        ins = refs[1 : 1 + count]
        outs = refs[1 + count : -1]
        sems = refs[-1]
        for i, mask in enumerate(masks):
            start_chosen(turn_of(sc, mask, count), ins, outs[i], sems.at[i])
        for i in range(len(masks)):
            pltpu.make_async_copy(ins[0], outs[i], sems.at[i]).wait()

    return pl.pallas_call(
        body,
        in_specs=[SMEM] + [ANY] * count,
        out_specs=[VMEM] * len(masks),
        out_shape=[f32(*pieces[0].shape)] * len(masks),
        scratch_shapes=[pltpu.SemaphoreType.DMA((len(masks),))],
        name="pick_for_cols",
    )(table, *pieces)


def place_rows(table, part, edge):
    size, width = part.shape
    rows = HALF * BLK

    def body(sc, part_ref, edge_ref, keep, send, window):
        window[:EDGE] = edge_ref[...]
        window[EDGE:] = part_ref[...]
        for target, half in ((keep, sc[SIB]), (send, 1 - sc[SIB])):
            for slot in range(HALF):
                place = sc[OWN_ROWS + half * HALF + slot]
                block = window[span(jnp.maximum(place, 0), BLK), :]
                target[slot * BLK : (slot + 1) * BLK, :] = jnp.where(place >= 0, block, 0.0)

    return pl.pallas_call(
        body,
        in_specs=[SMEM, VMEM, VMEM],
        out_specs=[VMEM, VMEM],
        out_shape=[f32(rows, width), f32(rows, width)],
        scratch_shapes=[pltpu.VMEM((size + EDGE, width), jnp.float32)],
        name="place_rows",
    )(table, part, edge)


def factor_slice(table, small, dealt, pivot_inverse):
    count = len(small)
    _, rows, sub = small[0].shape
    total = dealt[0].shape[0]
    below = total - PANEL // sub * rows

    def body(*refs):
        sc = refs[0]
        pieces = refs[1 : 1 + count]
        deal_refs = refs[1 + count : 1 + 2 * count]
        inverse_ref, out, order, child, parent, sums, sems = refs[1 + 2 * count :]
        parent_parts = [ref.at[pl.ds(below, total - below)] for ref in deal_refs]
        start_chosen(sc[COL], parent_parts, parent, sems.at[count])
        run_copies(
            [
                pltpu.make_async_copy(piece, order.at[sc[COL] ^ k], sems.at[k])
                for k, piece in enumerate(pieces)
            ]
        )
        pltpu.make_async_copy(parent_parts[0], parent, sems.at[count]).wait()
        for j in range(count):
            block, lane = divmod(j * sub, BLK)
            for sibling in range(2):
                child[sibling, block, :, lane : lane + sub] = order[j, sibling]
            sums[:, j * sub : (j + 1) * sub] = parent[j * rows : (j + 1) * rows]
        for p in range(PIV):
            lanes = slice(p * BLK, (p + 1) * BLK)
            added = sums[:, lanes]
            for sibling, base in ((0, OWN_PIVOT), (1, OTHER_PIVOT)):
                place = sc[base + p]
                block = child[sibling, jnp.maximum(place - HB, 0)]
                added += jnp.where(place >= HB, block, 0.0)
            sums[:, lanes] = added
        out[...] = times_transpose(halves(sums[...]), halves(inverse_ref[...]))

    return pl.pallas_call(
        body,
        in_specs=[SMEM] + [ANY] * (2 * count) + [VMEM],
        out_specs=VMEM,
        out_shape=f32(rows, PANEL),
        scratch_shapes=[
            pltpu.VMEM((count, 2, rows, sub), jnp.float32),
            pltpu.VMEM((2, PIV, rows, BLK), jnp.float32),
            pltpu.VMEM((total - below, sub), jnp.float32),
            pltpu.VMEM((rows, PANEL), jnp.float32),
            pltpu.SemaphoreType.DMA((count + 1,)),
        ],
        name="factor_slice",
    )(table, *small, *dealt, pivot_inverse)


def finish(table, parent, own, other, row_pieces, col_own, col_other):
    count = len(row_pieces)
    rows, width = parent.shape
    piece_rows = row_pieces[0].shape[0]
    size = own[0].shape[0]

    def body(*refs):
        sc, parent_ref = refs[:2]
        own_refs, other_refs = refs[2:6], refs[6:10]
        row_refs = refs[10 : 10 + count]
        col_own_refs = refs[10 + count : 10 + 2 * count]
        col_other_refs = refs[10 + 2 * count : 10 + 3 * count]
        out = refs[10 + 3 * count]
        own_win, other_win, row_factor, col_factor, products, sems = refs[11 + 3 * count :]
        low, high = slice(0, EDGE), slice(EDGE, EDGE + size)
        factors = gather_copies(sc, row_refs, row_factor, sems, piece_rows)
        factors += gather_copies(
            sc, col_own_refs, col_factor.at[sc[SIB]], sems, piece_rows, count
        )
        factors += gather_copies(
            sc, col_other_refs, col_factor.at[1 - sc[SIB]], sems, piece_rows, 2 * count
        )
        place = 3 * count
        windows = []
        for refs_in, window in ((own_refs, own_win), (other_refs, other_win)):
            spots = ((high, high), (high, low), (low, high), (low, low))
            for ref, (down, across) in zip(refs_in, spots):
                windows.append(
                    pltpu.make_async_copy(ref, window.at[down, across], sems.at[place])
                )
                place += 1
        for copy in factors + windows:
            copy.start()
        for copy in factors:
            copy.wait()
        left = halves(row_factor[...])
        for half in range(2):
            right = halves(col_factor[half])
            products[:, half * rows : (half + 1) * rows] = times_transpose(left, right)
        for copy in windows:
            copy.wait()
        first_row = (sc[ROW] * 2 + sc[SIB]) * HALF
        first_col = sc[COL] * PBD
        for q in range(PBD):
            cols = slice(q * BLK, (q + 1) * BLK)
            col_inside = first_col + q >= PIV
            for p in range(HALF):
                lines = slice(p * BLK, (p + 1) * BLK)
                total = parent_ref[lines, cols]
                for window, row_base, col_base in (
                    (own_win, OWN_ROWS, OWN_COLS),
                    (other_win, OTHER_ROWS, OTHER_COLS),
                ):
                    down = sc[row_base + sc[SIB] * HALF + p]
                    across = sc[col_base + q]
                    block = window[
                        span(jnp.maximum(down, 0), BLK), span(jnp.maximum(across, 0), BLK)
                    ]
                    total += jnp.where((down >= 0) & (across >= 0), block, 0.0)
                inside = col_inside & (first_row + p >= PIV)
                total = jnp.where(inside, total - products[lines, cols], total)
                if q < PIV:
                    total = jnp.where(sc[COL] == 0, row_factor[lines, cols], total)
                out[lines, cols] = total

    return pl.pallas_call(
        body,
        in_specs=[SMEM, VMEM] + [ANY] * (8 + 3 * count),
        out_specs=VMEM,
        out_shape=f32(rows, width),
        scratch_shapes=[
            pltpu.VMEM((size + EDGE, size + EDGE), jnp.float32),
            pltpu.VMEM((size + EDGE, size + EDGE), jnp.float32),
            pltpu.VMEM((rows, PANEL), jnp.float32),
            pltpu.VMEM((2, rows, PANEL), jnp.float32),
            pltpu.VMEM((rows, 2 * rows), jnp.float32),
            pltpu.SemaphoreType.DMA((3 * count + 8,)),
        ],
        name="finish",
    )(table, parent, *own, *other, *row_pieces, *col_own, *col_other)


def shards(child_front, child_panel, block_map, parent_front, pivot_inverse):
    front_index = lax.axis_index("sib")
    row_index = lax.axis_index("row")
    col_index = lax.axis_index("col")
    count = lax.axis_size("col")
    front = child_front[0]
    panel = child_panel[0]
    sub = panel.shape[0]
    parent_rows, parent_cols = parent_front.shape
    parent_span = parent_cols // BLK
    deal = parent_rows // count

    own_map = lax.dynamic_index_in_dim(block_map, front_index, 0, keepdims=False)
    other_map = lax.dynamic_index_in_dim(block_map, 1 - front_index, 0, keepdims=False)
    table = jnp.concatenate(
        [
            jnp.stack([row_index, col_index, front_index]).astype(jnp.int32),
            window_choice(own_map, row_index, parent_span),
            window_choice(other_map, row_index, parent_span),
            window_choice(own_map, col_index, parent_span),
            window_choice(other_map, col_index, parent_span),
            window_choice(own_map, 0, parent_span)[:PIV],
            window_choice(other_map, 0, parent_span)[:PIV],
        ]
    )

    def over_col(values):
        got = []
        for k, value in zip(range(1, count), values):
            got.append(swapped(value, "col", k))
        return got

    def over_row(value):
        got = [value]
        for d in range(1, count):
            got.append(rotated(value, "row", d))
        return got

    def to_sibling(value):
        return swapped(value, "sib", 1)

    turned = over_row(panel)
    rows = [panel] + over_col([panel] * (count - 1))

    dealt = []
    for j in range(count):
        lines = parent_front[j * deal : (j + 1) * deal, :PANEL]
        pieces = [lines[:, i : i + sub] for i in range(0, PANEL, sub)]
        value = jnp.concatenate([front[:, j * sub : (j + 1) * sub]] + pieces, axis=0)
        dealt.append(lax.ppermute(value, "col", [(0, j)]) if j else value)

    part, edge = pivot_product(table, rows, turned, dealt)
    edge = shifted(edge, "row")
    picked = pick_for_cols(table, turned, range(1, count))
    cols = over_col(picked)
    keep, send = place_rows(table, part, edge)
    both = jnp.stack([keep, to_sibling(send)])
    slices = [
        lax.dynamic_slice_in_dim(both, (col_index ^ k) * deal, deal, axis=1)
        for k in range(count)
    ]
    small = [slices[0]] + over_col(slices[1:])
    factor = factor_slice(table, small, dealt, pivot_inverse)
    factors = over_row(factor)
    row_pieces = [factor] + over_col([factor] * (count - 1))

    update, right, up, corner = update_product(table, rows, turned, cols, front)
    right = shifted(right, "col")
    up = shifted(up, "row")
    corner = shifted_both(corner, count)
    own = [update, right, up, corner]

    picked = pick_for_cols(table, factors, range(count))
    col_own = [picked[0]] + over_col(picked[1:])
    col_other = [to_sibling(value) for value in col_own]

    other = [to_sibling(value) for value in own]
    return finish(table, parent_front, own, other, row_pieces, col_own, col_other)


def solution(mesh):
    in_specs = (
        P("sib", "row", "col"),
        P("sib", ("row", "col"), None),
        P(),
        P(("row", "sib"), "col"),
        P(),
    )
    out_specs = P(("row", "sib"), "col")

    return jax.shard_map(shards, mesh=mesh, in_specs=in_specs, out_specs=out_specs, check_vma=False)
```

```python
import jax
import jax.numpy as jnp
from jax import lax
from jax.experimental import pallas as pl
from jax.experimental.pallas import tpu as pltpu
from jax.sharding import PartitionSpec as P


BLK = 128
CBD = 4
PBD = 6
HB = 2
PIV = 4
PANEL = 512
HALF = PBD // 2
EDGE = HB * BLK


SMEM = pl.BlockSpec(memory_space=pltpu.SMEM)
VMEM = pl.BlockSpec(memory_space=pltpu.VMEM)
ANY = pl.BlockSpec(memory_space=pl.ANY)

LIMITS = pltpu.CompilerParams(vmem_limit_bytes=16 << 20)

ROW, COL, SIB = 0, 1, 2
OWN_ROWS, OTHER_ROWS, OWN_COLS, OTHER_COLS = 3, 9, 15, 21
OWN_PIVOT, OTHER_PIVOT = 27, 31


def f32(*shape):
    return jax.ShapeDtypeStruct(shape, jnp.float32)


def halves(value):
    high = value.astype(jnp.bfloat16)
    low = (value - high.astype(jnp.float32)).astype(jnp.bfloat16)
    return high, low


def times_transpose(left, right):
    def dot(x, y):
        return lax.dot_general(
            x, y, (((1,), (1,)), ((), ())), preferred_element_type=jnp.float32
        )

    return dot(left[0], right[0]) + (dot(left[0], right[1]) + dot(left[1], right[0]))


def rotated(value, axis, steps):
    count = lax.axis_size(axis)
    return lax.ppermute(value, axis, [(i, (i + steps) % count) for i in range(count)])


def swapped(value, axis, mask):
    count = lax.axis_size(axis)
    return lax.ppermute(value, axis, [(i, i ^ mask) for i in range(count)])


def shifted(value, axis):
    count = lax.axis_size(axis)
    return lax.ppermute(value, axis, [(i, i + 1) for i in range(count - 1)])


def shifted_both(value, count):
    pairs = [
        (r * count + c, (r + 1) * count + c + 1)
        for r in range(count - 1)
        for c in range(count - 1)
    ]
    return lax.ppermute(value, ("row", "col"), pairs)


def run_copies(copies):
    for copy in copies:
        copy.start()
    for copy in copies:
        copy.wait()


def span(index, size):
    return pl.ds(pl.multiple_of(index * size, size), size)


def gather_copies(table, pieces, target, sems, size, base=0):
    return [
        pltpu.make_async_copy(piece, target.at[span(table[COL] ^ k, size)], sems.at[base + k])
        for k, piece in enumerate(pieces)
    ]


def window_choice(block_row, group, parent_span):
    padded = jnp.concatenate([jnp.full((HB,), -1, jnp.int32), block_row])
    window = lax.dynamic_slice_in_dim(padded, group * CBD, CBD + HB)
    target = group * parent_span + jnp.arange(parent_span, dtype=jnp.int32)
    places = jnp.arange(1, CBD + HB + 1, dtype=jnp.int32)
    hit = window[None, :] == target[:, None]
    return jnp.sum(jnp.where(hit, places[None, :], 0), axis=1).astype(jnp.int32) - 1


def start_chosen(chosen, choices, target, sem):
    for d, choice in enumerate(choices):

        @pl.when(chosen == d)
        def _():
            pltpu.make_async_copy(choice, target, sem).start()


def turn_of(sc, mask, count):
    return lax.rem(sc[ROW] - (sc[COL] ^ mask) + count, count)


def pivot_product(table, rows, turned, dealt):
    count = len(rows)
    sub, depth = rows[0].shape
    size = count * sub

    def body(*refs):
        sc = refs[0]
        row_refs = refs[1 : 1 + count]
        col_refs = refs[1 + count : 1 + 2 * count]
        deal_refs = refs[1 + 2 * count : 1 + 3 * count]
        out, edge, row_buf, col_buf, front, sems = refs[1 + 3 * count :]
        start_chosen(sc[ROW], col_refs, col_buf, sems.at[count])
        front_parts = [ref.at[pl.ds(0, size)] for ref in deal_refs]
        start_chosen(sc[COL], front_parts, front, sems.at[count + 1])
        run_copies(gather_copies(sc, row_refs, row_buf, sems, sub))
        pltpu.make_async_copy(col_refs[0], col_buf, sems.at[count]).wait()
        pltpu.make_async_copy(front_parts[0], front, sems.at[count + 1]).wait()
        part = front[...] - times_transpose(halves(row_buf[...]), halves(col_buf[...]))
        out[...] = part
        edge[...] = part[-EDGE:]

    return pl.pallas_call(
        body,
        in_specs=[SMEM] + [ANY] * (3 * count),
        out_specs=[VMEM, VMEM],
        out_shape=[f32(size, sub), f32(EDGE, sub)],
        scratch_shapes=[
            pltpu.VMEM((size, depth), jnp.float32),
            pltpu.VMEM((sub, depth), jnp.float32),
            pltpu.VMEM((size, sub), jnp.float32),
            pltpu.SemaphoreType.DMA((count + 2,)),
        ],
        name="pivot_product",
        compiler_params=LIMITS,
    )(table, *rows, *turned, *dealt)


def update_product(table, rows, turned, cols, front):
    count = len(rows)
    sub, depth = rows[0].shape
    size = count * sub

    def body(*refs):
        sc = refs[0]
        row_refs = refs[1 : 1 + count]
        turn_refs = refs[1 + count : 1 + 2 * count]
        col_refs = refs[1 + 2 * count : 3 * count]
        front_ref, out, right, up, corner, row_buf, col_buf, sems = refs[3 * count :]
        home = col_buf.at[span(sc[COL], sub)]
        start_chosen(turn_of(sc, 0, count), turn_refs, home, sems.at[count])
        copies = gather_copies(sc, row_refs, row_buf, sems, sub)
        copies += [
            pltpu.make_async_copy(
                ref, col_buf.at[span(sc[COL] ^ (k + 1), sub)], sems.at[count + 1 + k]
            )
            for k, ref in enumerate(col_refs)
        ]
        run_copies(copies)
        pltpu.make_async_copy(turn_refs[0], home, sems.at[count]).wait()
        part = front_ref[...] - times_transpose(halves(row_buf[...]), halves(col_buf[...]))
        out[...] = part
        right[...] = part[:, -EDGE:]
        up[...] = part[-EDGE:, :]
        corner[...] = part[-EDGE:, -EDGE:]

    return pl.pallas_call(
        body,
        in_specs=[SMEM] + [ANY] * (3 * count - 1) + [VMEM],
        out_specs=[VMEM] * 4,
        out_shape=[f32(size, size), f32(size, EDGE), f32(EDGE, size), f32(EDGE, EDGE)],
        scratch_shapes=[
            pltpu.VMEM((size, depth), jnp.float32),
            pltpu.VMEM((size, depth), jnp.float32),
            pltpu.SemaphoreType.DMA((2 * count,)),
        ],
        name="update_product",
        compiler_params=LIMITS,
    )(table, *rows, *turned, *cols, front)


def pick_for_cols(table, pieces, masks):
    count = len(pieces)

    def body(*refs):
        sc = refs[0]
        ins = refs[1 : 1 + count]
        outs = refs[1 + count : -1]
        sems = refs[-1]
        for i, mask in enumerate(masks):
            start_chosen(turn_of(sc, mask, count), ins, outs[i], sems.at[i])
        for i in range(len(masks)):
            pltpu.make_async_copy(ins[0], outs[i], sems.at[i]).wait()

    return pl.pallas_call(
        body,
        in_specs=[SMEM] + [ANY] * count,
        out_specs=[VMEM] * len(masks),
        out_shape=[f32(*pieces[0].shape)] * len(masks),
        scratch_shapes=[pltpu.SemaphoreType.DMA((len(masks),))],
        name="pick_for_cols",
        compiler_params=LIMITS,
    )(table, *pieces)


def place_rows(table, part, edge):
    size, width = part.shape
    rows = HALF * BLK

    def body(sc, part_ref, edge_ref, keep, send, window):
        window[:EDGE] = edge_ref[...]
        window[EDGE:] = part_ref[...]
        for target, half in ((keep, sc[SIB]), (send, 1 - sc[SIB])):
            for slot in range(HALF):
                place = sc[OWN_ROWS + half * HALF + slot]
                block = window[span(jnp.maximum(place, 0), BLK), :]
                target[slot * BLK : (slot + 1) * BLK, :] = jnp.where(place >= 0, block, 0.0)

    return pl.pallas_call(
        body,
        in_specs=[SMEM, VMEM, VMEM],
        out_specs=[VMEM, VMEM],
        out_shape=[f32(rows, width), f32(rows, width)],
        scratch_shapes=[pltpu.VMEM((size + EDGE, width), jnp.float32)],
        name="place_rows",
        compiler_params=LIMITS,
    )(table, part, edge)


def factor_slice(table, small, dealt, pivot_inverse):
    count = len(small)
    _, rows, sub = small[0].shape
    total = dealt[0].shape[0]
    below = total - PANEL // sub * rows

    def body(*refs):
        sc = refs[0]
        pieces = refs[1 : 1 + count]
        deal_refs = refs[1 + count : 1 + 2 * count]
        inverse_ref, out, order, child, parent, sums, sems = refs[1 + 2 * count :]
        parent_parts = [ref.at[pl.ds(below, total - below)] for ref in deal_refs]
        start_chosen(sc[COL], parent_parts, parent, sems.at[count])
        run_copies(
            [
                pltpu.make_async_copy(piece, order.at[sc[COL] ^ k], sems.at[k])
                for k, piece in enumerate(pieces)
            ]
        )
        pltpu.make_async_copy(parent_parts[0], parent, sems.at[count]).wait()
        for j in range(count):
            block, lane = divmod(j * sub, BLK)
            for sibling in range(2):
                child[sibling, block, :, lane : lane + sub] = order[j, sibling]
            sums[:, j * sub : (j + 1) * sub] = parent[j * rows : (j + 1) * rows]
        for p in range(PIV):
            lanes = slice(p * BLK, (p + 1) * BLK)
            added = sums[:, lanes]
            for sibling, base in ((0, OWN_PIVOT), (1, OTHER_PIVOT)):
                place = sc[base + p]
                block = child[sibling, jnp.maximum(place - HB, 0)]
                added += jnp.where(place >= HB, block, 0.0)
            sums[:, lanes] = added
        out[...] = times_transpose(halves(sums[...]), halves(inverse_ref[...]))

    return pl.pallas_call(
        body,
        in_specs=[SMEM] + [ANY] * (2 * count) + [VMEM],
        out_specs=VMEM,
        out_shape=f32(rows, PANEL),
        scratch_shapes=[
            pltpu.VMEM((count, 2, rows, sub), jnp.float32),
            pltpu.VMEM((2, PIV, rows, BLK), jnp.float32),
            pltpu.VMEM((total - below, sub), jnp.float32),
            pltpu.VMEM((rows, PANEL), jnp.float32),
            pltpu.SemaphoreType.DMA((count + 1,)),
        ],
        name="factor_slice",
        compiler_params=LIMITS,
    )(table, *small, *dealt, pivot_inverse)


def finish(table, parent, own, other, row_pieces, col_own, col_other):
    count = len(row_pieces)
    rows, width = parent.shape
    piece_rows = row_pieces[0].shape[0]
    size = own[0].shape[0]

    def body(*refs):
        sc, parent_ref = refs[:2]
        own_refs, other_refs = refs[2:6], refs[6:10]
        row_refs = refs[10 : 10 + count]
        col_own_refs = refs[10 + count : 10 + 2 * count]
        col_other_refs = refs[10 + 2 * count : 10 + 3 * count]
        out = refs[10 + 3 * count]
        own_win, other_win, row_factor, col_factor, products, sems = refs[11 + 3 * count :]
        low, high = slice(0, EDGE), slice(EDGE, EDGE + size)
        factors = gather_copies(sc, row_refs, row_factor, sems, piece_rows)
        factors += gather_copies(
            sc, col_own_refs, col_factor.at[sc[SIB]], sems, piece_rows, count
        )
        factors += gather_copies(
            sc, col_other_refs, col_factor.at[1 - sc[SIB]], sems, piece_rows, 2 * count
        )
        place = 3 * count
        windows = []
        for refs_in, window in ((own_refs, own_win), (other_refs, other_win)):
            spots = ((high, high), (high, low), (low, high), (low, low))
            for ref, (down, across) in zip(refs_in, spots):
                windows.append(
                    pltpu.make_async_copy(ref, window.at[down, across], sems.at[place])
                )
                place += 1
        for copy in factors + windows:
            copy.start()
        for copy in factors:
            copy.wait()
        left = halves(row_factor[...])
        for half in range(2):
            right = halves(col_factor[half])
            products[:, half * rows : (half + 1) * rows] = times_transpose(left, right)
        for copy in windows:
            copy.wait()
        first_row = (sc[ROW] * 2 + sc[SIB]) * HALF
        first_col = sc[COL] * PBD
        for q in range(PBD):
            cols = slice(q * BLK, (q + 1) * BLK)
            col_inside = first_col + q >= PIV
            for p in range(HALF):
                lines = slice(p * BLK, (p + 1) * BLK)
                total = parent_ref[lines, cols]
                for window, row_base, col_base in (
                    (own_win, OWN_ROWS, OWN_COLS),
                    (other_win, OTHER_ROWS, OTHER_COLS),
                ):
                    down = sc[row_base + sc[SIB] * HALF + p]
                    across = sc[col_base + q]
                    block = window[
                        span(jnp.maximum(down, 0), BLK), span(jnp.maximum(across, 0), BLK)
                    ]
                    total += jnp.where((down >= 0) & (across >= 0), block, 0.0)
                inside = col_inside & (first_row + p >= PIV)
                total = jnp.where(inside, total - products[lines, cols], total)
                if q < PIV:
                    total = jnp.where(sc[COL] == 0, row_factor[lines, cols], total)
                out[lines, cols] = total

    return pl.pallas_call(
        body,
        in_specs=[SMEM, VMEM] + [ANY] * (8 + 3 * count),
        out_specs=VMEM,
        out_shape=f32(rows, width),
        scratch_shapes=[
            pltpu.VMEM((size + EDGE, size + EDGE), jnp.float32),
            pltpu.VMEM((size + EDGE, size + EDGE), jnp.float32),
            pltpu.VMEM((rows, PANEL), jnp.float32),
            pltpu.VMEM((2, rows, PANEL), jnp.float32),
            pltpu.VMEM((rows, 2 * rows), jnp.float32),
            pltpu.SemaphoreType.DMA((3 * count + 8,)),
        ],
        name="finish",
        compiler_params=LIMITS,
    )(table, parent, *own, *other, *row_pieces, *col_own, *col_other)


def shards(child_front, child_panel, block_map, parent_front, pivot_inverse):
    front_index = lax.axis_index("sib")
    row_index = lax.axis_index("row")
    col_index = lax.axis_index("col")
    count = lax.axis_size("col")
    front = child_front[0]
    panel = child_panel[0]
    sub = panel.shape[0]
    parent_rows, parent_cols = parent_front.shape
    parent_span = parent_cols // BLK
    deal = parent_rows // count

    own_map = lax.dynamic_index_in_dim(block_map, front_index, 0, keepdims=False)
    other_map = lax.dynamic_index_in_dim(block_map, 1 - front_index, 0, keepdims=False)
    table = jnp.concatenate(
        [
            jnp.stack([row_index, col_index, front_index]).astype(jnp.int32),
            window_choice(own_map, row_index, parent_span),
            window_choice(other_map, row_index, parent_span),
            window_choice(own_map, col_index, parent_span),
            window_choice(other_map, col_index, parent_span),
            window_choice(own_map, 0, parent_span)[:PIV],
            window_choice(other_map, 0, parent_span)[:PIV],
        ]
    )

    def over_col(values):
        got = []
        for k, value in zip(range(1, count), values):
            got.append(swapped(value, "col", k))
        return got

    def over_row(value):
        got = [value]
        for d in range(1, count):
            got.append(rotated(value, "row", d))
        return got

    def to_sibling(value):
        return swapped(value, "sib", 1)

    turned = over_row(panel)
    rows = [panel] + over_col([panel] * (count - 1))

    dealt = []
    for j in range(count):
        lines = parent_front[j * deal : (j + 1) * deal, :PANEL]
        pieces = [lines[:, i : i + sub] for i in range(0, PANEL, sub)]
        value = jnp.concatenate([front[:, j * sub : (j + 1) * sub]] + pieces, axis=0)
        dealt.append(lax.ppermute(value, "col", [(0, j)]) if j else value)

    part, edge = pivot_product(table, rows, turned, dealt)
    edge = shifted(edge, "row")
    picked = pick_for_cols(table, turned, range(1, count))
    cols = over_col(picked)
    keep, send = place_rows(table, part, edge)
    both = jnp.stack([keep, to_sibling(send)])
    slices = [
        lax.dynamic_slice_in_dim(both, (col_index ^ k) * deal, deal, axis=1)
        for k in range(count)
    ]
    small = [slices[0]] + over_col(slices[1:])
    factor = factor_slice(table, small, dealt, pivot_inverse)
    factors = over_row(factor)
    row_pieces = [factor] + over_col([factor] * (count - 1))

    update, right, up, corner = update_product(table, rows, turned, cols, front)
    right = shifted(right, "col")
    up = shifted(up, "row")
    corner = shifted_both(corner, count)
    own = [update, right, up, corner]

    picked = pick_for_cols(table, factors, range(count))
    col_own = [picked[0]] + over_col(picked[1:])
    col_other = [to_sibling(value) for value in col_own]

    other = [to_sibling(value) for value in own]
    return finish(table, parent_front, own, other, row_pieces, col_own, col_other)


def solution(mesh):
    in_specs = (
        P("sib", "row", "col"),
        P("sib", ("row", "col"), None),
        P(),
        P(("row", "sib"), "col"),
        P(),
    )
    out_specs = P(("row", "sib"), "col")

    return jax.shard_map(shards, mesh=mesh, in_specs=in_specs, out_specs=out_specs, check_vma=False)
```

```python
import jax
import jax.numpy as jnp
from jax import lax
from jax.experimental import pallas as pl
from jax.experimental.pallas import tpu as pltpu
from jax.sharding import PartitionSpec as P


BLK = 128
CBD = 4
PBD = 6
HB = 2
PIV = 4
PANEL = 512
HALF = PBD // 2
EDGE = HB * BLK


SMEM = pl.BlockSpec(memory_space=pltpu.SMEM)
VMEM = pl.BlockSpec(memory_space=pltpu.VMEM)
ANY = pl.BlockSpec(memory_space=pl.ANY)


def limit_for(sub, mebibytes):
    if sub < BLK:
        mebibytes = 56
    return pltpu.CompilerParams(vmem_limit_bytes=mebibytes << 20)


ROW, COL, SIB = 0, 1, 2
OWN_ROWS, OTHER_ROWS, OWN_COLS, OTHER_COLS = 3, 9, 15, 21
OWN_PIVOT, OTHER_PIVOT = 27, 31


def f32(*shape):
    return jax.ShapeDtypeStruct(shape, jnp.float32)


def halves(value):
    high = value.astype(jnp.bfloat16)
    low = (value - high.astype(jnp.float32)).astype(jnp.bfloat16)
    return high, low


def times_transpose(left, right):
    def dot(x, y):
        return lax.dot_general(
            x, y, (((1,), (1,)), ((), ())), preferred_element_type=jnp.float32
        )

    return dot(left[0], right[0]) + (dot(left[0], right[1]) + dot(left[1], right[0]))


def rotated(value, axis, steps):
    count = lax.axis_size(axis)
    return lax.ppermute(value, axis, [(i, (i + steps) % count) for i in range(count)])


def swapped(value, axis, mask):
    count = lax.axis_size(axis)
    return lax.ppermute(value, axis, [(i, i ^ mask) for i in range(count)])


def shifted(value, axis):
    count = lax.axis_size(axis)
    return lax.ppermute(value, axis, [(i, i + 1) for i in range(count - 1)])


def run_copies(copies):
    for copy in copies:
        copy.start()
    for copy in copies:
        copy.wait()


def span(index, size):
    return pl.ds(pl.multiple_of(index * size, size), size)


def gather_copies(table, pieces, target, sems, size, base=0):
    return [
        pltpu.make_async_copy(piece, target.at[span(table[COL] ^ k, size)], sems.at[base + k])
        for k, piece in enumerate(pieces)
    ]


def window_choice(block_row, group, parent_span):
    padded = jnp.concatenate([jnp.full((HB,), -1, jnp.int32), block_row])
    window = lax.dynamic_slice_in_dim(padded, group * CBD, CBD + HB)
    target = group * parent_span + jnp.arange(parent_span, dtype=jnp.int32)
    places = jnp.arange(1, CBD + HB + 1, dtype=jnp.int32)
    hit = window[None, :] == target[:, None]
    return jnp.sum(jnp.where(hit, places[None, :], 0), axis=1).astype(jnp.int32) - 1


def start_chosen(chosen, choices, target, sem):
    for d, choice in enumerate(choices):

        @pl.when(chosen == d)
        def _():
            pltpu.make_async_copy(choice, target, sem).start()


def turn_of(sc, mask, count):
    return lax.rem(sc[ROW] - (sc[COL] ^ mask) + count, count)


def slice_place(sc, mask, count):
    half = count // 2
    diff = sc[ROW] - (sc[COL] ^ mask)
    near = (diff < 0) & (-diff < half)
    return jnp.where(near, 2 * half - 1 - diff, jnp.abs(diff))


def around_row(value):
    count = lax.axis_size("row")
    half = count // 2
    middle = rotated(value, "row", half)
    below, above, far = [], [], []
    for d in range(1, half):
        below.append(lax.ppermute(value, "row", [(i, i + d) for i in range(count - d)]))
        above.append(lax.ppermute(value, "row", [(i + d, i) for i in range(count - d)]))
        pairs = [(i, i + d) for i in range(half, count - d)]
        pairs += [(i, i - d) for i in range(d, half)]
        far.append(lax.ppermute(middle, "row", pairs))
    return [value] + below + [middle] + far + above


def slice_products(table, rows, around, fronts):
    count = len(rows)
    many = len(around)
    sub, depth = rows[0].shape
    size = count * sub

    def body(*refs):
        sc = refs[0]
        row_refs = refs[1 : 1 + count]
        around_refs = refs[1 + count : 1 + count + many]
        front_refs = refs[1 + count + many : 1 + 2 * count + many]
        outs = refs[1 + 2 * count + many :][:count]
        pivot, edge, up, previous, row_buf, col_buf, sems = refs[1 + 3 * count + many :]
        for m in range(count):
            group = sc[COL] ^ m
            start_chosen(
                slice_place(sc, m, count),
                around_refs,
                col_buf.at[span(group, sub)],
                sems.at[count + m],
            )
        run_copies(gather_copies(sc, row_refs, row_buf, sems, sub))
        for m in range(count):
            group = sc[COL] ^ m
            pltpu.make_async_copy(
                around_refs[0], col_buf.at[span(group, sub)], sems.at[count + m]
            ).wait()
        left = halves(row_buf[...])
        for m in range(count):
            group = sc[COL] ^ m
            right = halves(col_buf[span(group, sub), :])
            part = front_refs[m][...] - times_transpose(left, right)
            outs[m][...] = part

            @pl.when(group == 0)
            def _():
                pivot[...] = part
                edge[...] = part[-EDGE:]

            @pl.when(group > 0)
            def _():
                up[group - 1] = part[-EDGE:]

            @pl.when(group < count - 1)
            def _():
                previous[group] = part

    return pl.pallas_call(
        body,
        in_specs=[SMEM] + [ANY] * (count + many) + [VMEM] * count,
        out_specs=[VMEM] * (count + 4),
        out_shape=[f32(size, sub)] * (count + 1)
        + [f32(EDGE, sub), f32(count - 1, EDGE, sub), f32(count - 1, size, sub)],
        scratch_shapes=[
            pltpu.VMEM((size, depth), jnp.float32),
            pltpu.VMEM((size, depth), jnp.float32),
            pltpu.SemaphoreType.DMA((2 * count,)),
        ],
        compiler_params=limit_for(sub, 24),
        name="slice_products",
    )(table, *rows, *around, *fronts)


def pack_halo(table, previous, edge, up):
    less, size, sub = previous.shape
    count = less + 1

    def body(sc, previous_ref, edge_ref, up_ref, *refs):
        outs, ups, sems = refs[:count], refs[count], refs[count + 1]
        run_copies(
            [
                pltpu.make_async_copy(edge_ref, ups.at[0], sems.at[0]),
                pltpu.make_async_copy(up_ref, ups.at[pl.ds(1, less)], sems.at[1]),
            ]
        )
        copies = []
        for m, out in enumerate(outs):
            group = sc[COL] ^ m
            before = jnp.maximum(group - 1, 0)
            parts = (
                (previous_ref.at[before], pl.ds(0, size)),
                (ups.at[group], pl.ds(size, EDGE)),
                (ups.at[before], pl.ds(size + EDGE, EDGE)),
            )
            copies += [
                pltpu.make_async_copy(part, out.at[place], sems.at[3 * m + i])
                for i, (part, place) in enumerate(parts)
            ]
        run_copies(copies)

    return pl.pallas_call(
        body,
        in_specs=[SMEM] + [ANY] * 3,
        out_specs=[VMEM] * count,
        out_shape=[f32(size + 2 * EDGE, sub)] * count,
        scratch_shapes=[
            pltpu.VMEM((count, EDGE, sub), jnp.float32),
            pltpu.SemaphoreType.DMA((3 * count,)),
        ],
        compiler_params=limit_for(sub, 16),
        name="pack_halo",
    )(table, previous, edge, up)


def pick_for_cols(table, pieces, masks):
    count = len(pieces)

    def body(*refs):
        sc = refs[0]
        ins = refs[1 : 1 + count]
        outs = refs[1 + count : -1]
        sems = refs[-1]
        for i, mask in enumerate(masks):
            start_chosen(turn_of(sc, mask, count), ins, outs[i], sems.at[i])
        for i in range(len(masks)):
            pltpu.make_async_copy(ins[0], outs[i], sems.at[i]).wait()

    return pl.pallas_call(
        body,
        in_specs=[SMEM] + [ANY] * count,
        out_specs=[VMEM] * len(masks),
        out_shape=[f32(*pieces[0].shape)] * len(masks),
        scratch_shapes=[pltpu.SemaphoreType.DMA((len(masks),))],
        compiler_params=limit_for(BLK, 16),
        name="pick_for_cols",
    )(table, *pieces)


def place_rows(table, part, edge):
    size, width = part.shape
    rows = HALF * BLK

    def body(sc, part_ref, edge_ref, keep, send, window):
        window[:EDGE] = edge_ref[...]
        window[EDGE:] = part_ref[...]
        for target, half in ((keep, sc[SIB]), (send, 1 - sc[SIB])):
            for slot in range(HALF):
                place = sc[OWN_ROWS + half * HALF + slot]
                block = window[span(jnp.maximum(place, 0), BLK), :]
                target[slot * BLK : (slot + 1) * BLK, :] = jnp.where(place >= 0, block, 0.0)

    return pl.pallas_call(
        body,
        in_specs=[SMEM, VMEM, VMEM],
        out_specs=[VMEM, VMEM],
        out_shape=[f32(rows, width), f32(rows, width)],
        scratch_shapes=[pltpu.VMEM((size + EDGE, width), jnp.float32)],
        name="place_rows",
        compiler_params=limit_for(width, 16),
    )(table, part, edge)


def factor_slice(table, small, dealt, pivot_inverse):
    count = len(small)
    _, rows, sub = small[0].shape

    def body(*refs):
        sc = refs[0]
        pieces = refs[1 : 1 + count]
        deal_refs = refs[1 + count : 1 + 2 * count]
        inverse_ref, out, order, child, sums, sems = refs[1 + 2 * count :]
        start_chosen(sc[COL], deal_refs, sums, sems.at[count])
        run_copies(
            [
                pltpu.make_async_copy(piece, order.at[sc[COL] ^ k], sems.at[k])
                for k, piece in enumerate(pieces)
            ]
        )
        for j in range(count):
            block, lane = divmod(j * sub, BLK)
            for sibling in range(2):
                child[sibling, block, :, lane : lane + sub] = order[j, sibling]
        pltpu.make_async_copy(deal_refs[0], sums, sems.at[count]).wait()
        for p in range(PIV):
            lanes = slice(p * BLK, (p + 1) * BLK)
            added = sums[:, lanes]
            for sibling, base in ((0, OWN_PIVOT), (1, OTHER_PIVOT)):
                place = sc[base + p]
                block = child[sibling, jnp.maximum(place - HB, 0)]
                added += jnp.where(place >= HB, block, 0.0)
            sums[:, lanes] = added
        out[...] = times_transpose(halves(sums[...]), halves(inverse_ref[...]))

    return pl.pallas_call(
        body,
        in_specs=[SMEM] + [ANY] * (2 * count) + [VMEM],
        out_specs=VMEM,
        out_shape=f32(rows, PANEL),
        scratch_shapes=[
            pltpu.VMEM((count, 2, rows, sub), jnp.float32),
            pltpu.VMEM((2, PIV, rows, BLK), jnp.float32),
            pltpu.VMEM((rows, PANEL), jnp.float32),
            pltpu.SemaphoreType.DMA((count + 1,)),
        ],
        compiler_params=limit_for(sub, 16),
        name="factor_slice",
    )(table, *small, *dealt, pivot_inverse)


def finish(table, parent, own, other, row_pieces, col_own, col_other):
    count = len(row_pieces)
    rows, width = parent.shape
    piece_rows = row_pieces[0].shape[0]
    size, sub = own[0].shape
    half = count // 2
    split = BLK // sub

    def body(*refs):
        sc, parent_ref = refs[:2]
        own_refs, other_refs = refs[2 : 2 + 2 * count], refs[2 + 2 * count : 2 + 4 * count]
        at = 2 + 4 * count
        row_refs = refs[at : at + count]
        col_own_refs = refs[at + count : at + 2 * count]
        col_other_refs = refs[at + 2 * count : at + 3 * count]
        out = refs[at + 3 * count]
        own_win, other_win, row_factor, col_factor, products, sems = refs[at + 3 * count + 1 :]
        factors = gather_copies(sc, row_refs, row_factor, sems, piece_rows)
        factors += gather_copies(
            sc, col_own_refs, col_factor.at[sc[SIB]], sems, piece_rows, count
        )
        factors += gather_copies(
            sc, col_other_refs, col_factor.at[1 - sc[SIB]], sems, piece_rows, 2 * count
        )
        at = 3 * count
        always, edges = [], []
        for refs_in, window in ((own_refs, own_win), (other_refs, other_win)):
            for m in range(count):
                home, halo = refs_in[m], refs_in[count + m]
                piece = sc[COL] ^ m
                main = half + piece
                side = jnp.maximum(piece - half, 0)
                low, high = pl.ds(0, EDGE), pl.ds(EDGE, size)
                always += [
                    pltpu.make_async_copy(home, window.at[main, high], sems.at[at]),
                    pltpu.make_async_copy(
                        halo.at[pl.ds(size, EDGE)], window.at[main, low], sems.at[at + 1]
                    ),
                ]
                edges += [
                    (
                        piece,
                        pltpu.make_async_copy(
                            halo.at[pl.ds(0, size)], window.at[side, high], sems.at[at + 2]
                        ),
                        pltpu.make_async_copy(
                            halo.at[pl.ds(size + EDGE, EDGE)],
                            window.at[side, low],
                            sems.at[at + 3],
                        ),
                    )
                ]
                at += 4
        for copy in factors + always:
            copy.start()
        for piece, first, second in edges:

            @pl.when(piece >= half)
            def _():
                first.start()
                second.start()

        for copy in factors:
            copy.wait()
        left = halves(row_factor[...])
        for side in range(2):
            right = halves(col_factor[side])
            products[:, side * rows : (side + 1) * rows] = times_transpose(left, right)
        for copy in always:
            copy.wait()
        for piece, first, second in edges:

            @pl.when(piece >= half)
            def _():
                first.wait()
                second.wait()

        first_row = (sc[ROW] * 2 + sc[SIB]) * HALF
        first_col = sc[COL] * PBD
        for q in range(PBD):
            cols = slice(q * BLK, (q + 1) * BLK)
            col_inside = first_col + q >= PIV
            for p in range(HALF):
                lines = slice(p * BLK, (p + 1) * BLK)
                total = parent_ref[lines, cols]
                for window, row_base, col_base in (
                    (own_win, OWN_ROWS, OWN_COLS),
                    (other_win, OTHER_ROWS, OTHER_COLS),
                ):
                    down = sc[row_base + sc[SIB] * HALF + p]
                    across = sc[col_base + q]
                    start = jnp.maximum(across, 0) * split
                    pieces = [
                        window[start + i, span(jnp.maximum(down, 0), BLK), :] for i in range(split)
                    ]
                    block = pieces[0] if split == 1 else jnp.concatenate(pieces, axis=1)
                    total += jnp.where((down >= 0) & (across >= 0), block, 0.0)
                inside = col_inside & (first_row + p >= PIV)
                total = jnp.where(inside, total - products[lines, cols], total)
                if q < PIV:
                    total = jnp.where(sc[COL] == 0, row_factor[lines, cols], total)
                out[lines, cols] = total

    return pl.pallas_call(
        body,
        in_specs=[SMEM, VMEM] + [ANY] * (7 * count),
        out_specs=VMEM,
        out_shape=f32(rows, width),
        scratch_shapes=[
            pltpu.VMEM((half + count, size + EDGE, sub), jnp.float32),
            pltpu.VMEM((half + count, size + EDGE, sub), jnp.float32),
            pltpu.VMEM((rows, PANEL), jnp.float32),
            pltpu.VMEM((2, rows, PANEL), jnp.float32),
            pltpu.VMEM((rows, 2 * rows), jnp.float32),
            pltpu.SemaphoreType.DMA((11 * count,)),
        ],
        compiler_params=limit_for(sub, 24),
        name="finish",
    )(table, parent, *own, *other, *row_pieces, *col_own, *col_other)


def shards(child_front, child_panel, block_map, parent_front, pivot_inverse):
    front_index = lax.axis_index("sib")
    row_index = lax.axis_index("row")
    col_index = lax.axis_index("col")
    count = lax.axis_size("col")
    front = child_front[0]
    panel = child_panel[0]
    sub = panel.shape[0]
    parent_rows, parent_cols = parent_front.shape
    parent_span = parent_cols // BLK
    deal = parent_rows // count

    own_map = lax.dynamic_index_in_dim(block_map, front_index, 0, keepdims=False)
    other_map = lax.dynamic_index_in_dim(block_map, 1 - front_index, 0, keepdims=False)
    table = jnp.concatenate(
        [
            jnp.stack([row_index, col_index, front_index]).astype(jnp.int32),
            window_choice(own_map, row_index, parent_span),
            window_choice(other_map, row_index, parent_span),
            window_choice(own_map, col_index, parent_span),
            window_choice(other_map, col_index, parent_span),
            window_choice(own_map, 0, parent_span)[:PIV],
            window_choice(other_map, 0, parent_span)[:PIV],
        ]
    )

    def over_col(values):
        got = []
        for k, value in zip(range(1, count), values):
            got.append(swapped(value, "col", k))
        return got

    def over_row(value):
        got = [value]
        for d in range(1, count):
            got.append(rotated(value, "row", d))
        return got

    def to_sibling(value):
        return swapped(value, "sib", 1)

    around = around_row(panel)
    rows = [panel] + over_col([panel] * (count - 1))
    slices = [
        lax.dynamic_slice_in_dim(front, (col_index ^ k) * sub, sub, axis=1) for k in range(count)
    ]
    fronts = [slices[0]] + over_col(slices[1:])

    dealt = []
    for j in range(count):
        value = parent_front[j * deal : (j + 1) * deal, :PANEL]
        dealt.append(lax.ppermute(value, "col", [(0, j)]) if j else value)

    *homes, pivot, edge, up, previous = slice_products(table, rows, around, fronts)
    edge = shifted(edge, "row")
    own = [homes[0]] + over_col(homes[1:])
    up = shifted(up, "row")

    keep, send = place_rows(table, pivot, edge)
    both = jnp.stack([keep, to_sibling(send)])
    slices = [
        lax.dynamic_slice_in_dim(both, (col_index ^ k) * deal, deal, axis=1)
        for k in range(count)
    ]
    small = [slices[0]] + over_col(slices[1:])
    packed = pack_halo(table, previous, edge, up)
    own = own + [packed[0]] + over_col(packed[1:])
    factor = factor_slice(table, small, dealt, pivot_inverse)
    factors = over_row(factor)
    row_pieces = [factor] + over_col([factor] * (count - 1))

    picked = pick_for_cols(table, factors, range(count))
    col_own = [picked[0]] + over_col(picked[1:])
    col_other = [to_sibling(value) for value in col_own]

    other = [to_sibling(value) for value in own]
    return finish(table, parent_front, own, other, row_pieces, col_own, col_other)


def solution(mesh):
    in_specs = (
        P("sib", "row", "col"),
        P("sib", ("row", "col"), None),
        P(),
        P(("row", "sib"), "col"),
        P(),
    )
    out_specs = P(("row", "sib"), "col")

    return jax.shard_map(shards, mesh=mesh, in_specs=in_specs, out_specs=out_specs, check_vma=False)
```

```python
import jax
import jax.numpy as jnp
from jax import lax
from jax.experimental import pallas as pl
from jax.experimental.pallas import tpu as pltpu
from jax.sharding import PartitionSpec as P


BLK = 128
CBD = 4
PBD = 6
HB = 2
PIV = 4
PANEL = 512
HALF = PBD // 2
EDGE = HB * BLK


SMEM = pl.BlockSpec(memory_space=pltpu.SMEM)
VMEM = pl.BlockSpec(memory_space=pltpu.VMEM)
ANY = pl.BlockSpec(memory_space=pl.ANY)


def limit_for(sub, mebibytes):
    if sub < BLK:
        mebibytes = 56
    return pltpu.CompilerParams(vmem_limit_bytes=mebibytes << 20)


ROW, COL, SIB = 0, 1, 2
OWN_ROWS, OTHER_ROWS, OWN_COLS, OTHER_COLS = 3, 9, 15, 21
OWN_PIVOT, OTHER_PIVOT = 27, 31


def f32(*shape):
    return jax.ShapeDtypeStruct(shape, jnp.float32)


def halves(value):
    high = value.astype(jnp.bfloat16)
    low = (value - high.astype(jnp.float32)).astype(jnp.bfloat16)
    return high, low


def times_transpose(left, right):
    def dot(x, y):
        return lax.dot_general(
            x, y, (((1,), (1,)), ((), ())), preferred_element_type=jnp.float32
        )

    return dot(left[0], right[0]) + (dot(left[0], right[1]) + dot(left[1], right[0]))


def rotated(value, axis, steps):
    count = lax.axis_size(axis)
    return lax.ppermute(value, axis, [(i, (i + steps) % count) for i in range(count)])


def swapped(value, axis, mask):
    count = lax.axis_size(axis)
    return lax.ppermute(value, axis, [(i, i ^ mask) for i in range(count)])


def shifted(value, axis):
    count = lax.axis_size(axis)
    return lax.ppermute(value, axis, [(i, i + 1) for i in range(count - 1)])


def run_copies(copies):
    for copy in copies:
        copy.start()
    for copy in copies:
        copy.wait()


def span(index, size):
    return pl.ds(pl.multiple_of(index * size, size), size)


def gather_copies(table, pieces, target, sems, size, base=0):
    return [
        pltpu.make_async_copy(piece, target.at[span(table[COL] ^ k, size)], sems.at[base + k])
        for k, piece in enumerate(pieces)
    ]


def window_choice(block_row, group, parent_span):
    padded = jnp.concatenate([jnp.full((HB,), -1, jnp.int32), block_row])
    window = lax.dynamic_slice_in_dim(padded, group * CBD, CBD + HB)
    target = group * parent_span + jnp.arange(parent_span, dtype=jnp.int32)
    places = jnp.arange(1, CBD + HB + 1, dtype=jnp.int32)
    hit = window[None, :] == target[:, None]
    return jnp.sum(jnp.where(hit, places[None, :], 0), axis=1).astype(jnp.int32) - 1


def start_chosen(chosen, choices, target, sem):
    for d, choice in enumerate(choices):

        @pl.when(chosen == d)
        def _():
            pltpu.make_async_copy(choice, target, sem).start()


def turn_of(sc, mask, count):
    return lax.rem(sc[ROW] - (sc[COL] ^ mask) + count, count)


def slice_place(sc, mask, count):
    half = count // 2
    diff = sc[ROW] - (sc[COL] ^ mask)
    near = (diff < 0) & (-diff < half)
    return jnp.where(near, 2 * half - 1 - diff, jnp.abs(diff))


def around_row(value):
    count = lax.axis_size("row")
    half = count // 2
    middle = rotated(value, "row", half)
    below, above, far = [], [], []
    for d in range(1, half):
        below.append(lax.ppermute(value, "row", [(i, i + d) for i in range(count - d)]))
        above.append(lax.ppermute(value, "row", [(i + d, i) for i in range(count - d)]))
        pairs = [(i, i + d) for i in range(half, count - d)]
        pairs += [(i, i - d) for i in range(d, half)]
        far.append(lax.ppermute(middle, "row", pairs))
    return [value] + below + [middle] + far + above


def slice_products(table, rows, around, fronts):
    count = len(rows)
    many = len(around)
    sub, depth = rows[0].shape
    size = count * sub

    def body(*refs):
        sc = refs[0]
        row_refs = refs[1 : 1 + count]
        around_refs = refs[1 + count : 1 + count + many]
        front_refs = refs[1 + count + many : 1 + 2 * count + many]
        outs = refs[1 + 2 * count + many :][:count]
        edge, up, row_buf, col_buf, sems = refs[1 + 3 * count + many :]
        places = [col_buf.at[m * sub : (m + 1) * sub] for m in range(count)]
        rows_in = gather_copies(sc, row_refs, row_buf, sems, sub)
        for copy in rows_in:
            copy.start()
        for m, place in enumerate(places):
            start_chosen(slice_place(sc, m, count), around_refs, place, sems.at[count + m])
        for copy in rows_in:
            copy.wait()
        left = halves(row_buf[...])
        for m, place in enumerate(places):
            pltpu.make_async_copy(around_refs[0], place, sems.at[count + m]).wait()
        product = times_transpose(left, halves(col_buf[...]))
        for m in range(count):
            group = sc[COL] ^ m
            part = front_refs[m][...] - product[:, m * sub : (m + 1) * sub]
            outs[m][...] = part

            @pl.when(group == 0)
            def _():
                edge[...] = part[-EDGE:]

            @pl.when(group > 0)
            def _():
                up[group - 1] = part[-EDGE:]

    return pl.pallas_call(
        body,
        in_specs=[SMEM] + [ANY] * (count + many) + [VMEM] * count,
        out_specs=[VMEM] * (count + 2),
        out_shape=[f32(size, sub)] * count + [f32(EDGE, sub), f32(count - 1, EDGE, sub)],
        scratch_shapes=[
            pltpu.VMEM((size, depth), jnp.float32),
            pltpu.VMEM((size, depth), jnp.float32),
            pltpu.SemaphoreType.DMA((2 * count,)),
        ],
        compiler_params=limit_for(sub, 20),
        name="slice_products",
    )(table, *rows, *around, *fronts)


def pack_halo(table, homes, edge, up):
    count = len(homes)
    size, sub = homes[0].shape

    def body(*refs):
        sc = refs[0]
        home_refs = refs[1 : 1 + count]
        edge_ref, up_ref = refs[1 + count : 3 + count]
        outs = refs[3 + count : 3 + 2 * count]
        sems = refs[-1]
        near, far = pl.ds(size, EDGE), pl.ds(size + EDGE, EDGE)
        for m, out in enumerate(outs):
            group = sc[COL] ^ m
            before = jnp.maximum(group - 1, 0)
            start_chosen(before ^ sc[COL], home_refs, out.at[pl.ds(0, size)], sems.at[3 * m])
            for i, (wanted, place) in enumerate(((group, near), (before, far))):

                @pl.when(wanted == 0)
                def _():
                    pltpu.make_async_copy(edge_ref, out.at[place], sems.at[3 * m + 1 + i]).start()

                @pl.when(wanted > 0)
                def _():
                    pltpu.make_async_copy(
                        up_ref.at[jnp.maximum(wanted - 1, 0)], out.at[place], sems.at[3 * m + 1 + i]
                    ).start()

        for m, out in enumerate(outs):
            pltpu.make_async_copy(home_refs[0], out.at[pl.ds(0, size)], sems.at[3 * m]).wait()
            for i, place in enumerate((near, far)):
                pltpu.make_async_copy(edge_ref, out.at[place], sems.at[3 * m + 1 + i]).wait()

    return pl.pallas_call(
        body,
        in_specs=[SMEM] + [ANY] * (count + 2),
        out_specs=[VMEM] * count,
        out_shape=[f32(size + 2 * EDGE, sub)] * count,
        scratch_shapes=[pltpu.SemaphoreType.DMA((3 * count,))],
        compiler_params=limit_for(sub, 8),
        name="pack_halo",
    )(table, *homes, edge, up)


def pick_for_cols(table, pieces, masks):
    count = len(pieces)

    def body(*refs):
        sc = refs[0]
        ins = refs[1 : 1 + count]
        outs = refs[1 + count : -1]
        sems = refs[-1]
        for i, mask in enumerate(masks):
            start_chosen(turn_of(sc, mask, count), ins, outs[i], sems.at[i])
        for i in range(len(masks)):
            pltpu.make_async_copy(ins[0], outs[i], sems.at[i]).wait()

    return pl.pallas_call(
        body,
        in_specs=[SMEM] + [ANY] * count,
        out_specs=[VMEM] * len(masks),
        out_shape=[f32(*pieces[0].shape)] * len(masks),
        scratch_shapes=[pltpu.SemaphoreType.DMA((len(masks),))],
        compiler_params=limit_for(BLK, 16),
        name="pick_for_cols",
    )(table, *pieces)


def place_rows(table, homes, edge):
    count = len(homes)
    size, width = homes[0].shape
    rows = HALF * BLK

    def body(*refs):
        sc = refs[0]
        home_refs = refs[1 : 1 + count]
        edge_ref, keep, send, window, sems = refs[1 + count :]
        main = window.at[pl.ds(EDGE, size)]
        start_chosen(sc[COL], home_refs, main, sems.at[0])
        copy = pltpu.make_async_copy(edge_ref, window.at[pl.ds(0, EDGE)], sems.at[1])
        copy.start()
        copy.wait()
        pltpu.make_async_copy(home_refs[0], main, sems.at[0]).wait()
        for target, half in ((keep, sc[SIB]), (send, 1 - sc[SIB])):
            for slot in range(HALF):
                place = sc[OWN_ROWS + half * HALF + slot]
                block = window[span(jnp.maximum(place, 0), BLK), :]
                target[slot * BLK : (slot + 1) * BLK, :] = jnp.where(place >= 0, block, 0.0)

    return pl.pallas_call(
        body,
        in_specs=[SMEM] + [ANY] * (count + 1),
        out_specs=[VMEM, VMEM],
        out_shape=[f32(rows, width), f32(rows, width)],
        scratch_shapes=[
            pltpu.VMEM((size + EDGE, width), jnp.float32),
            pltpu.SemaphoreType.DMA((2,)),
        ],
        compiler_params=limit_for(width, 8),
        name="place_rows",
    )(table, *homes, edge)


def factor_slice(table, small, dealt, pivot_inverse):
    count = len(small)
    _, rows, sub = small[0].shape

    def body(*refs):
        sc = refs[0]
        pieces = refs[1 : 1 + count]
        deal_refs = refs[1 + count : 1 + 2 * count]
        inverse_ref, out, order, child, sums, sems = refs[1 + 2 * count :]
        start_chosen(sc[COL], deal_refs, sums, sems.at[count])
        run_copies(
            [
                pltpu.make_async_copy(piece, order.at[sc[COL] ^ k], sems.at[k])
                for k, piece in enumerate(pieces)
            ]
        )
        for j in range(count):
            block, lane = divmod(j * sub, BLK)
            for sibling in range(2):
                child[sibling, block, :, lane : lane + sub] = order[j, sibling]
        pltpu.make_async_copy(deal_refs[0], sums, sems.at[count]).wait()
        for p in range(PIV):
            lanes = slice(p * BLK, (p + 1) * BLK)
            added = sums[:, lanes]
            for sibling, base in ((0, OWN_PIVOT), (1, OTHER_PIVOT)):
                place = sc[base + p]
                block = child[sibling, jnp.maximum(place - HB, 0)]
                added += jnp.where(place >= HB, block, 0.0)
            sums[:, lanes] = added
        out[...] = times_transpose(halves(sums[...]), halves(inverse_ref[...]))

    return pl.pallas_call(
        body,
        in_specs=[SMEM] + [ANY] * (2 * count) + [VMEM],
        out_specs=VMEM,
        out_shape=f32(rows, PANEL),
        scratch_shapes=[
            pltpu.VMEM((count, 2, rows, sub), jnp.float32),
            pltpu.VMEM((2, PIV, rows, BLK), jnp.float32),
            pltpu.VMEM((rows, PANEL), jnp.float32),
            pltpu.SemaphoreType.DMA((count + 1,)),
        ],
        compiler_params=limit_for(sub, 16),
        name="factor_slice",
    )(table, *small, *dealt, pivot_inverse)


def assemble(table, parent, own, other):
    count = len(own) // 2
    rows, width = parent.shape
    size, sub = own[0].shape
    half = count // 2
    split = BLK // sub

    def body(*refs):
        sc, parent_ref = refs[:2]
        own_refs, other_refs = refs[2 : 2 + 2 * count], refs[2 + 2 * count : 2 + 4 * count]
        out, own_win, other_win, sems = refs[2 + 4 * count :]
        at = 0
        always, edges = [], []
        for refs_in, window in ((own_refs, own_win), (other_refs, other_win)):
            for m in range(count):
                home, halo = refs_in[m], refs_in[count + m]
                piece = sc[COL] ^ m
                main = half + piece
                side = jnp.maximum(piece - half, 0)
                low, high = pl.ds(0, EDGE), pl.ds(EDGE, size)
                always += [
                    pltpu.make_async_copy(home, window.at[main, high], sems.at[at]),
                    pltpu.make_async_copy(
                        halo.at[pl.ds(size, EDGE)], window.at[main, low], sems.at[at + 1]
                    ),
                ]
                edges += [
                    (
                        piece,
                        pltpu.make_async_copy(
                            halo.at[pl.ds(0, size)], window.at[side, high], sems.at[at + 2]
                        ),
                        pltpu.make_async_copy(
                            halo.at[pl.ds(size + EDGE, EDGE)],
                            window.at[side, low],
                            sems.at[at + 3],
                        ),
                    )
                ]
                at += 4
        for copy in always:
            copy.start()
        for piece, first, second in edges:

            @pl.when(piece >= half)
            def _():
                first.start()
                second.start()

        for copy in always:
            copy.wait()
        for piece, first, second in edges:

            @pl.when(piece >= half)
            def _():
                first.wait()
                second.wait()

        for q in range(PBD):
            cols = slice(q * BLK, (q + 1) * BLK)
            for p in range(HALF):
                lines = slice(p * BLK, (p + 1) * BLK)
                total = parent_ref[lines, cols]
                for window, row_base, col_base in (
                    (own_win, OWN_ROWS, OWN_COLS),
                    (other_win, OTHER_ROWS, OTHER_COLS),
                ):
                    down = sc[row_base + sc[SIB] * HALF + p]
                    across = sc[col_base + q]
                    start = jnp.maximum(across, 0) * split
                    pieces = [
                        window[start + i, span(jnp.maximum(down, 0), BLK), :] for i in range(split)
                    ]
                    block = pieces[0] if split == 1 else jnp.concatenate(pieces, axis=1)
                    total += jnp.where((down >= 0) & (across >= 0), block, 0.0)
                out[lines, cols] = total

    return pl.pallas_call(
        body,
        in_specs=[SMEM, VMEM] + [ANY] * (4 * count),
        out_specs=VMEM,
        out_shape=f32(rows, width),
        scratch_shapes=[
            pltpu.VMEM((half + count, size + EDGE, sub), jnp.float32),
            pltpu.VMEM((half + count, size + EDGE, sub), jnp.float32),
            pltpu.SemaphoreType.DMA((8 * count,)),
        ],
        compiler_params=limit_for(sub, 12),
        name="assemble",
    )(table, parent, *own, *other)


def finish(table, assembled, row_pieces, col_own, col_other):
    count = len(row_pieces)
    rows, width = assembled.shape
    piece_rows = row_pieces[0].shape[0]

    def body(*refs):
        sc = refs[0]
        row_refs = refs[1 : 1 + count]
        col_own_refs = refs[1 + count : 1 + 2 * count]
        col_other_refs = refs[1 + 2 * count : 1 + 3 * count]
        base_ref, out, row_factor, col_factor, sems = refs[1 + 3 * count :]
        copies = [
            gather_copies(sc, row_refs, row_factor, sems, piece_rows),
            gather_copies(sc, col_own_refs, col_factor.at[sc[SIB]], sems, piece_rows, count),
            gather_copies(
                sc, col_other_refs, col_factor.at[1 - sc[SIB]], sems, piece_rows, 2 * count
            ),
        ]
        for copy in sum(copies, []):
            copy.start()
        for copy in copies[0]:
            copy.wait()
        left = halves(row_factor[...])
        for copy in copies[1] + copies[2]:
            copy.wait()
        first_row = (sc[ROW] * 2 + sc[SIB]) * HALF
        first_col = sc[COL] * PBD
        for side in range(2):
            product = times_transpose(left, halves(col_factor[side]))
            for i in range(HALF):
                q = side * HALF + i
                cols = slice(q * BLK, (q + 1) * BLK)
                for p in range(HALF):
                    lines = slice(p * BLK, (p + 1) * BLK)
                    total = base_ref[lines, cols]
                    inside = (first_col + q >= PIV) & (first_row + p >= PIV)
                    reduced = total - product[lines, i * BLK : (i + 1) * BLK]
                    total = jnp.where(inside, reduced, total)
                    if q < PIV:
                        total = jnp.where(sc[COL] == 0, row_factor[lines, cols], total)
                    out[lines, cols] = total

    return pl.pallas_call(
        body,
        in_specs=[SMEM] + [ANY] * (3 * count) + [VMEM],
        out_specs=VMEM,
        out_shape=f32(rows, width),
        scratch_shapes=[
            pltpu.VMEM((rows, PANEL), jnp.float32),
            pltpu.VMEM((2, rows, PANEL), jnp.float32),
            pltpu.SemaphoreType.DMA((3 * count,)),
        ],
        compiler_params=limit_for(BLK, 16),
        name="finish",
    )(table, *row_pieces, *col_own, *col_other, assembled)


def shards(child_front, child_panel, block_map, parent_front, pivot_inverse):
    front_index = lax.axis_index("sib")
    row_index = lax.axis_index("row")
    col_index = lax.axis_index("col")
    count = lax.axis_size("col")
    front = child_front[0]
    panel = child_panel[0]
    sub = panel.shape[0]
    parent_rows, parent_cols = parent_front.shape
    parent_span = parent_cols // BLK
    deal = parent_rows // count

    own_map = lax.dynamic_index_in_dim(block_map, front_index, 0, keepdims=False)
    other_map = lax.dynamic_index_in_dim(block_map, 1 - front_index, 0, keepdims=False)
    table = jnp.concatenate(
        [
            jnp.stack([row_index, col_index, front_index]).astype(jnp.int32),
            window_choice(own_map, row_index, parent_span),
            window_choice(other_map, row_index, parent_span),
            window_choice(own_map, col_index, parent_span),
            window_choice(other_map, col_index, parent_span),
            window_choice(own_map, 0, parent_span)[:PIV],
            window_choice(other_map, 0, parent_span)[:PIV],
        ]
    )

    def over_col(values):
        got = []
        for k, value in zip(range(1, count), values):
            got.append(swapped(value, "col", k))
        return got

    def over_row(value):
        got = [value]
        for d in range(1, count):
            got.append(rotated(value, "row", d))
        return got

    def to_sibling(value):
        return swapped(value, "sib", 1)

    around = around_row(panel)
    rows = [panel] + over_col([panel] * (count - 1))
    slices = [
        lax.dynamic_slice_in_dim(front, (col_index ^ k) * sub, sub, axis=1) for k in range(count)
    ]
    fronts = [slices[0]] + over_col(slices[1:])

    dealt = []
    for j in range(count):
        value = parent_front[j * deal : (j + 1) * deal, :PANEL]
        dealt.append(lax.ppermute(value, "col", [(0, j)]) if j else value)

    *homes, edge, up = slice_products(table, rows, around, fronts)
    edge = shifted(edge, "row")
    up = shifted(up, "row")
    own = [homes[0]] + over_col(homes[1:])

    keep, send = place_rows(table, homes, edge)
    both = jnp.stack([keep, to_sibling(send)])
    slices = [
        lax.dynamic_slice_in_dim(both, (col_index ^ k) * deal, deal, axis=1)
        for k in range(count)
    ]
    small = [slices[0]] + over_col(slices[1:])
    packed = pack_halo(table, homes, edge, up)
    own = own + [packed[0]] + over_col(packed[1:])
    factor = factor_slice(table, small, dealt, pivot_inverse)
    factors = over_row(factor)
    row_pieces = [factor] + over_col([factor] * (count - 1))

    picked = pick_for_cols(table, factors, range(count))
    col_own = [picked[0]] + over_col(picked[1:])
    col_other = [to_sibling(value) for value in col_own]

    other = [to_sibling(value) for value in own]
    assembled = assemble(table, parent_front, own, other)
    return finish(table, assembled, row_pieces, col_own, col_other)


def solution(mesh):
    in_specs = (
        P("sib", "row", "col"),
        P("sib", ("row", "col"), None),
        P(),
        P(("row", "sib"), "col"),
        P(),
    )
    out_specs = P(("row", "sib"), "col")

    return jax.shard_map(shards, mesh=mesh, in_specs=in_specs, out_specs=out_specs, check_vma=False)
```

```python
import jax
import jax.numpy as jnp
from jax import lax
from jax.experimental import pallas as pl
from jax.experimental.pallas import tpu as pltpu
from jax.sharding import PartitionSpec as P


BLK = 128
CBD = 4
PBD = 6
HB = 2
PIV = 4
PANEL = 512
HALF = PBD // 2
EDGE = HB * BLK


SMEM = pl.BlockSpec(memory_space=pltpu.SMEM)
VMEM = pl.BlockSpec(memory_space=pltpu.VMEM)
ANY = pl.BlockSpec(memory_space=pl.ANY)


def limit_for(sub, mebibytes):
    if sub < BLK:
        mebibytes = 56
    return pltpu.CompilerParams(vmem_limit_bytes=mebibytes << 20)


ROW, COL, SIB = 0, 1, 2
OWN_ROWS, OTHER_ROWS, OWN_COLS, OTHER_COLS = 3, 9, 15, 21
OWN_PIVOT, OTHER_PIVOT = 27, 31


def f32(*shape):
    return jax.ShapeDtypeStruct(shape, jnp.float32)


def halves(value):
    high = value.astype(jnp.bfloat16)
    low = (value - high.astype(jnp.float32)).astype(jnp.bfloat16)
    return high, low


def times_transpose(left, right):
    def dot(x, y):
        return lax.dot_general(
            x, y, (((1,), (1,)), ((), ())), preferred_element_type=jnp.float32
        )

    return dot(left[0], right[0]) + (dot(left[0], right[1]) + dot(left[1], right[0]))


def rotated(value, axis, steps):
    count = lax.axis_size(axis)
    return lax.ppermute(value, axis, [(i, (i + steps) % count) for i in range(count)])


def swapped(value, axis, mask):
    count = lax.axis_size(axis)
    return lax.ppermute(value, axis, [(i, i ^ mask) for i in range(count)])


def shifted(value, axis):
    count = lax.axis_size(axis)
    return lax.ppermute(value, axis, [(i, i + 1) for i in range(count - 1)])


def run_copies(copies):
    for copy in copies:
        copy.start()
    for copy in copies:
        copy.wait()


def span(index, size):
    return pl.ds(pl.multiple_of(index * size, size), size)


def gather_copies(table, pieces, target, sems, size, base=0):
    return [
        pltpu.make_async_copy(piece, target.at[span(table[COL] ^ k, size)], sems.at[base + k])
        for k, piece in enumerate(pieces)
    ]


def lookup_table(block_map, parent_span):
    def body(map_ref, out):
        row, col, sib = (lax.axis_index(axis) for axis in ("row", "col", "sib"))
        out[ROW], out[COL], out[SIB] = row, col, sib
        for base, sibling, group, slots in (
            (OWN_ROWS, sib, row, PBD),
            (OTHER_ROWS, 1 - sib, row, PBD),
            (OWN_COLS, sib, col, PBD),
            (OTHER_COLS, 1 - sib, col, PBD),
            (OWN_PIVOT, sib, 0, PIV),
            (OTHER_PIVOT, 1 - sib, 0, PIV),
        ):
            window = []
            for w in range(CBD + HB):
                block = group * CBD + w - HB
                landed = map_ref[sibling, jnp.maximum(block, 0)]
                window.append(jnp.where(block >= 0, landed, -1))
            for slot in range(slots):
                place = jnp.int32(-1)
                for w, landed in enumerate(window):
                    place = jnp.where(landed == group * parent_span + slot, w, place)
                out[base + slot] = place

    return pl.pallas_call(
        body,
        in_specs=[SMEM],
        out_specs=SMEM,
        out_shape=jax.ShapeDtypeStruct((OTHER_PIVOT + PIV,), jnp.int32),
        compiler_params=limit_for(BLK, 4),
        name="lookup_table",
    )(block_map)


def cut_slices(table, front, parent, deal, sub):
    size = front.shape[0]
    count = parent.shape[0] // deal
    aligned = sub % BLK == 0

    def body(sc, front_ref, parent_ref, *refs):
        fronts, deals, sems = refs[: count * aligned], refs[count * aligned : -1], refs[-1]
        copies = [
            pltpu.make_async_copy(
                front_ref.at[:, span(sc[COL] ^ m, sub)], out, sems.at[m]
            )
            for m, out in enumerate(fronts)
        ]
        copies += [
            pltpu.make_async_copy(
                parent_ref.at[pl.ds(j * deal, deal), pl.ds(0, PANEL)], out, sems.at[count + j]
            )
            for j, out in enumerate(deals)
        ]
        run_copies(copies)

    outs = pl.pallas_call(
        body,
        in_specs=[SMEM, ANY, ANY],
        out_specs=[VMEM] * (count * aligned + count),
        out_shape=[f32(size, sub)] * (count * aligned) + [f32(deal, PANEL)] * count,
        scratch_shapes=[pltpu.SemaphoreType.DMA((2 * count,))],
        compiler_params=limit_for(sub, 8),
        name="cut_slices",
    )(table, front, parent)
    fronts, deals = outs[: count * aligned], outs[count * aligned :]
    if not aligned:
        col = lax.axis_index("col")
        fronts = [
            lax.dynamic_slice_in_dim(front, (col ^ k) * sub, sub, axis=1) for k in range(count)
        ]
    return fronts, deals


def start_chosen(chosen, choices, target, sem):
    for d, choice in enumerate(choices):

        @pl.when(chosen == d)
        def _():
            pltpu.make_async_copy(choice, target, sem).start()


def turn_of(sc, mask, count):
    return lax.rem(sc[ROW] - (sc[COL] ^ mask) + count, count)


def slice_place(sc, mask, count):
    half = count // 2
    diff = sc[ROW] - (sc[COL] ^ mask)
    near = (diff < 0) & (-diff < half)
    return jnp.where(near, 2 * half - 1 - diff, jnp.abs(diff))


def around_row(value):
    count = lax.axis_size("row")
    half = count // 2
    middle = rotated(value, "row", half)
    below, above, far = [], [], []
    for d in range(1, half):
        below.append(lax.ppermute(value, "row", [(i, i + d) for i in range(count - d)]))
        above.append(lax.ppermute(value, "row", [(i + d, i) for i in range(count - d)]))
        pairs = [(i, i + d) for i in range(half, count - d)]
        pairs += [(i, i - d) for i in range(d, half)]
        far.append(lax.ppermute(middle, "row", pairs))
    return [value] + below + [middle] + far + above


def slice_products(table, rows, around, fronts):
    count = len(rows)
    many = len(around)
    sub, depth = rows[0].shape
    size = count * sub

    def body(*refs):
        sc = refs[0]
        row_refs = refs[1 : 1 + count]
        around_refs = refs[1 + count : 1 + count + many]
        front_refs = refs[1 + count + many : 1 + 2 * count + many]
        outs = refs[1 + 2 * count + many :][:count]
        edge, up, row_buf, col_buf, sems = refs[1 + 3 * count + many :]
        places = [col_buf.at[m * sub : (m + 1) * sub] for m in range(count)]
        rows_in = gather_copies(sc, row_refs, row_buf, sems, sub)
        for copy in rows_in:
            copy.start()
        for m, place in enumerate(places):
            start_chosen(slice_place(sc, m, count), around_refs, place, sems.at[count + m])
        for copy in rows_in:
            copy.wait()
        left = halves(row_buf[...])
        for m, place in enumerate(places):
            pltpu.make_async_copy(around_refs[0], place, sems.at[count + m]).wait()
        product = times_transpose(left, halves(col_buf[...]))
        for m in range(count):
            group = sc[COL] ^ m
            part = front_refs[m][...] - product[:, m * sub : (m + 1) * sub]
            outs[m][...] = part

            @pl.when(group == 0)
            def _():
                edge[...] = part[-EDGE:]

            @pl.when(group > 0)
            def _():
                up[group - 1] = part[-EDGE:]

    return pl.pallas_call(
        body,
        in_specs=[SMEM] + [ANY] * (count + many) + [VMEM] * count,
        out_specs=[VMEM] * (count + 2),
        out_shape=[f32(size, sub)] * count + [f32(EDGE, sub), f32(count - 1, EDGE, sub)],
        scratch_shapes=[
            pltpu.VMEM((size, depth), jnp.float32),
            pltpu.VMEM((size, depth), jnp.float32),
            pltpu.SemaphoreType.DMA((2 * count,)),
        ],
        compiler_params=limit_for(sub, 20),
        name="slice_products",
    )(table, *rows, *around, *fronts)


def pack_halo(table, homes, edge, up):
    count = len(homes)
    size, sub = homes[0].shape

    def body(*refs):
        sc = refs[0]
        home_refs = refs[1 : 1 + count]
        edge_ref, up_ref = refs[1 + count : 3 + count]
        outs = refs[3 + count : 3 + 2 * count]
        sems = refs[-1]
        near, far = pl.ds(size, EDGE), pl.ds(size + EDGE, EDGE)
        for m, out in enumerate(outs):
            group = sc[COL] ^ m
            before = jnp.maximum(group - 1, 0)
            start_chosen(before ^ sc[COL], home_refs, out.at[pl.ds(0, size)], sems.at[3 * m])
            for i, (wanted, place) in enumerate(((group, near), (before, far))):

                @pl.when(wanted == 0)
                def _():
                    pltpu.make_async_copy(edge_ref, out.at[place], sems.at[3 * m + 1 + i]).start()

                @pl.when(wanted > 0)
                def _():
                    pltpu.make_async_copy(
                        up_ref.at[jnp.maximum(wanted - 1, 0)], out.at[place], sems.at[3 * m + 1 + i]
                    ).start()

        for m, out in enumerate(outs):
            pltpu.make_async_copy(home_refs[0], out.at[pl.ds(0, size)], sems.at[3 * m]).wait()
            for i, place in enumerate((near, far)):
                pltpu.make_async_copy(edge_ref, out.at[place], sems.at[3 * m + 1 + i]).wait()

    return pl.pallas_call(
        body,
        in_specs=[SMEM] + [ANY] * (count + 2),
        out_specs=[VMEM] * count,
        out_shape=[f32(size + 2 * EDGE, sub)] * count,
        scratch_shapes=[pltpu.SemaphoreType.DMA((3 * count,))],
        compiler_params=limit_for(sub, 8),
        name="pack_halo",
    )(table, *homes, edge, up)


def pick_for_cols(table, pieces, masks):
    count = len(pieces)

    def body(*refs):
        sc = refs[0]
        ins = refs[1 : 1 + count]
        outs = refs[1 + count : -1]
        sems = refs[-1]
        for i, mask in enumerate(masks):
            start_chosen(turn_of(sc, mask, count), ins, outs[i], sems.at[i])
        for i in range(len(masks)):
            pltpu.make_async_copy(ins[0], outs[i], sems.at[i]).wait()

    return pl.pallas_call(
        body,
        in_specs=[SMEM] + [ANY] * count,
        out_specs=[VMEM] * len(masks),
        out_shape=[f32(*pieces[0].shape)] * len(masks),
        scratch_shapes=[pltpu.SemaphoreType.DMA((len(masks),))],
        compiler_params=limit_for(BLK, 16),
        name="pick_for_cols",
    )(table, *pieces)


def place_rows(table, homes, edge, deal):
    count = len(homes)
    size, width = homes[0].shape
    rows = HALF * BLK

    def body(*refs):
        sc = refs[0]
        home_refs = refs[1 : 1 + count]
        edge_ref = refs[1 + count]
        outs = refs[2 + count : 2 + 2 * count]
        window, placed, sems = refs[2 + 2 * count :]
        main = window.at[pl.ds(EDGE, size)]
        start_chosen(sc[COL], home_refs, main, sems.at[0])
        copy = pltpu.make_async_copy(edge_ref, window.at[pl.ds(0, EDGE)], sems.at[1])
        copy.start()
        copy.wait()
        pltpu.make_async_copy(home_refs[0], main, sems.at[0]).wait()
        for which, half in ((0, sc[SIB]), (1, 1 - sc[SIB])):
            for slot in range(HALF):
                place = sc[OWN_ROWS + half * HALF + slot]
                block = window[span(jnp.maximum(place, 0), BLK), :]
                lines = slice(slot * BLK, (slot + 1) * BLK)
                placed[which, lines, :] = jnp.where(place >= 0, block, 0.0)
        for m, out in enumerate(outs):
            for which in range(2):
                out[which] = placed[which, span(sc[COL] ^ m, deal), :]

    return pl.pallas_call(
        body,
        in_specs=[SMEM] + [ANY] * (count + 1),
        out_specs=[VMEM] * count,
        out_shape=[f32(2, deal, width)] * count,
        scratch_shapes=[
            pltpu.VMEM((size + EDGE, width), jnp.float32),
            pltpu.VMEM((2, rows, width), jnp.float32),
            pltpu.SemaphoreType.DMA((2,)),
        ],
        compiler_params=limit_for(width, 8),
        name="place_rows",
    )(table, *homes, edge)


def factor_slice(table, small, small_other, dealt, pivot_inverse):
    count = len(small)
    _, rows, sub = small[0].shape

    def body(*refs):
        sc = refs[0]
        pieces = refs[1 : 1 + count]
        other_refs = refs[1 + count : 1 + 2 * count]
        deal_refs = refs[1 + 2 * count : 1 + 3 * count]
        inverse_ref, out, order, child, sums, sems = refs[1 + 3 * count :]
        start_chosen(sc[COL], deal_refs, sums, sems.at[2 * count])
        copies = []
        for k in range(count):
            place = order.at[sc[COL] ^ k]
            copies += [
                pltpu.make_async_copy(pieces[k].at[0], place.at[0], sems.at[2 * k]),
                pltpu.make_async_copy(other_refs[k].at[1], place.at[1], sems.at[2 * k + 1]),
            ]
        run_copies(copies)
        for j in range(count):
            block, lane = divmod(j * sub, BLK)
            for sibling in range(2):
                child[sibling, block, :, lane : lane + sub] = order[j, sibling]
        pltpu.make_async_copy(deal_refs[0], sums, sems.at[2 * count]).wait()
        for p in range(PIV):
            lanes = slice(p * BLK, (p + 1) * BLK)
            added = sums[:, lanes]
            for sibling, base in ((0, OWN_PIVOT), (1, OTHER_PIVOT)):
                place = sc[base + p]
                block = child[sibling, jnp.maximum(place - HB, 0)]
                added += jnp.where(place >= HB, block, 0.0)
            sums[:, lanes] = added
        out[...] = times_transpose(halves(sums[...]), halves(inverse_ref[...]))

    return pl.pallas_call(
        body,
        in_specs=[SMEM] + [ANY] * (3 * count) + [VMEM],
        out_specs=VMEM,
        out_shape=f32(rows, PANEL),
        scratch_shapes=[
            pltpu.VMEM((count, 2, rows, sub), jnp.float32),
            pltpu.VMEM((2, PIV, rows, BLK), jnp.float32),
            pltpu.VMEM((rows, PANEL), jnp.float32),
            pltpu.SemaphoreType.DMA((2 * count + 1,)),
        ],
        compiler_params=limit_for(sub, 16),
        name="factor_slice",
    )(table, *small, *small_other, *dealt, pivot_inverse)


def assemble(table, parent, own, other):
    count = len(own) // 2
    rows, width = parent.shape
    size, sub = own[0].shape
    half = count // 2
    split = BLK // sub

    def body(*refs):
        sc, parent_ref = refs[:2]
        own_refs, other_refs = refs[2 : 2 + 2 * count], refs[2 + 2 * count : 2 + 4 * count]
        out, own_win, other_win, sems = refs[2 + 4 * count :]
        at = 0
        always, edges = [], []
        for refs_in, window in ((own_refs, own_win), (other_refs, other_win)):
            for m in range(count):
                home, halo = refs_in[m], refs_in[count + m]
                piece = sc[COL] ^ m
                main = half + piece
                side = jnp.maximum(piece - half, 0)
                low, high = pl.ds(0, EDGE), pl.ds(EDGE, size)
                always += [
                    pltpu.make_async_copy(home, window.at[main, high], sems.at[at]),
                    pltpu.make_async_copy(
                        halo.at[pl.ds(size, EDGE)], window.at[main, low], sems.at[at + 1]
                    ),
                ]
                edges += [
                    (
                        piece,
                        pltpu.make_async_copy(
                            halo.at[pl.ds(0, size)], window.at[side, high], sems.at[at + 2]
                        ),
                        pltpu.make_async_copy(
                            halo.at[pl.ds(size + EDGE, EDGE)],
                            window.at[side, low],
                            sems.at[at + 3],
                        ),
                    )
                ]
                at += 4
        for copy in always:
            copy.start()
        for piece, first, second in edges:

            @pl.when(piece >= half)
            def _():
                first.start()
                second.start()

        for copy in always:
            copy.wait()
        for piece, first, second in edges:

            @pl.when(piece >= half)
            def _():
                first.wait()
                second.wait()

        for q in range(PBD):
            cols = slice(q * BLK, (q + 1) * BLK)
            for p in range(HALF):
                lines = slice(p * BLK, (p + 1) * BLK)
                total = parent_ref[lines, cols]
                for window, row_base, col_base in (
                    (own_win, OWN_ROWS, OWN_COLS),
                    (other_win, OTHER_ROWS, OTHER_COLS),
                ):
                    down = sc[row_base + sc[SIB] * HALF + p]
                    across = sc[col_base + q]
                    start = jnp.maximum(across, 0) * split
                    pieces = [
                        window[start + i, span(jnp.maximum(down, 0), BLK), :] for i in range(split)
                    ]
                    block = pieces[0] if split == 1 else jnp.concatenate(pieces, axis=1)
                    total += jnp.where((down >= 0) & (across >= 0), block, 0.0)
                out[lines, cols] = total

    return pl.pallas_call(
        body,
        in_specs=[SMEM, VMEM] + [ANY] * (4 * count),
        out_specs=VMEM,
        out_shape=f32(rows, width),
        scratch_shapes=[
            pltpu.VMEM((half + count, size + EDGE, sub), jnp.float32),
            pltpu.VMEM((half + count, size + EDGE, sub), jnp.float32),
            pltpu.SemaphoreType.DMA((8 * count,)),
        ],
        compiler_params=limit_for(sub, 12),
        name="assemble",
    )(table, parent, *own, *other)


def finish(table, assembled, row_pieces, col_own, col_other):
    count = len(row_pieces)
    rows, width = assembled.shape
    piece_rows = row_pieces[0].shape[0]

    def body(*refs):
        sc = refs[0]
        row_refs = refs[1 : 1 + count]
        col_own_refs = refs[1 + count : 1 + 2 * count]
        col_other_refs = refs[1 + 2 * count : 1 + 3 * count]
        base_ref, out, row_factor, col_factor, sems = refs[1 + 3 * count :]
        copies = [
            gather_copies(sc, row_refs, row_factor, sems, piece_rows),
            gather_copies(sc, col_own_refs, col_factor.at[sc[SIB]], sems, piece_rows, count),
            gather_copies(
                sc, col_other_refs, col_factor.at[1 - sc[SIB]], sems, piece_rows, 2 * count
            ),
        ]
        for copy in sum(copies, []):
            copy.start()
        for copy in copies[0]:
            copy.wait()
        left = halves(row_factor[...])
        for copy in copies[1] + copies[2]:
            copy.wait()
        first_row = (sc[ROW] * 2 + sc[SIB]) * HALF
        first_col = sc[COL] * PBD
        for side in range(2):
            product = times_transpose(left, halves(col_factor[side]))
            for i in range(HALF):
                q = side * HALF + i
                cols = slice(q * BLK, (q + 1) * BLK)
                for p in range(HALF):
                    lines = slice(p * BLK, (p + 1) * BLK)
                    total = base_ref[lines, cols]
                    inside = (first_col + q >= PIV) & (first_row + p >= PIV)
                    reduced = total - product[lines, i * BLK : (i + 1) * BLK]
                    total = jnp.where(inside, reduced, total)
                    if q < PIV:
                        total = jnp.where(sc[COL] == 0, row_factor[lines, cols], total)
                    out[lines, cols] = total

    return pl.pallas_call(
        body,
        in_specs=[SMEM] + [ANY] * (3 * count) + [VMEM],
        out_specs=VMEM,
        out_shape=f32(rows, width),
        scratch_shapes=[
            pltpu.VMEM((rows, PANEL), jnp.float32),
            pltpu.VMEM((2, rows, PANEL), jnp.float32),
            pltpu.SemaphoreType.DMA((3 * count,)),
        ],
        compiler_params=limit_for(BLK, 16),
        name="finish",
    )(table, *row_pieces, *col_own, *col_other, assembled)


def shards(child_front, child_panel, block_map, parent_front, pivot_inverse):
    count = lax.axis_size("col")
    front = child_front[0]
    panel = child_panel[0]
    sub = panel.shape[0]
    parent_rows, parent_cols = parent_front.shape
    parent_span = parent_cols // BLK
    deal = parent_rows // count

    table = lookup_table(block_map, parent_span)

    def over_col(values):
        got = []
        for k, value in zip(range(1, count), values):
            got.append(swapped(value, "col", k))
        return got

    def over_row(value):
        got = [value]
        for d in range(1, count):
            got.append(rotated(value, "row", d))
        return got

    def to_sibling(value):
        return swapped(value, "sib", 1)

    around = around_row(panel)
    rows = [panel] + over_col([panel] * (count - 1))
    slices, deals = cut_slices(table, front, parent_front, deal, sub)
    fronts = [slices[0]] + over_col(slices[1:])

    dealt = []
    for j in range(count):
        value = deals[j]
        dealt.append(lax.ppermute(value, "col", [(0, j)]) if j else value)

    *homes, edge, up = slice_products(table, rows, around, fronts)
    edge = shifted(edge, "row")
    up = shifted(up, "row")
    own = [homes[0]] + over_col(homes[1:])

    small = place_rows(table, homes, edge, deal)
    small = [small[0]] + over_col(small[1:])
    small_other = [to_sibling(value) for value in small]
    packed = pack_halo(table, homes, edge, up)
    own = own + [packed[0]] + over_col(packed[1:])
    factor = factor_slice(table, small, small_other, dealt, pivot_inverse)
    factors = over_row(factor)
    row_pieces = [factor] + over_col([factor] * (count - 1))

    picked = pick_for_cols(table, factors, range(count))
    col_own = [picked[0]] + over_col(picked[1:])
    col_other = [to_sibling(value) for value in col_own]

    other = [to_sibling(value) for value in own]
    assembled = assemble(table, parent_front, own, other)
    return finish(table, assembled, row_pieces, col_own, col_other)


def solution(mesh):
    in_specs = (
        P("sib", "row", "col"),
        P("sib", ("row", "col"), None),
        P(),
        P(("row", "sib"), "col"),
        P(),
    )
    out_specs = P(("row", "sib"), "col")

    return jax.shard_map(shards, mesh=mesh, in_specs=in_specs, out_specs=out_specs, check_vma=False)
```

```python
import jax
import jax.numpy as jnp
from jax import lax
from jax.experimental import pallas as pl
from jax.experimental.pallas import tpu as pltpu
from jax.sharding import PartitionSpec as P


BLK = 128
CBD = 4
PBD = 6
HB = 2
PIV = 4
PANEL = 512
HALF = PBD // 2
EDGE = HB * BLK


SMEM = pl.BlockSpec(memory_space=pltpu.SMEM)
VMEM = pl.BlockSpec(memory_space=pltpu.VMEM)
ANY = pl.BlockSpec(memory_space=pl.ANY)


def limit_for(sub, mebibytes):
    if sub < BLK:
        mebibytes = 56
    return pltpu.CompilerParams(vmem_limit_bytes=mebibytes << 20)


ROW, COL, SIB = 0, 1, 2
OWN_ROWS, OTHER_ROWS, OWN_COLS, OTHER_COLS = 3, 9, 15, 21
OWN_PIVOT, OTHER_PIVOT = 27, 31


def f32(*shape):
    return jax.ShapeDtypeStruct(shape, jnp.float32)


def halves(value):
    high = value.astype(jnp.bfloat16)
    low = (value - high.astype(jnp.float32)).astype(jnp.bfloat16)
    return high, low


def times_transpose(left, right):
    def dot(x, y):
        return lax.dot_general(
            x, y, (((1,), (1,)), ((), ())), preferred_element_type=jnp.float32
        )

    return dot(left[0], right[0]) + (dot(left[0], right[1]) + dot(left[1], right[0]))


def rotated(value, axis, steps):
    count = lax.axis_size(axis)
    return lax.ppermute(value, axis, [(i, (i + steps) % count) for i in range(count)])


def swapped(value, axis, mask):
    count = lax.axis_size(axis)
    return lax.ppermute(value, axis, [(i, i ^ mask) for i in range(count)])


def shifted(value, axis):
    count = lax.axis_size(axis)
    return lax.ppermute(value, axis, [(i, i + 1) for i in range(count - 1)])


def run_copies(copies):
    for copy in copies:
        copy.start()
    for copy in copies:
        copy.wait()


def span(index, size):
    return pl.ds(pl.multiple_of(index * size, size), size)


def gather_copies(table, pieces, target, sems, size, base=0):
    return [
        pltpu.make_async_copy(piece, target.at[span(table[COL] ^ k, size)], sems.at[base + k])
        for k, piece in enumerate(pieces)
    ]


def lookup_table(block_map, parent_span):
    def body(map_ref, out):
        row, col, sib = (lax.axis_index(axis) for axis in ("row", "col", "sib"))
        out[ROW], out[COL], out[SIB] = row, col, sib
        for base, sibling, group, slots in (
            (OWN_ROWS, sib, row, PBD),
            (OTHER_ROWS, 1 - sib, row, PBD),
            (OWN_COLS, sib, col, PBD),
            (OTHER_COLS, 1 - sib, col, PBD),
            (OWN_PIVOT, sib, 0, PIV),
            (OTHER_PIVOT, 1 - sib, 0, PIV),
        ):
            window = []
            for w in range(CBD + HB):
                block = group * CBD + w - HB
                landed = map_ref[sibling, jnp.maximum(block, 0)]
                window.append(jnp.where(block >= 0, landed, -1))
            for slot in range(slots):
                place = jnp.int32(-1)
                for w, landed in enumerate(window):
                    place = jnp.where(landed == group * parent_span + slot, w, place)
                out[base + slot] = place

    return pl.pallas_call(
        body,
        in_specs=[SMEM],
        out_specs=SMEM,
        out_shape=jax.ShapeDtypeStruct((OTHER_PIVOT + PIV,), jnp.int32),
        compiler_params=limit_for(BLK, 4),
        name="lookup_table",
    )(block_map)


def cut_slices(table, front, parent, deal, sub):
    size = front.shape[0]
    count = parent.shape[0] // deal
    aligned = sub % BLK == 0

    def body(sc, front_ref, parent_ref, *refs):
        fronts, deals, sems = refs[: count * aligned], refs[count * aligned : -1], refs[-1]
        copies = [
            pltpu.make_async_copy(
                front_ref.at[:, span(sc[COL] ^ m, sub)], out, sems.at[m]
            )
            for m, out in enumerate(fronts)
        ]
        copies += [
            pltpu.make_async_copy(
                parent_ref.at[pl.ds(j * deal, deal), pl.ds(0, PANEL)], out, sems.at[count + j]
            )
            for j, out in enumerate(deals)
        ]
        run_copies(copies)

    outs = pl.pallas_call(
        body,
        in_specs=[SMEM, ANY, ANY],
        out_specs=[VMEM] * (count * aligned + count),
        out_shape=[f32(size, sub)] * (count * aligned) + [f32(deal, PANEL)] * count,
        scratch_shapes=[pltpu.SemaphoreType.DMA((2 * count,))],
        compiler_params=limit_for(sub, 8),
        name="cut_slices",
    )(table, front, parent)
    fronts, deals = outs[: count * aligned], outs[count * aligned :]
    if not aligned:
        col = lax.axis_index("col")
        fronts = [
            lax.dynamic_slice_in_dim(front, (col ^ k) * sub, sub, axis=1) for k in range(count)
        ]
    return fronts, deals


def start_chosen(chosen, choices, target, sem):
    for d, choice in enumerate(choices):

        @pl.when(chosen == d)
        def _():
            pltpu.make_async_copy(choice, target, sem).start()


def turn_of(sc, mask, count):
    return lax.rem(sc[ROW] - (sc[COL] ^ mask) + count, count)


def slice_place(sc, mask, count):
    half = count // 2
    diff = sc[ROW] - (sc[COL] ^ mask)
    near = (diff < 0) & (-diff < half)
    return jnp.where(near, 2 * half - 1 - diff, jnp.abs(diff))


def around_row(value):
    count = lax.axis_size("row")
    half = count // 2
    middle = rotated(value, "row", half)
    below, above, far = [], [], []
    for d in range(1, half):
        below.append(lax.ppermute(value, "row", [(i, i + d) for i in range(count - d)]))
        above.append(lax.ppermute(value, "row", [(i + d, i) for i in range(count - d)]))
        pairs = [(i, i + d) for i in range(half, count - d)]
        pairs += [(i, i - d) for i in range(d, half)]
        far.append(lax.ppermute(middle, "row", pairs))
    return [value] + below + [middle] + far + above


def slice_products(table, rows, around, fronts):
    count = len(rows)
    many = len(around)
    sub, depth = rows[0].shape
    size = count * sub

    def body(*refs):
        sc = refs[0]
        row_refs = refs[1 : 1 + count]
        around_refs = refs[1 + count : 1 + count + many]
        front_refs = refs[1 + count + many : 1 + 2 * count + many]
        outs = refs[1 + 2 * count + many :][:count]
        edge, up, row_buf, col_buf, sems = refs[1 + 3 * count + many :]
        places = [col_buf.at[m * sub : (m + 1) * sub] for m in range(count)]
        rows_in = gather_copies(sc, row_refs, row_buf, sems, sub)
        for copy in rows_in:
            copy.start()
        for m, place in enumerate(places):
            start_chosen(slice_place(sc, m, count), around_refs, place, sems.at[count + m])
        for copy in rows_in:
            copy.wait()
        left = halves(row_buf[...])
        for m, place in enumerate(places):
            pltpu.make_async_copy(around_refs[0], place, sems.at[count + m]).wait()
        product = times_transpose(left, halves(col_buf[...]))
        for m in range(count):
            group = sc[COL] ^ m
            part = front_refs[m][...] - product[:, m * sub : (m + 1) * sub]
            outs[m][...] = part

            @pl.when(group == 0)
            def _():
                edge[...] = part[-EDGE:]

            @pl.when(group > 0)
            def _():
                up[group - 1] = part[-EDGE:]

    return pl.pallas_call(
        body,
        in_specs=[SMEM] + [ANY] * (count + many) + [VMEM] * count,
        out_specs=[VMEM] * (count + 2),
        out_shape=[f32(size, sub)] * count + [f32(EDGE, sub), f32(count - 1, EDGE, sub)],
        scratch_shapes=[
            pltpu.VMEM((size, depth), jnp.float32),
            pltpu.VMEM((size, depth), jnp.float32),
            pltpu.SemaphoreType.DMA((2 * count,)),
        ],
        compiler_params=limit_for(sub, 20),
        name="slice_products",
    )(table, *rows, *around, *fronts)


def pack_halo(table, homes, edge, up):
    count = len(homes)
    size, sub = homes[0].shape

    def body(*refs):
        sc = refs[0]
        home_refs = refs[1 : 1 + count]
        edge_ref, up_ref = refs[1 + count : 3 + count]
        above_outs = refs[3 + count : 3 + 2 * count]
        side_outs = refs[3 + 2 * count : 3 + 3 * count]
        sems = refs[-1]
        for m in range(count):
            group = sc[COL] ^ m
            before = jnp.maximum(group - 1, 0)
            main, tail = side_outs[m].at[pl.ds(0, size)], side_outs[m].at[pl.ds(size, EDGE)]
            start_chosen(before ^ sc[COL], home_refs, main, sems.at[3 * m])
            for i, (wanted, place) in enumerate(((group, above_outs[m]), (before, tail))):

                @pl.when(wanted == 0)
                def _():
                    pltpu.make_async_copy(edge_ref, place, sems.at[3 * m + 1 + i]).start()

                @pl.when(wanted > 0)
                def _():
                    pltpu.make_async_copy(
                        up_ref.at[jnp.maximum(wanted - 1, 0)], place, sems.at[3 * m + 1 + i]
                    ).start()

        for m in range(count):
            main, tail = side_outs[m].at[pl.ds(0, size)], side_outs[m].at[pl.ds(size, EDGE)]
            pltpu.make_async_copy(home_refs[0], main, sems.at[3 * m]).wait()
            pltpu.make_async_copy(edge_ref, above_outs[m], sems.at[3 * m + 1]).wait()
            pltpu.make_async_copy(edge_ref, tail, sems.at[3 * m + 2]).wait()

    outs = pl.pallas_call(
        body,
        in_specs=[SMEM] + [ANY] * (count + 2),
        out_specs=[VMEM] * (2 * count),
        out_shape=[f32(EDGE, sub)] * count + [f32(size + EDGE, sub)] * count,
        scratch_shapes=[pltpu.SemaphoreType.DMA((3 * count,))],
        compiler_params=limit_for(sub, 8),
        name="pack_halo",
    )(table, *homes, edge, up)
    return outs[:count], outs[count:]


def to_next_group(packed):
    count = len(packed)
    half = count // 2

    def send(mask):
        pairs = [(i, i ^ mask) for i in range(half, count)]
        if mask > half:
            pairs = [(i, j) for i, j in pairs if j > 0 and (i, j) != (half, 1)]
        if not pairs:
            return None
        return lax.ppermute(packed[mask], "col", pairs)

    got = [packed[0]] + [send(mask) for mask in range(1, count)]
    forwarded = lax.ppermute(got[half], "col", [(0, 1)])
    direct = got[half + 1]
    if direct is not None:
        forwarded = jnp.where(lax.axis_index("col") == 1, forwarded, direct)
    got[half + 1] = forwarded
    return got


def pick_for_cols(table, pieces, masks):
    count = len(pieces)

    def body(*refs):
        sc = refs[0]
        ins = refs[1 : 1 + count]
        outs = refs[1 + count : -1]
        sems = refs[-1]
        for i, mask in enumerate(masks):
            start_chosen(turn_of(sc, mask, count), ins, outs[i], sems.at[i])
        for i in range(len(masks)):
            pltpu.make_async_copy(ins[0], outs[i], sems.at[i]).wait()

    return pl.pallas_call(
        body,
        in_specs=[SMEM] + [ANY] * count,
        out_specs=[VMEM] * len(masks),
        out_shape=[f32(*pieces[0].shape)] * len(masks),
        scratch_shapes=[pltpu.SemaphoreType.DMA((len(masks),))],
        compiler_params=limit_for(BLK, 16),
        name="pick_for_cols",
    )(table, *pieces)


def place_rows(table, homes, edge, deal):
    count = len(homes)
    size, width = homes[0].shape
    rows = HALF * BLK

    def body(*refs):
        sc = refs[0]
        home_refs = refs[1 : 1 + count]
        edge_ref = refs[1 + count]
        outs = refs[2 + count : 2 + 2 * count]
        window, placed, sems = refs[2 + 2 * count :]
        main = window.at[pl.ds(EDGE, size)]
        start_chosen(sc[COL], home_refs, main, sems.at[0])
        copy = pltpu.make_async_copy(edge_ref, window.at[pl.ds(0, EDGE)], sems.at[1])
        copy.start()
        copy.wait()
        pltpu.make_async_copy(home_refs[0], main, sems.at[0]).wait()
        for which, half in ((0, sc[SIB]), (1, 1 - sc[SIB])):
            for slot in range(HALF):
                place = sc[OWN_ROWS + half * HALF + slot]
                block = window[span(jnp.maximum(place, 0), BLK), :]
                lines = slice(slot * BLK, (slot + 1) * BLK)
                placed[which, lines, :] = jnp.where(place >= 0, block, 0.0)
        for m, out in enumerate(outs):
            for which in range(2):
                out[which] = placed[which, span(sc[COL] ^ m, deal), :]

    return pl.pallas_call(
        body,
        in_specs=[SMEM] + [ANY] * (count + 1),
        out_specs=[VMEM] * count,
        out_shape=[f32(2, deal, width)] * count,
        scratch_shapes=[
            pltpu.VMEM((size + EDGE, width), jnp.float32),
            pltpu.VMEM((2, rows, width), jnp.float32),
            pltpu.SemaphoreType.DMA((2,)),
        ],
        compiler_params=limit_for(width, 8),
        name="place_rows",
    )(table, *homes, edge)


def factor_slice(table, small, small_other, dealt, pivot_inverse):
    count = len(small)
    _, rows, sub = small[0].shape

    def body(*refs):
        sc = refs[0]
        pieces = refs[1 : 1 + count]
        other_refs = refs[1 + count : 1 + 2 * count]
        deal_refs = refs[1 + 2 * count : 1 + 3 * count]
        inverse_ref, out, order, child, sums, sems = refs[1 + 3 * count :]
        start_chosen(sc[COL], deal_refs, sums, sems.at[2 * count])
        copies = []
        for k in range(count):
            place = order.at[sc[COL] ^ k]
            copies += [
                pltpu.make_async_copy(pieces[k].at[0], place.at[0], sems.at[2 * k]),
                pltpu.make_async_copy(other_refs[k].at[1], place.at[1], sems.at[2 * k + 1]),
            ]
        run_copies(copies)
        for j in range(count):
            block, lane = divmod(j * sub, BLK)
            for sibling in range(2):
                child[sibling, block, :, lane : lane + sub] = order[j, sibling]
        pltpu.make_async_copy(deal_refs[0], sums, sems.at[2 * count]).wait()
        for p in range(PIV):
            lanes = slice(p * BLK, (p + 1) * BLK)
            added = sums[:, lanes]
            for sibling, base in ((0, OWN_PIVOT), (1, OTHER_PIVOT)):
                place = sc[base + p]
                block = child[sibling, jnp.maximum(place - HB, 0)]
                added += jnp.where(place >= HB, block, 0.0)
            sums[:, lanes] = added
        out[...] = times_transpose(halves(sums[...]), halves(inverse_ref[...]))

    return pl.pallas_call(
        body,
        in_specs=[SMEM] + [ANY] * (3 * count) + [VMEM],
        out_specs=VMEM,
        out_shape=f32(rows, PANEL),
        scratch_shapes=[
            pltpu.VMEM((count, 2, rows, sub), jnp.float32),
            pltpu.VMEM((2, PIV, rows, BLK), jnp.float32),
            pltpu.VMEM((rows, PANEL), jnp.float32),
            pltpu.SemaphoreType.DMA((2 * count + 1,)),
        ],
        compiler_params=limit_for(sub, 16),
        name="factor_slice",
    )(table, *small, *small_other, *dealt, pivot_inverse)


def assemble(table, parent, own, other, row_pieces):
    count = len(row_pieces)
    rows, width = parent.shape
    piece_rows = row_pieces[0].shape[0]
    size, sub = own[0].shape
    half = count // 2
    split = BLK // sub

    def body(*refs):
        sc, parent_ref = refs[:2]
        own_refs, other_refs = refs[2 : 2 + 3 * count], refs[2 + 3 * count : 2 + 6 * count]
        row_refs = refs[2 + 6 * count : 2 + 7 * count]
        out, high_out, low_out, own_win, other_win, row_factor, sems = refs[2 + 7 * count :]
        low, high = pl.ds(0, EDGE), pl.ds(EDGE, size)
        always = gather_copies(sc, row_refs, row_factor, sems, piece_rows)
        at = count
        edges = []
        for refs_in, window in ((own_refs, own_win), (other_refs, other_win)):
            for m in range(count):
                home, above, packed = (refs_in[i * count + m] for i in range(3))
                piece = sc[COL] ^ m
                main = half + piece
                side = jnp.maximum(piece - half, 0)
                always += [
                    pltpu.make_async_copy(home, window.at[main, high], sems.at[at]),
                    pltpu.make_async_copy(above, window.at[main, low], sems.at[at + 1]),
                ]
                edges += [
                    (
                        piece,
                        pltpu.make_async_copy(
                            packed.at[pl.ds(0, size)], window.at[side, high], sems.at[at + 2]
                        ),
                        pltpu.make_async_copy(
                            packed.at[pl.ds(size, EDGE)], window.at[side, low], sems.at[at + 3]
                        ),
                    )
                ]
                at += 4
        for copy in always:
            copy.start()
        for piece, first, second in edges:

            @pl.when(piece >= half)
            def _():
                first.start()
                second.start()

        for copy in always[:count]:
            copy.wait()
        high_out[...], low_out[...] = halves(row_factor[...])
        for copy in always[count:]:
            copy.wait()
        for piece, first, second in edges:

            @pl.when(piece >= half)
            def _():
                first.wait()
                second.wait()

        for q in range(PBD):
            cols = slice(q * BLK, (q + 1) * BLK)
            for p in range(HALF):
                lines = slice(p * BLK, (p + 1) * BLK)
                total = parent_ref[lines, cols]
                for window, row_base, col_base in (
                    (own_win, OWN_ROWS, OWN_COLS),
                    (other_win, OTHER_ROWS, OTHER_COLS),
                ):
                    down = sc[row_base + sc[SIB] * HALF + p]
                    across = sc[col_base + q]
                    start = jnp.maximum(across, 0) * split
                    pieces = [
                        window[start + i, span(jnp.maximum(down, 0), BLK), :] for i in range(split)
                    ]
                    block = pieces[0] if split == 1 else jnp.concatenate(pieces, axis=1)
                    total += jnp.where((down >= 0) & (across >= 0), block, 0.0)
                if q < PIV:
                    total = jnp.where(sc[COL] == 0, row_factor[lines, cols], total)
                out[lines, cols] = total

    part = jax.ShapeDtypeStruct((rows, PANEL), jnp.bfloat16)
    return pl.pallas_call(
        body,
        in_specs=[SMEM, VMEM] + [ANY] * (7 * count),
        out_specs=[VMEM] * 3,
        out_shape=[f32(rows, width), part, part],
        scratch_shapes=[
            pltpu.VMEM((half + count, size + EDGE, sub), jnp.float32),
            pltpu.VMEM((half + count, size + EDGE, sub), jnp.float32),
            pltpu.VMEM((rows, PANEL), jnp.float32),
            pltpu.SemaphoreType.DMA((9 * count,)),
        ],
        compiler_params=limit_for(sub, 14),
        name="assemble",
    )(table, parent, *own, *other, *row_pieces)


def finish(table, assembled, row_high, row_low, col_own, col_other):
    count = len(col_own)
    rows, width = assembled.shape
    piece_rows = col_own[0].shape[0]

    def body(*refs):
        sc = refs[0]
        own_refs = refs[1 : 1 + count]
        other_refs = refs[1 + count : 1 + 2 * count]
        base_ref, high_ref, low_ref, out, col_factor, sems = refs[1 + 2 * count :]
        own = gather_copies(sc, own_refs, col_factor.at[sc[SIB]], sems, piece_rows)
        other = gather_copies(
            sc, other_refs, col_factor.at[1 - sc[SIB]], sems, piece_rows, count
        )
        run_copies(own + other)
        left = high_ref[...], low_ref[...]
        first_row = (sc[ROW] * 2 + sc[SIB]) * HALF
        first_col = sc[COL] * PBD
        for side in range(2):
            product = times_transpose(left, halves(col_factor[side]))
            for i in range(HALF):
                q = side * HALF + i
                cols = slice(q * BLK, (q + 1) * BLK)
                for p in range(HALF):
                    lines = slice(p * BLK, (p + 1) * BLK)
                    total = base_ref[lines, cols]
                    inside = (first_col + q >= PIV) & (first_row + p >= PIV)
                    reduced = total - product[lines, i * BLK : (i + 1) * BLK]
                    out[lines, cols] = jnp.where(inside, reduced, total)

    return pl.pallas_call(
        body,
        in_specs=[SMEM] + [ANY] * (2 * count) + [VMEM] * 3,
        out_specs=VMEM,
        out_shape=f32(rows, width),
        scratch_shapes=[
            pltpu.VMEM((2, rows, PANEL), jnp.float32),
            pltpu.SemaphoreType.DMA((2 * count,)),
        ],
        compiler_params=limit_for(BLK, 16),
        name="finish",
    )(table, *col_own, *col_other, assembled, row_high, row_low)


def shards(child_front, child_panel, block_map, parent_front, pivot_inverse):
    count = lax.axis_size("col")
    front = child_front[0]
    panel = child_panel[0]
    sub = panel.shape[0]
    parent_rows, parent_cols = parent_front.shape
    parent_span = parent_cols // BLK
    deal = parent_rows // count

    table = lookup_table(block_map, parent_span)

    def over_col(values):
        got = []
        for k, value in zip(range(1, count), values):
            got.append(swapped(value, "col", k))
        return got

    def over_row(value):
        got = [value]
        for d in range(1, count):
            got.append(rotated(value, "row", d))
        return got

    def to_sibling(value):
        return swapped(value, "sib", 1)

    around = around_row(panel)
    rows = [panel] + over_col([panel] * (count - 1))
    slices, deals = cut_slices(table, front, parent_front, deal, sub)
    fronts = [slices[0]] + over_col(slices[1:])

    dealt = []
    for j in range(count):
        value = deals[j]
        dealt.append(lax.ppermute(value, "col", [(0, j)]) if j else value)

    *homes, edge, up = slice_products(table, rows, around, fronts)
    edge = shifted(edge, "row")
    up = shifted(up, "row")
    own = [homes[0]] + over_col(homes[1:])

    small = place_rows(table, homes, edge, deal)
    small = [small[0]] + over_col(small[1:])
    small_other = [to_sibling(value) for value in small]
    above, packed = pack_halo(table, homes, edge, up)
    own = own + [above[0]] + over_col(above[1:]) + to_next_group(packed)
    factor = factor_slice(table, small, small_other, dealt, pivot_inverse)
    factors = over_row(factor)
    row_pieces = [factor] + over_col([factor] * (count - 1))

    picked = pick_for_cols(table, factors, range(count))
    col_own = [picked[0]] + over_col(picked[1:])
    col_other = [to_sibling(value) for value in col_own]

    other = [to_sibling(value) for value in own]
    assembled, high, low = assemble(table, parent_front, own, other, row_pieces)
    return finish(table, assembled, high, low, col_own, col_other)


def solution(mesh):
    in_specs = (
        P("sib", "row", "col"),
        P("sib", ("row", "col"), None),
        P(),
        P(("row", "sib"), "col"),
        P(),
    )
    out_specs = P(("row", "sib"), "col")

    return jax.shard_map(shards, mesh=mesh, in_specs=in_specs, out_specs=out_specs, check_vma=False)
```

```python
import jax
import jax.numpy as jnp
from jax import lax
from jax.experimental import pallas as pl
from jax.experimental.pallas import tpu as pltpu
from jax.sharding import PartitionSpec as P


BLK = 128
CBD = 4
PBD = 6
HB = 2
PIV = 4
PANEL = 512
HALF = PBD // 2
EDGE = HB * BLK


SMEM = pl.BlockSpec(memory_space=pltpu.SMEM)
VMEM = pl.BlockSpec(memory_space=pltpu.VMEM)
ANY = pl.BlockSpec(memory_space=pl.ANY)


def limit_for(sub, mebibytes):
    if sub < BLK:
        mebibytes = 56
    return pltpu.CompilerParams(vmem_limit_bytes=mebibytes << 20)


ROW, COL, SIB = 0, 1, 2
OWN_ROWS, OTHER_ROWS, OWN_COLS, OTHER_COLS = 3, 9, 15, 21
OWN_PIVOT, OTHER_PIVOT = 27, 31


def f32(*shape):
    return jax.ShapeDtypeStruct(shape, jnp.float32)


def halves(value):
    high = value.astype(jnp.bfloat16)
    low = (value - high.astype(jnp.float32)).astype(jnp.bfloat16)
    return high, low


def times_transpose(left, right):
    def dot(x, y):
        return lax.dot_general(
            x, y, (((1,), (1,)), ((), ())), preferred_element_type=jnp.float32
        )

    return dot(left[0], right[0]) + (dot(left[0], right[1]) + dot(left[1], right[0]))


def rotated(value, axis, steps):
    count = lax.axis_size(axis)
    return lax.ppermute(value, axis, [(i, (i + steps) % count) for i in range(count)])


def swapped(value, axis, mask):
    count = lax.axis_size(axis)
    return lax.ppermute(value, axis, [(i, i ^ mask) for i in range(count)])


def shifted(value, axis):
    count = lax.axis_size(axis)
    return lax.ppermute(value, axis, [(i, i + 1) for i in range(count - 1)])


def run_copies(copies):
    for copy in copies:
        copy.start()
    for copy in copies:
        copy.wait()


def span(index, size):
    return pl.ds(pl.multiple_of(index * size, size), size)


def gather_copies(table, pieces, target, sems, size, base=0):
    return [
        pltpu.make_async_copy(piece, target.at[span(table[COL] ^ k, size)], sems.at[base + k])
        for k, piece in enumerate(pieces)
    ]


def lookup_table(block_map, parent_span):
    def body(map_ref, out):
        row, col, sib = (lax.axis_index(axis) for axis in ("row", "col", "sib"))
        out[ROW], out[COL], out[SIB] = row, col, sib
        for base, sibling, group, slots in (
            (OWN_ROWS, sib, row, PBD),
            (OTHER_ROWS, 1 - sib, row, PBD),
            (OWN_COLS, sib, col, PBD),
            (OTHER_COLS, 1 - sib, col, PBD),
            (OWN_PIVOT, sib, 0, PIV),
            (OTHER_PIVOT, 1 - sib, 0, PIV),
        ):
            window = []
            for w in range(CBD + HB):
                block = group * CBD + w - HB
                landed = map_ref[sibling, jnp.maximum(block, 0)]
                window.append(jnp.where(block >= 0, landed, -1))
            for slot in range(slots):
                place = jnp.int32(-1)
                for w, landed in enumerate(window):
                    place = jnp.where(landed == group * parent_span + slot, w, place)
                out[base + slot] = place

    return pl.pallas_call(
        body,
        in_specs=[SMEM],
        out_specs=SMEM,
        out_shape=jax.ShapeDtypeStruct((OTHER_PIVOT + PIV,), jnp.int32),
        compiler_params=limit_for(BLK, 4),
        name="lookup_table",
    )(block_map)


def cut_slices(table, front, parent, deal, sub):
    size = front.shape[0]
    count = parent.shape[0] // deal
    aligned = sub % BLK == 0

    def body(sc, front_ref, parent_ref, *refs):
        fronts, deals, sems = refs[: count * aligned], refs[count * aligned : -1], refs[-1]
        copies = [
            pltpu.make_async_copy(
                front_ref.at[:, span(sc[COL] ^ m, sub)], out, sems.at[m]
            )
            for m, out in enumerate(fronts)
        ]
        copies += [
            pltpu.make_async_copy(
                parent_ref.at[pl.ds(j * deal, deal), pl.ds(0, PANEL)], out, sems.at[count + j]
            )
            for j, out in enumerate(deals)
        ]
        run_copies(copies)

    outs = pl.pallas_call(
        body,
        in_specs=[SMEM, ANY, ANY],
        out_specs=[VMEM] * (count * aligned + count),
        out_shape=[f32(size, sub)] * (count * aligned) + [f32(deal, PANEL)] * count,
        scratch_shapes=[pltpu.SemaphoreType.DMA((2 * count,))],
        compiler_params=limit_for(sub, 8),
        name="cut_slices",
    )(table, front, parent)
    fronts, deals = outs[: count * aligned], outs[count * aligned :]
    if not aligned:
        col = lax.axis_index("col")
        fronts = [
            lax.dynamic_slice_in_dim(front, (col ^ k) * sub, sub, axis=1) for k in range(count)
        ]
    return fronts, deals


def start_chosen(chosen, choices, target, sem):
    for d, choice in enumerate(choices):

        @pl.when(chosen == d)
        def _():
            pltpu.make_async_copy(choice, target, sem).start()


def turn_of(sc, mask, count):
    return lax.rem(sc[ROW] - (sc[COL] ^ mask) + count, count)


def slice_place(sc, mask, count):
    half = count // 2
    diff = sc[ROW] - (sc[COL] ^ mask)
    near = (diff < 0) & (-diff < half)
    return jnp.where(near, 2 * half - 1 - diff, jnp.abs(diff))


def around_row(value):
    count = lax.axis_size("row")
    half = count // 2
    middle = rotated(value, "row", half)
    below, above, far = [], [], []
    for d in range(1, half):
        below.append(lax.ppermute(value, "row", [(i, i + d) for i in range(count - d)]))
        above.append(lax.ppermute(value, "row", [(i + d, i) for i in range(count - d)]))
        pairs = [(i, i + d) for i in range(half, count - d)]
        pairs += [(i, i - d) for i in range(d, half)]
        far.append(lax.ppermute(middle, "row", pairs))
    return [value] + below + [middle] + far + above


def slice_products(table, rows, around, fronts):
    count = len(rows)
    many = len(around)
    sub, depth = rows[0].shape
    size = count * sub

    def body(*refs):
        sc = refs[0]
        row_refs = refs[1 : 1 + count]
        around_refs = refs[1 + count : 1 + count + many]
        front_refs = refs[1 + count + many : 1 + 2 * count + many]
        outs = refs[1 + 2 * count + many :][:count]
        sides = refs[1 + 3 * count + many :][:count]
        edge, up, row_buf, col_buf, sems = refs[1 + 4 * count + many :]
        places = [col_buf.at[m * sub : (m + 1) * sub] for m in range(count)]
        rows_in = gather_copies(sc, row_refs, row_buf, sems, sub)
        for copy in rows_in:
            copy.start()
        for m, place in enumerate(places):
            start_chosen(slice_place(sc, m, count), around_refs, place, sems.at[count + m])
        for copy in rows_in:
            copy.wait()
        left = halves(row_buf[...])
        for m, place in enumerate(places):
            pltpu.make_async_copy(around_refs[0], place, sems.at[count + m]).wait()
        product = times_transpose(left, halves(col_buf[...]))
        for m in range(count):
            group = sc[COL] ^ m
            part = front_refs[m][...] - product[:, m * sub : (m + 1) * sub]
            outs[m][...] = part

            @pl.when(group == 0)
            def _():
                edge[...] = part[-EDGE:]

            @pl.when(group > 0)
            def _():
                up[group - 1] = part[-EDGE:]

            for mask, side in enumerate(sides):

                @pl.when(group == jnp.maximum((sc[COL] ^ mask) - 1, 0))
                def _():
                    side[...] = part

    return pl.pallas_call(
        body,
        in_specs=[SMEM] + [ANY] * (count + many) + [VMEM] * count,
        out_specs=[VMEM] * (2 * count + 2),
        out_shape=[f32(size, sub)] * (2 * count) + [f32(EDGE, sub), f32(count - 1, EDGE, sub)],
        scratch_shapes=[
            pltpu.VMEM((size, depth), jnp.float32),
            pltpu.VMEM((size, depth), jnp.float32),
            pltpu.SemaphoreType.DMA((2 * count,)),
        ],
        compiler_params=limit_for(sub, 20),
        name="slice_products",
    )(table, *rows, *around, *fronts)


def pack_halo(table, edge, up):
    count = up.shape[0] + 1
    sub = edge.shape[1]

    def body(sc, edge_ref, up_ref, *refs):
        outs, sems = refs[:count], refs[count]
        places = [[out.at[pl.ds(i * EDGE, EDGE)] for i in range(2)] for out in outs]
        for m in range(count):
            group = sc[COL] ^ m
            for i, wanted in enumerate((group, jnp.maximum(group - 1, 0))):

                @pl.when(wanted == 0)
                def _():
                    pltpu.make_async_copy(edge_ref, places[m][i], sems.at[2 * m + i]).start()

                @pl.when(wanted > 0)
                def _():
                    pltpu.make_async_copy(
                        up_ref.at[jnp.maximum(wanted - 1, 0)], places[m][i], sems.at[2 * m + i]
                    ).start()

        for m in range(count):
            for i in range(2):
                pltpu.make_async_copy(edge_ref, places[m][i], sems.at[2 * m + i]).wait()

    return pl.pallas_call(
        body,
        in_specs=[SMEM] + [ANY] * 2,
        out_specs=[VMEM] * count,
        out_shape=[f32(2 * EDGE, sub)] * count,
        scratch_shapes=[pltpu.SemaphoreType.DMA((2 * count,))],
        compiler_params=limit_for(sub, 8),
        name="pack_halo",
    )(table, edge, up)


def to_next_group(packed):
    count = len(packed)
    half = count // 2

    def send(mask):
        pairs = [(i, i ^ mask) for i in range(half, count)]
        if mask > half:
            pairs = [(i, j) for i, j in pairs if j > 0 and (i, j) != (half, 1)]
        if not pairs:
            return None
        return lax.ppermute(packed[mask], "col", pairs)

    got = [packed[0]] + [send(mask) for mask in range(1, count)]
    forwarded = lax.ppermute(got[half], "col", [(0, 1)])
    direct = got[half + 1]
    if direct is not None:
        forwarded = jnp.where(lax.axis_index("col") == 1, forwarded, direct)
    got[half + 1] = forwarded
    return got


def pick_for_cols(table, pieces, masks):
    count = len(pieces)

    def body(*refs):
        sc = refs[0]
        ins = refs[1 : 1 + count]
        outs = refs[1 + count : -1]
        sems = refs[-1]
        for i, mask in enumerate(masks):
            start_chosen(turn_of(sc, mask, count), ins, outs[i], sems.at[i])
        for i in range(len(masks)):
            pltpu.make_async_copy(ins[0], outs[i], sems.at[i]).wait()

    return pl.pallas_call(
        body,
        in_specs=[SMEM] + [ANY] * count,
        out_specs=[VMEM] * len(masks),
        out_shape=[f32(*pieces[0].shape)] * len(masks),
        scratch_shapes=[pltpu.SemaphoreType.DMA((len(masks),))],
        compiler_params=limit_for(BLK, 16),
        name="pick_for_cols",
    )(table, *pieces)


def place_rows(table, homes, edge, deal):
    count = len(homes)
    size, width = homes[0].shape
    rows = HALF * BLK

    def body(*refs):
        sc = refs[0]
        home_refs = refs[1 : 1 + count]
        edge_ref = refs[1 + count]
        outs = refs[2 + count : 2 + 2 * count]
        window, placed, sems = refs[2 + 2 * count :]
        main = window.at[pl.ds(EDGE, size)]
        start_chosen(sc[COL], home_refs, main, sems.at[0])
        copy = pltpu.make_async_copy(edge_ref, window.at[pl.ds(0, EDGE)], sems.at[1])
        copy.start()
        copy.wait()
        pltpu.make_async_copy(home_refs[0], main, sems.at[0]).wait()
        for which, half in ((0, sc[SIB]), (1, 1 - sc[SIB])):
            for slot in range(HALF):
                place = sc[OWN_ROWS + half * HALF + slot]
                block = window[span(jnp.maximum(place, 0), BLK), :]
                lines = slice(slot * BLK, (slot + 1) * BLK)
                placed[which, lines, :] = jnp.where(place >= 0, block, 0.0)
        for m, out in enumerate(outs):
            for which in range(2):
                out[which] = placed[which, span(sc[COL] ^ m, deal), :]

    return pl.pallas_call(
        body,
        in_specs=[SMEM] + [ANY] * (count + 1),
        out_specs=[VMEM] * count,
        out_shape=[f32(2, deal, width)] * count,
        scratch_shapes=[
            pltpu.VMEM((size + EDGE, width), jnp.float32),
            pltpu.VMEM((2, rows, width), jnp.float32),
            pltpu.SemaphoreType.DMA((2,)),
        ],
        compiler_params=limit_for(width, 8),
        name="place_rows",
    )(table, *homes, edge)


def factor_slice(table, small, small_other, dealt, pivot_inverse):
    count = len(small)
    _, rows, sub = small[0].shape

    def body(*refs):
        sc = refs[0]
        pieces = refs[1 : 1 + count]
        other_refs = refs[1 + count : 1 + 2 * count]
        deal_refs = refs[1 + 2 * count : 1 + 3 * count]
        inverse_ref, out, order, child, sums, sems = refs[1 + 3 * count :]
        start_chosen(sc[COL], deal_refs, sums, sems.at[2 * count])
        copies = []
        for k in range(count):
            place = order.at[sc[COL] ^ k]
            copies += [
                pltpu.make_async_copy(pieces[k].at[0], place.at[0], sems.at[2 * k]),
                pltpu.make_async_copy(other_refs[k].at[1], place.at[1], sems.at[2 * k + 1]),
            ]
        run_copies(copies)
        for j in range(count):
            block, lane = divmod(j * sub, BLK)
            for sibling in range(2):
                child[sibling, block, :, lane : lane + sub] = order[j, sibling]
        pltpu.make_async_copy(deal_refs[0], sums, sems.at[2 * count]).wait()
        for p in range(PIV):
            lanes = slice(p * BLK, (p + 1) * BLK)
            added = sums[:, lanes]
            for sibling, base in ((0, OWN_PIVOT), (1, OTHER_PIVOT)):
                place = sc[base + p]
                block = child[sibling, jnp.maximum(place - HB, 0)]
                added += jnp.where(place >= HB, block, 0.0)
            sums[:, lanes] = added
        out[...] = times_transpose(halves(sums[...]), halves(inverse_ref[...]))

    return pl.pallas_call(
        body,
        in_specs=[SMEM] + [ANY] * (3 * count) + [VMEM],
        out_specs=VMEM,
        out_shape=f32(rows, PANEL),
        scratch_shapes=[
            pltpu.VMEM((count, 2, rows, sub), jnp.float32),
            pltpu.VMEM((2, PIV, rows, BLK), jnp.float32),
            pltpu.VMEM((rows, PANEL), jnp.float32),
            pltpu.SemaphoreType.DMA((2 * count + 1,)),
        ],
        compiler_params=limit_for(sub, 16),
        name="factor_slice",
    )(table, *small, *small_other, *dealt, pivot_inverse)


def lay_rows(table, pieces):
    count = len(pieces)
    piece_rows, width = pieces[0].shape
    rows = count * piece_rows

    def body(*refs):
        sc = refs[0]
        ins = refs[1 : 1 + count]
        out, high, low, sems = refs[1 + count :]
        run_copies(gather_copies(sc, ins, out, sems, piece_rows))
        high[...], low[...] = halves(out[...])

    part = jax.ShapeDtypeStruct((rows, width), jnp.bfloat16)
    return pl.pallas_call(
        body,
        in_specs=[SMEM] + [ANY] * count,
        out_specs=[VMEM] * 3,
        out_shape=[f32(rows, width), part, part],
        scratch_shapes=[pltpu.SemaphoreType.DMA((count,))],
        compiler_params=limit_for(BLK, 8),
        name="lay_rows",
    )(table, *pieces)


def assemble(table, parent, own, other, row_factor):
    count = len(own) // 3
    rows, width = parent.shape
    size, sub = own[0].shape
    half = count // 2
    split = BLK // sub

    def body(*refs):
        sc, parent_ref = refs[:2]
        own_refs, other_refs = refs[2 : 2 + 3 * count], refs[2 + 3 * count : 2 + 6 * count]
        factor_ref, out, own_win, other_win, sems = refs[2 + 6 * count :]
        low, high = pl.ds(0, EDGE), pl.ds(EDGE, size)
        always, edges = [], []
        at = 0
        for refs_in, window in ((own_refs, own_win), (other_refs, other_win)):
            for m in range(count):
                home, above, before = (refs_in[i * count + m] for i in range(3))
                piece = sc[COL] ^ m
                main = half + piece
                side = jnp.maximum(piece - half, 0)
                always += [
                    pltpu.make_async_copy(home, window.at[main, high], sems.at[at]),
                    pltpu.make_async_copy(
                        above.at[low], window.at[main, low], sems.at[at + 1]
                    ),
                ]
                edges += [
                    (
                        piece,
                        pltpu.make_async_copy(before, window.at[side, high], sems.at[at + 2]),
                        pltpu.make_async_copy(
                            above.at[pl.ds(EDGE, EDGE)], window.at[side, low], sems.at[at + 3]
                        ),
                    )
                ]
                at += 4
        for copy in always:
            copy.start()
        for piece, first, second in edges:

            @pl.when(piece >= half)
            def _():
                first.start()
                second.start()

        for copy in always:
            copy.wait()
        for piece, first, second in edges:

            @pl.when(piece >= half)
            def _():
                first.wait()
                second.wait()

        for q in range(PBD):
            cols = slice(q * BLK, (q + 1) * BLK)
            for p in range(HALF):
                lines = slice(p * BLK, (p + 1) * BLK)
                total = parent_ref[lines, cols]
                for window, row_base, col_base in (
                    (own_win, OWN_ROWS, OWN_COLS),
                    (other_win, OTHER_ROWS, OTHER_COLS),
                ):
                    down = sc[row_base + sc[SIB] * HALF + p]
                    across = sc[col_base + q]
                    start = jnp.maximum(across, 0) * split
                    pieces = [
                        window[start + i, span(jnp.maximum(down, 0), BLK), :] for i in range(split)
                    ]
                    block = pieces[0] if split == 1 else jnp.concatenate(pieces, axis=1)
                    total += jnp.where((down >= 0) & (across >= 0), block, 0.0)
                if q < PIV:
                    total = jnp.where(sc[COL] == 0, factor_ref[lines, cols], total)
                out[lines, cols] = total

    return pl.pallas_call(
        body,
        in_specs=[SMEM, VMEM] + [ANY] * (6 * count) + [VMEM],
        out_specs=VMEM,
        out_shape=f32(rows, width),
        scratch_shapes=[
            pltpu.VMEM((half + count, size + EDGE, sub), jnp.float32),
            pltpu.VMEM((half + count, size + EDGE, sub), jnp.float32),
            pltpu.SemaphoreType.DMA((8 * count,)),
        ],
        compiler_params=limit_for(sub, 14),
        name="assemble",
    )(table, parent, *own, *other, row_factor)


def finish(table, assembled, row_high, row_low, col_own, col_other):
    count = len(col_own)
    rows, width = assembled.shape
    piece_rows = col_own[0].shape[0]

    def body(*refs):
        sc = refs[0]
        own_refs = refs[1 : 1 + count]
        other_refs = refs[1 + count : 1 + 2 * count]
        base_ref, high_ref, low_ref, out, col_factor, sems = refs[1 + 2 * count :]
        own = gather_copies(sc, own_refs, col_factor.at[sc[SIB]], sems, piece_rows)
        other = gather_copies(
            sc, other_refs, col_factor.at[1 - sc[SIB]], sems, piece_rows, count
        )
        run_copies(own + other)
        left = high_ref[...], low_ref[...]
        first_row = (sc[ROW] * 2 + sc[SIB]) * HALF
        first_col = sc[COL] * PBD
        for side in range(2):
            product = times_transpose(left, halves(col_factor[side]))
            for i in range(HALF):
                q = side * HALF + i
                cols = slice(q * BLK, (q + 1) * BLK)
                for p in range(HALF):
                    lines = slice(p * BLK, (p + 1) * BLK)
                    total = base_ref[lines, cols]
                    inside = (first_col + q >= PIV) & (first_row + p >= PIV)
                    reduced = total - product[lines, i * BLK : (i + 1) * BLK]
                    out[lines, cols] = jnp.where(inside, reduced, total)

    return pl.pallas_call(
        body,
        in_specs=[SMEM] + [ANY] * (2 * count) + [VMEM] * 3,
        out_specs=VMEM,
        out_shape=f32(rows, width),
        scratch_shapes=[
            pltpu.VMEM((2, rows, PANEL), jnp.float32),
            pltpu.SemaphoreType.DMA((2 * count,)),
        ],
        compiler_params=limit_for(BLK, 16),
        name="finish",
    )(table, *col_own, *col_other, assembled, row_high, row_low)


def shards(child_front, child_panel, block_map, parent_front, pivot_inverse):
    count = lax.axis_size("col")
    front = child_front[0]
    panel = child_panel[0]
    sub = panel.shape[0]
    parent_rows, parent_cols = parent_front.shape
    parent_span = parent_cols // BLK
    deal = parent_rows // count

    table = lookup_table(block_map, parent_span)

    def over_col(values):
        got = []
        for k, value in zip(range(1, count), values):
            got.append(swapped(value, "col", k))
        return got

    def over_row(value):
        got = [value]
        for d in range(1, count):
            got.append(rotated(value, "row", d))
        return got

    def to_sibling(value):
        return swapped(value, "sib", 1)

    around = around_row(panel)
    rows = [panel] + over_col([panel] * (count - 1))
    slices, deals = cut_slices(table, front, parent_front, deal, sub)
    fronts = [slices[0]] + over_col(slices[1:])

    dealt = []
    for j in range(count):
        value = deals[j]
        dealt.append(lax.ppermute(value, "col", [(0, j)]) if j else value)

    *slices, edge, up = slice_products(table, rows, around, fronts)
    homes, sides = slices[:count], slices[count:]
    edge = shifted(edge, "row")
    up = shifted(up, "row")
    own = [homes[0]] + over_col(homes[1:])

    small = place_rows(table, homes, edge, deal)
    small = [small[0]] + over_col(small[1:])
    small_other = [to_sibling(value) for value in small]
    above = pack_halo(table, edge, up)
    own = own + [above[0]] + over_col(above[1:]) + to_next_group(sides)
    factor = factor_slice(table, small, small_other, dealt, pivot_inverse)
    factors = over_row(factor)
    row_pieces = [factor] + over_col([factor] * (count - 1))

    row_factor, high, low = lay_rows(table, row_pieces)

    picked = pick_for_cols(table, factors, range(count))
    col_own = [picked[0]] + over_col(picked[1:])
    col_other = [to_sibling(value) for value in col_own]

    other = [to_sibling(value) for value in own]
    assembled = assemble(table, parent_front, own, other, row_factor)
    return finish(table, assembled, high, low, col_own, col_other)


def solution(mesh):
    in_specs = (
        P("sib", "row", "col"),
        P("sib", ("row", "col"), None),
        P(),
        P(("row", "sib"), "col"),
        P(),
    )
    out_specs = P(("row", "sib"), "col")

    return jax.shard_map(shards, mesh=mesh, in_specs=in_specs, out_specs=out_specs, check_vma=False)
```

```python
import jax
import jax.numpy as jnp
from jax import lax
from jax.experimental import pallas as pl
from jax.experimental.pallas import tpu as pltpu
from jax.sharding import PartitionSpec as P


BLK = 128
CBD = 4
PBD = 6
HB = 2
PIV = 4
PANEL = 512
HALF = PBD // 2
EDGE = HB * BLK


SMEM = pl.BlockSpec(memory_space=pltpu.SMEM)
VMEM = pl.BlockSpec(memory_space=pltpu.VMEM)
ANY = pl.BlockSpec(memory_space=pl.ANY)


def limit_for(sub, mebibytes):
    if sub < BLK:
        mebibytes = 56
    return pltpu.CompilerParams(vmem_limit_bytes=mebibytes << 20)


ROW, COL, SIB = 0, 1, 2
OWN_ROWS, OTHER_ROWS, OWN_COLS, OTHER_COLS = 3, 9, 15, 21
OWN_PIVOT, OTHER_PIVOT = 27, 31


def f32(*shape):
    return jax.ShapeDtypeStruct(shape, jnp.float32)


def halves(value):
    high = value.astype(jnp.bfloat16)
    low = (value - high.astype(jnp.float32)).astype(jnp.bfloat16)
    return high, low


def times_transpose(left, right):
    def dot(x, y):
        return lax.dot_general(
            x, y, (((1,), (1,)), ((), ())), preferred_element_type=jnp.float32
        )

    return dot(left[0], right[0]) + (dot(left[0], right[1]) + dot(left[1], right[0]))


def rotated(value, axis, steps):
    count = lax.axis_size(axis)
    return lax.ppermute(value, axis, [(i, (i + steps) % count) for i in range(count)])


def swapped(value, axis, mask):
    count = lax.axis_size(axis)
    return lax.ppermute(value, axis, [(i, i ^ mask) for i in range(count)])


def shifted(value, axis):
    count = lax.axis_size(axis)
    return lax.ppermute(value, axis, [(i, i + 1) for i in range(count - 1)])


def run_copies(copies):
    for copy in copies:
        copy.start()
    for copy in copies:
        copy.wait()


def span(index, size):
    return pl.ds(pl.multiple_of(index * size, size), size)


def gather_copies(table, pieces, target, sems, size, base=0):
    return [
        pltpu.make_async_copy(piece, target.at[span(table[COL] ^ k, size)], sems.at[base + k])
        for k, piece in enumerate(pieces)
    ]


def lookup_table(block_map, parent_span):
    def body(map_ref, out):
        row, col, sib = (lax.axis_index(axis) for axis in ("row", "col", "sib"))
        out[ROW], out[COL], out[SIB] = row, col, sib
        for base, sibling, group, slots in (
            (OWN_ROWS, sib, row, PBD),
            (OTHER_ROWS, 1 - sib, row, PBD),
            (OWN_COLS, sib, col, PBD),
            (OTHER_COLS, 1 - sib, col, PBD),
            (OWN_PIVOT, sib, 0, PIV),
            (OTHER_PIVOT, 1 - sib, 0, PIV),
        ):
            window = []
            for w in range(CBD + HB):
                block = group * CBD + w - HB
                landed = map_ref[sibling, jnp.maximum(block, 0)]
                window.append(jnp.where(block >= 0, landed, -1))
            for slot in range(slots):
                place = jnp.int32(-1)
                for w, landed in enumerate(window):
                    place = jnp.where(landed == group * parent_span + slot, w, place)
                out[base + slot] = place

    return pl.pallas_call(
        body,
        in_specs=[SMEM],
        out_specs=SMEM,
        out_shape=jax.ShapeDtypeStruct((OTHER_PIVOT + PIV,), jnp.int32),
        compiler_params=limit_for(BLK, 4),
        name="lookup_table",
    )(block_map)


def cut_slices(table, front, parent, deal, sub):
    size = front.shape[0]
    count = parent.shape[0] // deal
    aligned = sub % BLK == 0

    def body(sc, front_ref, parent_ref, *refs):
        fronts, deals, sems = refs[: count * aligned], refs[count * aligned : -1], refs[-1]
        copies = [
            pltpu.make_async_copy(
                front_ref.at[:, span(sc[COL] ^ m, sub)], out, sems.at[m]
            )
            for m, out in enumerate(fronts)
        ]
        copies += [
            pltpu.make_async_copy(
                parent_ref.at[pl.ds(j * deal, deal), pl.ds(0, PANEL)], out, sems.at[count + j]
            )
            for j, out in enumerate(deals)
        ]
        run_copies(copies)

    outs = pl.pallas_call(
        body,
        in_specs=[SMEM, ANY, ANY],
        out_specs=[VMEM] * (count * aligned + count),
        out_shape=[f32(size, sub)] * (count * aligned) + [f32(deal, PANEL)] * count,
        scratch_shapes=[pltpu.SemaphoreType.DMA((2 * count,))],
        compiler_params=limit_for(sub, 8),
        name="cut_slices",
    )(table, front, parent)
    fronts, deals = outs[: count * aligned], outs[count * aligned :]
    if not aligned:
        col = lax.axis_index("col")
        fronts = [
            lax.dynamic_slice_in_dim(front, (col ^ k) * sub, sub, axis=1) for k in range(count)
        ]
    return fronts, deals


def start_chosen(chosen, choices, target, sem):
    for d, choice in enumerate(choices):

        @pl.when(chosen == d)
        def _():
            pltpu.make_async_copy(choice, target, sem).start()


def turn_of(sc, mask, count):
    return lax.rem(sc[ROW] - (sc[COL] ^ mask) + count, count)


def slice_place(sc, mask, count):
    half = count // 2
    diff = sc[ROW] - (sc[COL] ^ mask)
    near = (diff < 0) & (-diff < half)
    return jnp.where(near, 2 * half - 1 - diff, jnp.abs(diff))


def around_row(value):
    count = lax.axis_size("row")
    half = count // 2
    rows = value.shape[0] // 2
    middle, far = [], [[] for _ in range(1, half)]
    for part in range(2):
        middle.append(rotated(value[part * rows : (part + 1) * rows], "row", half))
    below, above = [], []
    for d in range(1, half):
        below.append(lax.ppermute(value, "row", [(i, i + d) for i in range(count - d)]))
        above.append(lax.ppermute(value, "row", [(i + d, i) for i in range(count - d)]))
        pairs = [(i, i + d) for i in range(half, count - d)]
        pairs += [(i, i - d) for i in range(d, half)]
        for part in range(2):
            far[d - 1].append(lax.ppermute(middle[part], "row", pairs))
    return [[value]] + [[v] for v in below] + [middle] + far + [[v] for v in above]


def slice_products(table, rows, around, fronts):
    count = len(rows)
    flat = sum(around, [])
    many = len(flat)
    sub, depth = rows[0].shape
    size = count * sub
    part_rows = sub // 2

    def body(*refs):
        sc = refs[0]
        row_refs = refs[1 : 1 + count]
        around_refs = refs[1 + count : 1 + count + many]
        front_refs = refs[1 + count + many : 1 + 2 * count + many]
        outs = refs[1 + 2 * count + many :][:count]
        edge, up, row_buf, col_buf, sems = refs[1 + 3 * count + many :]
        places = [col_buf.at[m * sub : (m + 1) * sub] for m in range(count)]
        rows_in = gather_copies(sc, row_refs, row_buf, sems, sub)
        for copy in rows_in:
            copy.start()
        choices, taken = ([], []), 0
        for group_parts in around:
            found = around_refs[taken : taken + len(group_parts)]
            taken += len(group_parts)
            for part in range(2):
                lines = pl.ds(part * part_rows, part_rows)
                choices[part].append(found[part] if len(found) == 2 else found[0].at[lines])
        targets = [
            (m, part, place.at[part * part_rows : (part + 1) * part_rows])
            for m, place in enumerate(places)
            for part in range(2)
        ]
        for m, part, target in targets:
            start_chosen(
                slice_place(sc, m, count), choices[part], target, sems.at[count + 2 * m + part]
            )
        for copy in rows_in:
            copy.wait()
        left = halves(row_buf[...])
        for m, part, target in targets:
            pltpu.make_async_copy(choices[part][0], target, sems.at[count + 2 * m + part]).wait()
        product = times_transpose(left, halves(col_buf[...]))
        for m in range(count):
            group = sc[COL] ^ m
            part = front_refs[m][...] - product[:, m * sub : (m + 1) * sub]
            outs[m][...] = part

            @pl.when(group == 0)
            def _():
                edge[...] = part[-EDGE:]

            @pl.when(group > 0)
            def _():
                up[group - 1] = part[-EDGE:]

    return pl.pallas_call(
        body,
        in_specs=[SMEM] + [ANY] * (count + many) + [VMEM] * count,
        out_specs=[VMEM] * (count + 2),
        out_shape=[f32(size, sub)] * count + [f32(EDGE, sub), f32(count - 1, EDGE, sub)],
        scratch_shapes=[
            pltpu.VMEM((size, depth), jnp.float32),
            pltpu.VMEM((size, depth), jnp.float32),
            pltpu.SemaphoreType.DMA((3 * count,)),
        ],
        compiler_params=limit_for(sub, 20),
        name="slice_products",
    )(table, *rows, *flat, *fronts)


def pack_halo(table, homes, edge, up):
    count = len(homes)
    size, sub = homes[0].shape

    def body(*refs):
        sc = refs[0]
        home_refs = refs[1 : 1 + count]
        edge_ref, up_ref = refs[1 + count : 3 + count]
        outs = refs[3 + count : 3 + 2 * count]
        sems = refs[-1]
        near, far = pl.ds(size, EDGE), pl.ds(size + EDGE, EDGE)
        for m, out in enumerate(outs):
            group = sc[COL] ^ m
            before = jnp.maximum(group - 1, 0)
            start_chosen(before ^ sc[COL], home_refs, out.at[pl.ds(0, size)], sems.at[3 * m])
            for i, (wanted, place) in enumerate(((group, near), (before, far))):

                @pl.when(wanted == 0)
                def _():
                    pltpu.make_async_copy(edge_ref, out.at[place], sems.at[3 * m + 1 + i]).start()

                @pl.when(wanted > 0)
                def _():
                    pltpu.make_async_copy(
                        up_ref.at[jnp.maximum(wanted - 1, 0)], out.at[place], sems.at[3 * m + 1 + i]
                    ).start()

        for m, out in enumerate(outs):
            pltpu.make_async_copy(home_refs[0], out.at[pl.ds(0, size)], sems.at[3 * m]).wait()
            for i, place in enumerate((near, far)):
                pltpu.make_async_copy(edge_ref, out.at[place], sems.at[3 * m + 1 + i]).wait()

    return pl.pallas_call(
        body,
        in_specs=[SMEM] + [ANY] * (count + 2),
        out_specs=[VMEM] * count,
        out_shape=[f32(size + 2 * EDGE, sub)] * count,
        scratch_shapes=[pltpu.SemaphoreType.DMA((3 * count,))],
        compiler_params=limit_for(sub, 8),
        name="pack_halo",
    )(table, *homes, edge, up)


def pick_for_cols(table, pieces, masks):
    count = len(pieces)

    def body(*refs):
        sc = refs[0]
        ins = refs[1 : 1 + count]
        outs = refs[1 + count : -1]
        sems = refs[-1]
        for i, mask in enumerate(masks):
            start_chosen(turn_of(sc, mask, count), ins, outs[i], sems.at[i])
        for i in range(len(masks)):
            pltpu.make_async_copy(ins[0], outs[i], sems.at[i]).wait()

    return pl.pallas_call(
        body,
        in_specs=[SMEM] + [ANY] * count,
        out_specs=[VMEM] * len(masks),
        out_shape=[f32(*pieces[0].shape)] * len(masks),
        scratch_shapes=[pltpu.SemaphoreType.DMA((len(masks),))],
        compiler_params=limit_for(BLK, 16),
        name="pick_for_cols",
    )(table, *pieces)


def place_rows(table, homes, edge, deal):
    count = len(homes)
    size, width = homes[0].shape
    rows = HALF * BLK

    def body(*refs):
        sc = refs[0]
        home_refs = refs[1 : 1 + count]
        edge_ref = refs[1 + count]
        outs = refs[2 + count : 2 + 2 * count]
        window, placed, sems = refs[2 + 2 * count :]
        main = window.at[pl.ds(EDGE, size)]
        start_chosen(sc[COL], home_refs, main, sems.at[0])
        copy = pltpu.make_async_copy(edge_ref, window.at[pl.ds(0, EDGE)], sems.at[1])
        copy.start()
        copy.wait()
        pltpu.make_async_copy(home_refs[0], main, sems.at[0]).wait()
        for which, half in ((0, sc[SIB]), (1, 1 - sc[SIB])):
            for slot in range(HALF):
                place = sc[OWN_ROWS + half * HALF + slot]
                block = window[span(jnp.maximum(place, 0), BLK), :]
                lines = slice(slot * BLK, (slot + 1) * BLK)
                placed[which, lines, :] = jnp.where(place >= 0, block, 0.0)
        for m, out in enumerate(outs):
            for which in range(2):
                out[which] = placed[which, span(sc[COL] ^ m, deal), :]

    return pl.pallas_call(
        body,
        in_specs=[SMEM] + [ANY] * (count + 1),
        out_specs=[VMEM] * count,
        out_shape=[f32(2, deal, width)] * count,
        scratch_shapes=[
            pltpu.VMEM((size + EDGE, width), jnp.float32),
            pltpu.VMEM((2, rows, width), jnp.float32),
            pltpu.SemaphoreType.DMA((2,)),
        ],
        compiler_params=limit_for(width, 8),
        name="place_rows",
    )(table, *homes, edge)


def factor_slice(table, small, small_other, dealt, pivot_inverse):
    count = len(small)
    _, rows, sub = small[0].shape

    def body(*refs):
        sc = refs[0]
        pieces = refs[1 : 1 + count]
        other_refs = refs[1 + count : 1 + 2 * count]
        deal_refs = refs[1 + 2 * count : 1 + 3 * count]
        inverse_ref, out, order, child, sums, sems = refs[1 + 3 * count :]
        start_chosen(sc[COL], deal_refs, sums, sems.at[2 * count])
        copies = []
        for k in range(count):
            place = order.at[sc[COL] ^ k]
            copies += [
                pltpu.make_async_copy(pieces[k].at[0], place.at[0], sems.at[2 * k]),
                pltpu.make_async_copy(other_refs[k].at[1], place.at[1], sems.at[2 * k + 1]),
            ]
        run_copies(copies)
        for j in range(count):
            block, lane = divmod(j * sub, BLK)
            for sibling in range(2):
                child[sibling, block, :, lane : lane + sub] = order[j, sibling]
        pltpu.make_async_copy(deal_refs[0], sums, sems.at[2 * count]).wait()
        for p in range(PIV):
            lanes = slice(p * BLK, (p + 1) * BLK)
            added = sums[:, lanes]
            for sibling, base in ((0, OWN_PIVOT), (1, OTHER_PIVOT)):
                place = sc[base + p]
                block = child[sibling, jnp.maximum(place - HB, 0)]
                added += jnp.where(place >= HB, block, 0.0)
            sums[:, lanes] = added
        out[...] = times_transpose(halves(sums[...]), halves(inverse_ref[...]))

    return pl.pallas_call(
        body,
        in_specs=[SMEM] + [ANY] * (3 * count) + [VMEM],
        out_specs=VMEM,
        out_shape=f32(rows, PANEL),
        scratch_shapes=[
            pltpu.VMEM((count, 2, rows, sub), jnp.float32),
            pltpu.VMEM((2, PIV, rows, BLK), jnp.float32),
            pltpu.VMEM((rows, PANEL), jnp.float32),
            pltpu.SemaphoreType.DMA((2 * count + 1,)),
        ],
        compiler_params=limit_for(sub, 16),
        name="factor_slice",
    )(table, *small, *small_other, *dealt, pivot_inverse)


def lay_rows(table, pieces):
    count = len(pieces)
    piece_rows, width = pieces[0].shape
    rows = count * piece_rows

    def body(*refs):
        sc = refs[0]
        ins = refs[1 : 1 + count]
        out, high, low, sems = refs[1 + count :]
        run_copies(gather_copies(sc, ins, out, sems, piece_rows))
        high[...], low[...] = halves(out[...])

    part = jax.ShapeDtypeStruct((rows, width), jnp.bfloat16)
    return pl.pallas_call(
        body,
        in_specs=[SMEM] + [ANY] * count,
        out_specs=[VMEM] * 3,
        out_shape=[f32(rows, width), part, part],
        scratch_shapes=[pltpu.SemaphoreType.DMA((count,))],
        compiler_params=limit_for(BLK, 8),
        name="lay_rows",
    )(table, *pieces)


def assemble(table, parent, own, other, row_factor):
    count = len(own) // 2
    rows, width = parent.shape
    size, sub = own[0].shape
    half = count // 2
    split = BLK // sub

    def body(*refs):
        sc, parent_ref = refs[:2]
        own_refs, other_refs = refs[2 : 2 + 2 * count], refs[2 + 2 * count : 2 + 4 * count]
        factor_ref, out, own_win, other_win, sems = refs[2 + 4 * count :]
        at = 0
        always, edges = [], []
        for refs_in, window in ((own_refs, own_win), (other_refs, other_win)):
            for m in range(count):
                home, halo = refs_in[m], refs_in[count + m]
                piece = sc[COL] ^ m
                main = half + piece
                side = jnp.maximum(piece - half, 0)
                low, high = pl.ds(0, EDGE), pl.ds(EDGE, size)
                always += [
                    pltpu.make_async_copy(home, window.at[main, high], sems.at[at]),
                    pltpu.make_async_copy(
                        halo.at[pl.ds(size, EDGE)], window.at[main, low], sems.at[at + 1]
                    ),
                ]
                edges += [
                    (
                        piece,
                        pltpu.make_async_copy(
                            halo.at[pl.ds(0, size)], window.at[side, high], sems.at[at + 2]
                        ),
                        pltpu.make_async_copy(
                            halo.at[pl.ds(size + EDGE, EDGE)],
                            window.at[side, low],
                            sems.at[at + 3],
                        ),
                    )
                ]
                at += 4
        for copy in always:
            copy.start()
        for piece, first, second in edges:

            @pl.when(piece >= half)
            def _():
                first.start()
                second.start()

        for copy in always:
            copy.wait()
        for piece, first, second in edges:

            @pl.when(piece >= half)
            def _():
                first.wait()
                second.wait()

        for q in range(PBD):
            cols = slice(q * BLK, (q + 1) * BLK)
            for p in range(HALF):
                lines = slice(p * BLK, (p + 1) * BLK)
                total = parent_ref[lines, cols]
                for window, row_base, col_base in (
                    (own_win, OWN_ROWS, OWN_COLS),
                    (other_win, OTHER_ROWS, OTHER_COLS),
                ):
                    down = sc[row_base + sc[SIB] * HALF + p]
                    across = sc[col_base + q]
                    start = jnp.maximum(across, 0) * split
                    pieces = [
                        window[start + i, span(jnp.maximum(down, 0), BLK), :] for i in range(split)
                    ]
                    block = pieces[0] if split == 1 else jnp.concatenate(pieces, axis=1)
                    total += jnp.where((down >= 0) & (across >= 0), block, 0.0)
                if q < PIV:
                    total = jnp.where(sc[COL] == 0, factor_ref[lines, cols], total)
                out[lines, cols] = total

    return pl.pallas_call(
        body,
        in_specs=[SMEM, VMEM] + [ANY] * (4 * count) + [VMEM],
        out_specs=VMEM,
        out_shape=f32(rows, width),
        scratch_shapes=[
            pltpu.VMEM((half + count, size + EDGE, sub), jnp.float32),
            pltpu.VMEM((half + count, size + EDGE, sub), jnp.float32),
            pltpu.SemaphoreType.DMA((8 * count,)),
        ],
        compiler_params=limit_for(sub, 14),
        name="assemble",
    )(table, parent, *own, *other, row_factor)


def finish(table, assembled, row_high, row_low, col_own, col_other):
    count = len(col_own)
    rows, width = assembled.shape
    piece_rows = col_own[0].shape[0]

    def body(*refs):
        sc = refs[0]
        own_refs = refs[1 : 1 + count]
        other_refs = refs[1 + count : 1 + 2 * count]
        base_ref, high_ref, low_ref, out, col_factor, sems = refs[1 + 2 * count :]
        own = gather_copies(sc, own_refs, col_factor.at[sc[SIB]], sems, piece_rows)
        other = gather_copies(
            sc, other_refs, col_factor.at[1 - sc[SIB]], sems, piece_rows, count
        )
        run_copies(own + other)
        left = high_ref[...], low_ref[...]
        first_row = (sc[ROW] * 2 + sc[SIB]) * HALF
        first_col = sc[COL] * PBD
        for side in range(2):
            product = times_transpose(left, halves(col_factor[side]))
            for i in range(HALF):
                q = side * HALF + i
                cols = slice(q * BLK, (q + 1) * BLK)
                for p in range(HALF):
                    lines = slice(p * BLK, (p + 1) * BLK)
                    total = base_ref[lines, cols]
                    inside = (first_col + q >= PIV) & (first_row + p >= PIV)
                    reduced = total - product[lines, i * BLK : (i + 1) * BLK]
                    out[lines, cols] = jnp.where(inside, reduced, total)

    return pl.pallas_call(
        body,
        in_specs=[SMEM] + [ANY] * (2 * count) + [VMEM] * 3,
        out_specs=VMEM,
        out_shape=f32(rows, width),
        scratch_shapes=[
            pltpu.VMEM((2, rows, PANEL), jnp.float32),
            pltpu.SemaphoreType.DMA((2 * count,)),
        ],
        compiler_params=limit_for(BLK, 16),
        name="finish",
    )(table, *col_own, *col_other, assembled, row_high, row_low)


def shards(child_front, child_panel, block_map, parent_front, pivot_inverse):
    count = lax.axis_size("col")
    front = child_front[0]
    panel = child_panel[0]
    sub = panel.shape[0]
    parent_rows, parent_cols = parent_front.shape
    parent_span = parent_cols // BLK
    deal = parent_rows // count

    table = lookup_table(block_map, parent_span)

    def over_col(values):
        got = []
        for k, value in zip(range(1, count), values):
            got.append(swapped(value, "col", k))
        return got

    def over_row(value):
        got = [value]
        for d in range(1, count):
            got.append(rotated(value, "row", d))
        return got

    def to_sibling(value):
        return swapped(value, "sib", 1)

    around = around_row(panel)
    rows = [panel] + over_col([panel] * (count - 1))
    slices, deals = cut_slices(table, front, parent_front, deal, sub)
    fronts = [slices[0]] + over_col(slices[1:])

    dealt = []
    for j in range(count):
        value = deals[j]
        dealt.append(lax.ppermute(value, "col", [(0, j)]) if j else value)

    *homes, edge, up = slice_products(table, rows, around, fronts)
    edge = shifted(edge, "row")
    up = shifted(up, "row")
    own = [homes[0]] + over_col(homes[1:])

    small = place_rows(table, homes, edge, deal)
    small = [small[0]] + over_col(small[1:])
    small_other = [to_sibling(value) for value in small]
    packed = pack_halo(table, homes, edge, up)
    own = own + [packed[0]] + over_col(packed[1:])
    factor = factor_slice(table, small, small_other, dealt, pivot_inverse)
    factors = over_row(factor)
    row_pieces = [factor] + over_col([factor] * (count - 1))

    row_factor, high, low = lay_rows(table, row_pieces)

    picked = pick_for_cols(table, factors, range(count))
    col_own = [picked[0]] + over_col(picked[1:])
    col_other = [to_sibling(value) for value in col_own]

    other = [to_sibling(value) for value in own]
    assembled = assemble(table, parent_front, own, other, row_factor)
    return finish(table, assembled, high, low, col_own, col_other)


def solution(mesh):
    in_specs = (
        P("sib", "row", "col"),
        P("sib", ("row", "col"), None),
        P(),
        P(("row", "sib"), "col"),
        P(),
    )
    out_specs = P(("row", "sib"), "col")

    return jax.shard_map(shards, mesh=mesh, in_specs=in_specs, out_specs=out_specs, check_vma=False)
```

```python
import jax
import jax.numpy as jnp
from jax import lax
from jax.experimental import pallas as pl
from jax.experimental.pallas import tpu as pltpu
from jax.sharding import PartitionSpec as P


BLK = 128
CBD = 4
PBD = 6
HB = 2
PIV = 4
PANEL = 512
HALF = PBD // 2
EDGE = HB * BLK


SMEM = pl.BlockSpec(memory_space=pltpu.SMEM)
VMEM = pl.BlockSpec(memory_space=pltpu.VMEM)
ANY = pl.BlockSpec(memory_space=pl.ANY)


def limit_for(sub, mebibytes):
    if sub < BLK:
        mebibytes = 56
    return pltpu.CompilerParams(vmem_limit_bytes=mebibytes << 20)


ROW, COL, SIB = 0, 1, 2
OWN_ROWS, OTHER_ROWS, OWN_COLS, OTHER_COLS = 3, 9, 15, 21
OWN_PIVOT, OTHER_PIVOT = 27, 31


def f32(*shape):
    return jax.ShapeDtypeStruct(shape, jnp.float32)


def halves(value):
    high = value.astype(jnp.bfloat16)
    low = (value - high.astype(jnp.float32)).astype(jnp.bfloat16)
    return high, low


def times_transpose(left, right):
    def dot(x, y):
        return lax.dot_general(
            x, y, (((1,), (1,)), ((), ())), preferred_element_type=jnp.float32
        )

    return dot(left[0], right[0]) + (dot(left[0], right[1]) + dot(left[1], right[0]))


def rotated(value, axis, steps):
    count = lax.axis_size(axis)
    return lax.ppermute(value, axis, [(i, (i + steps) % count) for i in range(count)])


def swapped(value, axis, mask):
    count = lax.axis_size(axis)
    return lax.ppermute(value, axis, [(i, i ^ mask) for i in range(count)])


def shifted(value, axis):
    count = lax.axis_size(axis)
    return lax.ppermute(value, axis, [(i, i + 1) for i in range(count - 1)])


def run_copies(copies):
    for copy in copies:
        copy.start()
    for copy in copies:
        copy.wait()


def span(index, size):
    return pl.ds(pl.multiple_of(index * size, size), size)


def gather_copies(table, pieces, target, sems, size, base=0):
    return [
        pltpu.make_async_copy(piece, target.at[span(table[COL] ^ k, size)], sems.at[base + k])
        for k, piece in enumerate(pieces)
    ]


def lookup_table(block_map, parent_span):
    def body(map_ref, out):
        row, col, sib = (lax.axis_index(axis) for axis in ("row", "col", "sib"))
        out[ROW], out[COL], out[SIB] = row, col, sib
        for base, sibling, group, slots in (
            (OWN_ROWS, sib, row, PBD),
            (OTHER_ROWS, 1 - sib, row, PBD),
            (OWN_COLS, sib, col, PBD),
            (OTHER_COLS, 1 - sib, col, PBD),
            (OWN_PIVOT, sib, 0, PIV),
            (OTHER_PIVOT, 1 - sib, 0, PIV),
        ):
            window = []
            for w in range(CBD + HB):
                block = group * CBD + w - HB
                landed = map_ref[sibling, jnp.maximum(block, 0)]
                window.append(jnp.where(block >= 0, landed, -1))
            for slot in range(slots):
                place = jnp.int32(-1)
                for w, landed in enumerate(window):
                    place = jnp.where(landed == group * parent_span + slot, w, place)
                out[base + slot] = place

    return pl.pallas_call(
        body,
        in_specs=[SMEM],
        out_specs=SMEM,
        out_shape=jax.ShapeDtypeStruct((OTHER_PIVOT + PIV,), jnp.int32),
        compiler_params=limit_for(BLK, 4),
        name="lookup_table",
    )(block_map)


def cut_slices(table, front, parent, deal, sub):
    size = front.shape[0]
    count = parent.shape[0] // deal
    aligned = sub % BLK == 0

    def body(sc, front_ref, parent_ref, *refs):
        fronts, deals, sems = refs[: count * aligned], refs[count * aligned : -1], refs[-1]
        copies = [
            pltpu.make_async_copy(
                front_ref.at[:, span(sc[COL] ^ m, sub)], out, sems.at[m]
            )
            for m, out in enumerate(fronts)
        ]
        copies += [
            pltpu.make_async_copy(
                parent_ref.at[pl.ds(j * deal, deal), pl.ds(0, PANEL)], out, sems.at[count + j]
            )
            for j, out in enumerate(deals)
        ]
        run_copies(copies)

    outs = pl.pallas_call(
        body,
        in_specs=[SMEM, ANY, ANY],
        out_specs=[VMEM] * (count * aligned + count),
        out_shape=[f32(size, sub)] * (count * aligned) + [f32(deal, PANEL)] * count,
        scratch_shapes=[pltpu.SemaphoreType.DMA((2 * count,))],
        compiler_params=limit_for(sub, 8),
        name="cut_slices",
    )(table, front, parent)
    fronts, deals = outs[: count * aligned], outs[count * aligned :]
    if not aligned:
        col = lax.axis_index("col")
        fronts = [
            lax.dynamic_slice_in_dim(front, (col ^ k) * sub, sub, axis=1) for k in range(count)
        ]
    return fronts, deals


def start_chosen(chosen, choices, target, sem):
    for d, choice in enumerate(choices):

        @pl.when(chosen == d)
        def _():
            pltpu.make_async_copy(choice, target, sem).start()


def turn_of(sc, mask, count):
    return lax.rem(sc[ROW] - (sc[COL] ^ mask) + count, count)


def slice_place(sc, mask, count):
    half = count // 2
    diff = sc[ROW] - (sc[COL] ^ mask)
    near = (diff < 0) & (-diff < half)
    return jnp.where(near, 2 * half - 1 - diff, jnp.abs(diff))


def around_row(value):
    count = lax.axis_size("row")
    half = count // 2
    middle = rotated(value, "row", half)
    below, above, far = [], [], []
    for d in range(1, half):
        below.append(lax.ppermute(value, "row", [(i, i + d) for i in range(count - d)]))
        above.append(lax.ppermute(value, "row", [(i + d, i) for i in range(count - d)]))
        pairs = [(i, i + d) for i in range(half, count - d)]
        pairs += [(i, i - d) for i in range(d, half)]
        far.append(lax.ppermute(middle, "row", pairs))
    return [value] + below + [middle] + far + above


def slice_products(table, rows, around, fronts):
    count = len(rows)
    many = len(around)
    sub, depth = rows[0].shape
    size = count * sub

    def body(*refs):
        sc = refs[0]
        row_refs = refs[1 : 1 + count]
        around_refs = refs[1 + count : 1 + count + many]
        front_refs = refs[1 + count + many : 1 + 2 * count + many]
        outs = refs[1 + 2 * count + many :][:count]
        edge, up, row_buf, col_buf, sems = refs[1 + 3 * count + many :]
        places = [col_buf.at[m * sub : (m + 1) * sub] for m in range(count)]
        rows_in = gather_copies(sc, row_refs, row_buf, sems, sub)
        for copy in rows_in:
            copy.start()
        for m, place in enumerate(places):
            start_chosen(slice_place(sc, m, count), around_refs, place, sems.at[count + m])
        for copy in rows_in:
            copy.wait()
        left = halves(row_buf[...])
        for m, place in enumerate(places):
            pltpu.make_async_copy(around_refs[0], place, sems.at[count + m]).wait()
        product = times_transpose(left, halves(col_buf[...]))
        for m in range(count):
            group = sc[COL] ^ m
            part = front_refs[m][...] - product[:, m * sub : (m + 1) * sub]
            outs[m][...] = part

            @pl.when(group == 0)
            def _():
                edge[...] = part[-EDGE:]

            @pl.when(group > 0)
            def _():
                up[group - 1] = part[-EDGE:]

    return pl.pallas_call(
        body,
        in_specs=[SMEM] + [ANY] * (count + many) + [VMEM] * count,
        out_specs=[VMEM] * (count + 2),
        out_shape=[f32(size, sub)] * count + [f32(EDGE, sub), f32(count - 1, EDGE, sub)],
        scratch_shapes=[
            pltpu.VMEM((size, depth), jnp.float32),
            pltpu.VMEM((size, depth), jnp.float32),
            pltpu.SemaphoreType.DMA((2 * count,)),
        ],
        compiler_params=limit_for(sub, 20),
        name="slice_products",
    )(table, *rows, *around, *fronts)


def pack_halo(table, homes, edge, up):
    count = len(homes)
    size, sub = homes[0].shape

    def body(*refs):
        sc = refs[0]
        home_refs = refs[1 : 1 + count]
        edge_ref, up_ref = refs[1 + count : 3 + count]
        outs = refs[3 + count : 3 + 2 * count]
        sems = refs[-1]
        near, far = pl.ds(size, EDGE), pl.ds(size + EDGE, EDGE)
        for m, out in enumerate(outs):
            group = sc[COL] ^ m
            before = jnp.maximum(group - 1, 0)
            start_chosen(before ^ sc[COL], home_refs, out.at[pl.ds(0, size)], sems.at[3 * m])
            for i, (wanted, place) in enumerate(((group, near), (before, far))):

                @pl.when(wanted == 0)
                def _():
                    pltpu.make_async_copy(edge_ref, out.at[place], sems.at[3 * m + 1 + i]).start()

                @pl.when(wanted > 0)
                def _():
                    pltpu.make_async_copy(
                        up_ref.at[jnp.maximum(wanted - 1, 0)], out.at[place], sems.at[3 * m + 1 + i]
                    ).start()

        for m, out in enumerate(outs):
            pltpu.make_async_copy(home_refs[0], out.at[pl.ds(0, size)], sems.at[3 * m]).wait()
            for i, place in enumerate((near, far)):
                pltpu.make_async_copy(edge_ref, out.at[place], sems.at[3 * m + 1 + i]).wait()

    return pl.pallas_call(
        body,
        in_specs=[SMEM] + [ANY] * (count + 2),
        out_specs=[VMEM] * count,
        out_shape=[f32(size + 2 * EDGE, sub)] * count,
        scratch_shapes=[pltpu.SemaphoreType.DMA((3 * count,))],
        compiler_params=limit_for(sub, 8),
        name="pack_halo",
    )(table, *homes, edge, up)


def pick_for_cols(table, pieces, masks):
    count = len(pieces)

    def body(*refs):
        sc = refs[0]
        ins = refs[1 : 1 + count]
        outs = refs[1 + count : -1]
        sems = refs[-1]
        for i, mask in enumerate(masks):
            start_chosen(turn_of(sc, mask, count), ins, outs[i], sems.at[i])
        for i in range(len(masks)):
            pltpu.make_async_copy(ins[0], outs[i], sems.at[i]).wait()

    return pl.pallas_call(
        body,
        in_specs=[SMEM] + [ANY] * count,
        out_specs=[VMEM] * len(masks),
        out_shape=[f32(*pieces[0].shape)] * len(masks),
        scratch_shapes=[pltpu.SemaphoreType.DMA((len(masks),))],
        compiler_params=limit_for(BLK, 16),
        name="pick_for_cols",
    )(table, *pieces)


def place_rows(table, homes, edge, deal):
    count = len(homes)
    size, width = homes[0].shape
    rows = HALF * BLK

    def body(*refs):
        sc = refs[0]
        home_refs = refs[1 : 1 + count]
        edge_ref = refs[1 + count]
        outs = refs[2 + count : 2 + 2 * count]
        window, placed, sems = refs[2 + 2 * count :]
        main = window.at[pl.ds(EDGE, size)]
        start_chosen(sc[COL], home_refs, main, sems.at[0])
        copy = pltpu.make_async_copy(edge_ref, window.at[pl.ds(0, EDGE)], sems.at[1])
        copy.start()
        copy.wait()
        pltpu.make_async_copy(home_refs[0], main, sems.at[0]).wait()
        for which, half in ((0, sc[SIB]), (1, 1 - sc[SIB])):
            for slot in range(HALF):
                place = sc[OWN_ROWS + half * HALF + slot]
                block = window[span(jnp.maximum(place, 0), BLK), :]
                lines = slice(slot * BLK, (slot + 1) * BLK)
                placed[which, lines, :] = jnp.where(place >= 0, block, 0.0)
        for m, out in enumerate(outs):
            for which in range(2):
                out[which] = placed[which, span(sc[COL] ^ m, deal), :]

    return pl.pallas_call(
        body,
        in_specs=[SMEM] + [ANY] * (count + 1),
        out_specs=[VMEM] * count,
        out_shape=[f32(2, deal, width)] * count,
        scratch_shapes=[
            pltpu.VMEM((size + EDGE, width), jnp.float32),
            pltpu.VMEM((2, rows, width), jnp.float32),
            pltpu.SemaphoreType.DMA((2,)),
        ],
        compiler_params=limit_for(width, 8),
        name="place_rows",
    )(table, *homes, edge)


def factor_slice(table, small, small_other, dealt, pivot_inverse):
    count = len(small)
    _, rows, sub = small[0].shape

    def body(*refs):
        sc = refs[0]
        pieces = refs[1 : 1 + count]
        other_refs = refs[1 + count : 1 + 2 * count]
        deal_refs = refs[1 + 2 * count : 1 + 3 * count]
        inverse_ref, out, order, child, sums, sems = refs[1 + 3 * count :]
        start_chosen(sc[COL], deal_refs, sums, sems.at[2 * count])
        copies = []
        for k in range(count):
            place = order.at[sc[COL] ^ k]
            copies += [
                pltpu.make_async_copy(pieces[k].at[0], place.at[0], sems.at[2 * k]),
                pltpu.make_async_copy(other_refs[k].at[1], place.at[1], sems.at[2 * k + 1]),
            ]
        run_copies(copies)
        for j in range(count):
            block, lane = divmod(j * sub, BLK)
            for sibling in range(2):
                child[sibling, block, :, lane : lane + sub] = order[j, sibling]
        pltpu.make_async_copy(deal_refs[0], sums, sems.at[2 * count]).wait()
        for p in range(PIV):
            lanes = slice(p * BLK, (p + 1) * BLK)
            added = sums[:, lanes]
            for sibling, base in ((0, OWN_PIVOT), (1, OTHER_PIVOT)):
                place = sc[base + p]
                block = child[sibling, jnp.maximum(place - HB, 0)]
                added += jnp.where(place >= HB, block, 0.0)
            sums[:, lanes] = added
        out[...] = times_transpose(halves(sums[...]), halves(inverse_ref[...]))

    return pl.pallas_call(
        body,
        in_specs=[SMEM] + [ANY] * (3 * count) + [VMEM],
        out_specs=VMEM,
        out_shape=f32(rows, PANEL),
        scratch_shapes=[
            pltpu.VMEM((count, 2, rows, sub), jnp.float32),
            pltpu.VMEM((2, PIV, rows, BLK), jnp.float32),
            pltpu.VMEM((rows, PANEL), jnp.float32),
            pltpu.SemaphoreType.DMA((2 * count + 1,)),
        ],
        compiler_params=limit_for(sub, 16),
        name="factor_slice",
    )(table, *small, *small_other, *dealt, pivot_inverse)


def lay_rows(table, pieces):
    count = len(pieces)
    piece_rows, width = pieces[0].shape
    rows = count * piece_rows

    def body(*refs):
        sc = refs[0]
        ins = refs[1 : 1 + count]
        out, high, low, sems = refs[1 + count :]
        run_copies(gather_copies(sc, ins, out, sems, piece_rows))
        high[...], low[...] = halves(out[...])

    part = jax.ShapeDtypeStruct((rows, width), jnp.bfloat16)
    return pl.pallas_call(
        body,
        in_specs=[SMEM] + [ANY] * count,
        out_specs=[VMEM] * 3,
        out_shape=[f32(rows, width), part, part],
        scratch_shapes=[pltpu.SemaphoreType.DMA((count,))],
        compiler_params=limit_for(BLK, 8),
        name="lay_rows",
    )(table, *pieces)


def assemble(table, parent, own, other, row_factor):
    count = len(own) // 2
    rows, width = parent.shape
    size, sub = own[0].shape
    half = count // 2
    split = BLK // sub

    def body(*refs):
        sc, parent_ref = refs[:2]
        own_refs, other_refs = refs[2 : 2 + 2 * count], refs[2 + 2 * count : 2 + 4 * count]
        factor_ref, out, own_win, other_win, sems = refs[2 + 4 * count :]
        at = 0
        always, edges = [], []
        for refs_in, window in ((own_refs, own_win), (other_refs, other_win)):
            for m in range(count):
                home, halo = refs_in[m], refs_in[count + m]
                piece = sc[COL] ^ m
                main = half + piece
                side = jnp.maximum(piece - half, 0)
                low, high = pl.ds(0, EDGE), pl.ds(EDGE, size)
                always += [
                    pltpu.make_async_copy(home, window.at[main, high], sems.at[at]),
                    pltpu.make_async_copy(
                        halo.at[pl.ds(size, EDGE)], window.at[main, low], sems.at[at + 1]
                    ),
                ]
                edges += [
                    (
                        piece,
                        pltpu.make_async_copy(
                            halo.at[pl.ds(0, size)], window.at[side, high], sems.at[at + 2]
                        ),
                        pltpu.make_async_copy(
                            halo.at[pl.ds(size + EDGE, EDGE)],
                            window.at[side, low],
                            sems.at[at + 3],
                        ),
                    )
                ]
                at += 4
        for copy in always:
            copy.start()
        for piece, first, second in edges:

            @pl.when(piece >= half)
            def _():
                first.start()
                second.start()

        for copy in always:
            copy.wait()
        for piece, first, second in edges:

            @pl.when(piece >= half)
            def _():
                first.wait()
                second.wait()

        for q in range(PBD):
            cols = slice(q * BLK, (q + 1) * BLK)
            for p in range(HALF):
                lines = slice(p * BLK, (p + 1) * BLK)
                total = parent_ref[lines, cols]
                for window, row_base, col_base in (
                    (own_win, OWN_ROWS, OWN_COLS),
                    (other_win, OTHER_ROWS, OTHER_COLS),
                ):
                    down = sc[row_base + sc[SIB] * HALF + p]
                    across = sc[col_base + q]
                    start = jnp.maximum(across, 0) * split
                    pieces = [
                        window[start + i, span(jnp.maximum(down, 0), BLK), :] for i in range(split)
                    ]
                    block = pieces[0] if split == 1 else jnp.concatenate(pieces, axis=1)
                    total += jnp.where((down >= 0) & (across >= 0), block, 0.0)
                if q < PIV:
                    total = jnp.where(sc[COL] == 0, factor_ref[lines, cols], total)
                out[lines, cols] = total

    return pl.pallas_call(
        body,
        in_specs=[SMEM, VMEM] + [ANY] * (4 * count) + [VMEM],
        out_specs=VMEM,
        out_shape=f32(rows, width),
        scratch_shapes=[
            pltpu.VMEM((half + count, size + EDGE, sub), jnp.float32),
            pltpu.VMEM((half + count, size + EDGE, sub), jnp.float32),
            pltpu.SemaphoreType.DMA((8 * count,)),
        ],
        compiler_params=limit_for(sub, 14),
        name="assemble",
    )(table, parent, *own, *other, row_factor)


def finish(table, assembled, row_high, row_low, col_own, col_other):
    count = len(col_own)
    rows, width = assembled.shape
    piece_rows = col_own[0].shape[0]

    def body(*refs):
        sc = refs[0]
        own_refs = refs[1 : 1 + count]
        other_refs = refs[1 + count : 1 + 2 * count]
        base_ref, high_ref, low_ref, out, col_factor, result, sems = refs[1 + 2 * count :]
        own = gather_copies(sc, own_refs, col_factor.at[0], sems, piece_rows)
        other = gather_copies(sc, other_refs, col_factor.at[1], sems, piece_rows, count)
        for copy in own + other:
            copy.start()
        left = high_ref[...], low_ref[...]
        first_row = (sc[ROW] * 2 + sc[SIB]) * HALF
        first_col = sc[COL] * PBD
        writes = []
        for which, copies in ((0, own), (1, other)):
            for copy in copies:
                copy.wait()
            side = jnp.abs(sc[SIB] - which)
            lanes = span(side, rows)
            product = times_transpose(left, halves(col_factor[which]))
            for p in range(HALF):
                lines = slice(p * BLK, (p + 1) * BLK)
                for i in range(HALF):
                    cols = slice(i * BLK, (i + 1) * BLK)
                    here = span(side * HALF + i, BLK)
                    total = base_ref[lines, here]
                    inside = (first_col + side * HALF + i >= PIV) & (first_row + p >= PIV)
                    reduced = total - product[lines, cols]
                    result[which, lines, cols] = jnp.where(inside, reduced, total)
            write = pltpu.make_async_copy(
                result.at[which], out.at[:, lanes], sems.at[2 * count + which]
            )
            write.start()
            writes.append(write)
        for write in writes:
            write.wait()

    return pl.pallas_call(
        body,
        in_specs=[SMEM] + [ANY] * (2 * count) + [VMEM] * 3,
        out_specs=ANY,
        out_shape=f32(rows, width),
        scratch_shapes=[
            pltpu.VMEM((2, rows, PANEL), jnp.float32),
            pltpu.VMEM((2, rows, rows), jnp.float32),
            pltpu.SemaphoreType.DMA((2 * count + 2,)),
        ],
        compiler_params=limit_for(BLK, 16),
        name="finish",
    )(table, *col_own, *col_other, assembled, row_high, row_low)


def shards(child_front, child_panel, block_map, parent_front, pivot_inverse):
    count = lax.axis_size("col")
    front = child_front[0]
    panel = child_panel[0]
    sub = panel.shape[0]
    parent_rows, parent_cols = parent_front.shape
    parent_span = parent_cols // BLK
    deal = parent_rows // count

    table = lookup_table(block_map, parent_span)

    def over_col(values):
        got = []
        for k, value in zip(range(1, count), values):
            got.append(swapped(value, "col", k))
        return got

    def over_row(value):
        got = [value]
        for d in range(1, count):
            got.append(rotated(value, "row", d))
        return got

    def to_sibling(value):
        return swapped(value, "sib", 1)

    around = around_row(panel)
    rows = [panel] + over_col([panel] * (count - 1))
    slices, deals = cut_slices(table, front, parent_front, deal, sub)
    fronts = [slices[0]] + over_col(slices[1:])

    dealt = []
    for j in range(count):
        value = deals[j]
        dealt.append(lax.ppermute(value, "col", [(0, j)]) if j else value)

    *homes, edge, up = slice_products(table, rows, around, fronts)
    edge = shifted(edge, "row")
    up = shifted(up, "row")
    own = [homes[0]] + over_col(homes[1:])

    small = place_rows(table, homes, edge, deal)
    small = [small[0]] + over_col(small[1:])
    small_other = [to_sibling(value) for value in small]
    packed = pack_halo(table, homes, edge, up)
    own = own + [packed[0]] + over_col(packed[1:])
    factor = factor_slice(table, small, small_other, dealt, pivot_inverse)
    factors = over_row(factor)
    row_pieces = [factor] + over_col([factor] * (count - 1))

    row_factor, high, low = lay_rows(table, row_pieces)

    picked = pick_for_cols(table, factors, range(count))
    col_own = [picked[0]] + over_col(picked[1:])
    col_other = [to_sibling(value) for value in col_own]

    other = [to_sibling(value) for value in own]
    assembled = assemble(table, parent_front, own, other, row_factor)
    return finish(table, assembled, high, low, col_own, col_other)


def solution(mesh):
    in_specs = (
        P("sib", "row", "col"),
        P("sib", ("row", "col"), None),
        P(),
        P(("row", "sib"), "col"),
        P(),
    )
    out_specs = P(("row", "sib"), "col")

    return jax.shard_map(shards, mesh=mesh, in_specs=in_specs, out_specs=out_specs, check_vma=False)
```

```python
import jax
import jax.numpy as jnp
from jax import lax
from jax.experimental import pallas as pl
from jax.experimental.pallas import tpu as pltpu
from jax.sharding import PartitionSpec as P


BLK = 128
CBD = 4
PBD = 6
HB = 2
PIV = 4
PANEL = 512
HALF = PBD // 2
EDGE = HB * BLK


SMEM = pl.BlockSpec(memory_space=pltpu.SMEM)
VMEM = pl.BlockSpec(memory_space=pltpu.VMEM)
ANY = pl.BlockSpec(memory_space=pl.ANY)


def limit_for(sub, mebibytes):
    if sub < BLK:
        mebibytes = 56
    return pltpu.CompilerParams(vmem_limit_bytes=mebibytes << 20)


ROW, COL, SIB = 0, 1, 2
OWN_ROWS, OTHER_ROWS, OWN_COLS, OTHER_COLS = 3, 9, 15, 21
OWN_PIVOT, OTHER_PIVOT = 27, 31


def f32(*shape):
    return jax.ShapeDtypeStruct(shape, jnp.float32)


def halves(value):
    high = value.astype(jnp.bfloat16)
    low = (value - high.astype(jnp.float32)).astype(jnp.bfloat16)
    return high, low


def times_transpose(left, right):
    def dot(x, y):
        return lax.dot_general(
            x, y, (((1,), (1,)), ((), ())), preferred_element_type=jnp.float32
        )

    return dot(left[0], right[0]) + (dot(left[0], right[1]) + dot(left[1], right[0]))


def rotated(value, axis, steps):
    count = lax.axis_size(axis)
    return lax.ppermute(value, axis, [(i, (i + steps) % count) for i in range(count)])


def swapped(value, axis, mask):
    count = lax.axis_size(axis)
    return lax.ppermute(value, axis, [(i, i ^ mask) for i in range(count)])


def shifted(value, axis):
    count = lax.axis_size(axis)
    return lax.ppermute(value, axis, [(i, i + 1) for i in range(count - 1)])


def run_copies(copies):
    for copy in copies:
        copy.start()
    for copy in copies:
        copy.wait()


def span(index, size):
    return pl.ds(pl.multiple_of(index * size, size), size)


def gather_copies(table, pieces, target, sems, size, base=0):
    return [
        pltpu.make_async_copy(piece, target.at[span(table[COL] ^ k, size)], sems.at[base + k])
        for k, piece in enumerate(pieces)
    ]


def lookup_table(block_map, parent_span):
    def body(map_ref, out):
        row, col, sib = (lax.axis_index(axis) for axis in ("row", "col", "sib"))
        out[ROW], out[COL], out[SIB] = row, col, sib
        for base, sibling, group, slots in (
            (OWN_ROWS, sib, row, PBD),
            (OTHER_ROWS, 1 - sib, row, PBD),
            (OWN_COLS, sib, col, PBD),
            (OTHER_COLS, 1 - sib, col, PBD),
            (OWN_PIVOT, sib, 0, PIV),
            (OTHER_PIVOT, 1 - sib, 0, PIV),
        ):
            window = []
            for w in range(CBD + HB):
                block = group * CBD + w - HB
                landed = map_ref[sibling, jnp.maximum(block, 0)]
                window.append(jnp.where(block >= 0, landed, -1))
            for slot in range(slots):
                place = jnp.int32(-1)
                for w, landed in enumerate(window):
                    place = jnp.where(landed == group * parent_span + slot, w, place)
                out[base + slot] = place

    return pl.pallas_call(
        body,
        in_specs=[SMEM],
        out_specs=SMEM,
        out_shape=jax.ShapeDtypeStruct((OTHER_PIVOT + PIV,), jnp.int32),
        compiler_params=limit_for(BLK, 4),
        name="lookup_table",
    )(block_map)


def cut_slices(table, front, parent, deal, sub):
    size = front.shape[0]
    count = parent.shape[0] // deal
    aligned = sub % BLK == 0

    def body(sc, front_ref, parent_ref, *refs):
        fronts, deals, sems = refs[: count * aligned], refs[count * aligned : -1], refs[-1]
        copies = [
            pltpu.make_async_copy(
                front_ref.at[:, span(sc[COL] ^ m, sub)], out, sems.at[m]
            )
            for m, out in enumerate(fronts)
        ]
        copies += [
            pltpu.make_async_copy(
                parent_ref.at[pl.ds(j * deal, deal), pl.ds(0, PANEL)], out, sems.at[count + j]
            )
            for j, out in enumerate(deals)
        ]
        run_copies(copies)

    outs = pl.pallas_call(
        body,
        in_specs=[SMEM, ANY, ANY],
        out_specs=[VMEM] * (count * aligned + count),
        out_shape=[f32(size, sub)] * (count * aligned) + [f32(deal, PANEL)] * count,
        scratch_shapes=[pltpu.SemaphoreType.DMA((2 * count,))],
        compiler_params=limit_for(sub, 8),
        name="cut_slices",
    )(table, front, parent)
    fronts, deals = outs[: count * aligned], outs[count * aligned :]
    if not aligned:
        col = lax.axis_index("col")
        fronts = [
            lax.dynamic_slice_in_dim(front, (col ^ k) * sub, sub, axis=1) for k in range(count)
        ]
    return fronts, deals


def start_chosen(chosen, choices, target, sem):
    for d, choice in enumerate(choices):

        @pl.when(chosen == d)
        def _():
            pltpu.make_async_copy(choice, target, sem).start()


def turn_of(sc, mask, count):
    return lax.rem(sc[ROW] - (sc[COL] ^ mask) + count, count)


def slice_place(sc, mask, count):
    half = count // 2
    diff = sc[ROW] - (sc[COL] ^ mask)
    near = (diff < 0) & (-diff < half)
    return jnp.where(near, 2 * half - 1 - diff, jnp.abs(diff))


def around_row(value):
    count = lax.axis_size("row")
    half = count // 2
    middle = rotated(value, "row", half)
    below, above, far = [], [], []
    for d in range(1, half):
        below.append(lax.ppermute(value, "row", [(i, i + d) for i in range(count - d)]))
        above.append(lax.ppermute(value, "row", [(i + d, i) for i in range(count - d)]))
        pairs = [(i, i + d) for i in range(half, count - d)]
        pairs += [(i, i - d) for i in range(d, half)]
        far.append(lax.ppermute(middle, "row", pairs))
    return [value] + below + [middle] + far + above


def slice_products(table, rows, around, fronts):
    count = len(rows)
    many = len(around)
    sub, depth = rows[0].shape
    size = count * sub

    def body(*refs):
        sc = refs[0]
        row_refs = refs[1 : 1 + count]
        around_refs = refs[1 + count : 1 + count + many]
        front_refs = refs[1 + count + many : 1 + 2 * count + many]
        outs = refs[1 + 2 * count + many :][:count]
        sides = refs[1 + 3 * count + many :][:count]
        edge, up, row_buf, col_buf, sems = refs[1 + 4 * count + many :]
        places = [col_buf.at[m * sub : (m + 1) * sub] for m in range(count)]
        rows_in = gather_copies(sc, row_refs, row_buf, sems, sub)
        for copy in rows_in:
            copy.start()
        for m, place in enumerate(places):
            start_chosen(slice_place(sc, m, count), around_refs, place, sems.at[count + m])
        for copy in rows_in:
            copy.wait()
        left = halves(row_buf[...])
        for m, place in enumerate(places):
            pltpu.make_async_copy(around_refs[0], place, sems.at[count + m]).wait()
        product = times_transpose(left, halves(col_buf[...]))
        for m in range(count):
            group = sc[COL] ^ m
            part = front_refs[m][...] - product[:, m * sub : (m + 1) * sub]
            outs[m][...] = part

            @pl.when(group == 0)
            def _():
                edge[...] = part[-EDGE:]

            @pl.when(group > 0)
            def _():
                up[group - 1] = part[-EDGE:]

            for mask, side in enumerate(sides):

                @pl.when(group == jnp.maximum((sc[COL] ^ mask) - 1, 0))
                def _():
                    side[...] = part

    return pl.pallas_call(
        body,
        in_specs=[SMEM] + [ANY] * (count + many) + [VMEM] * count,
        out_specs=[VMEM] * (2 * count + 2),
        out_shape=[f32(size, sub)] * (2 * count) + [f32(EDGE, sub), f32(count - 1, EDGE, sub)],
        scratch_shapes=[
            pltpu.VMEM((size, depth), jnp.float32),
            pltpu.VMEM((size, depth), jnp.float32),
            pltpu.SemaphoreType.DMA((2 * count,)),
        ],
        compiler_params=limit_for(sub, 20),
        name="slice_products",
    )(table, *rows, *around, *fronts)


def pack_halo(table, edge, up):
    count = up.shape[0] + 1
    sub = edge.shape[1]

    def body(sc, edge_ref, up_ref, *refs):
        outs, sems = refs[:count], refs[count]
        places = [[out.at[pl.ds(i * EDGE, EDGE)] for i in range(2)] for out in outs]
        for m in range(count):
            group = sc[COL] ^ m
            for i, wanted in enumerate((group, jnp.maximum(group - 1, 0))):

                @pl.when(wanted == 0)
                def _():
                    pltpu.make_async_copy(edge_ref, places[m][i], sems.at[2 * m + i]).start()

                @pl.when(wanted > 0)
                def _():
                    pltpu.make_async_copy(
                        up_ref.at[jnp.maximum(wanted - 1, 0)], places[m][i], sems.at[2 * m + i]
                    ).start()

        for m in range(count):
            for i in range(2):
                pltpu.make_async_copy(edge_ref, places[m][i], sems.at[2 * m + i]).wait()

    return pl.pallas_call(
        body,
        in_specs=[SMEM] + [ANY] * 2,
        out_specs=[VMEM] * count,
        out_shape=[f32(2 * EDGE, sub)] * count,
        scratch_shapes=[pltpu.SemaphoreType.DMA((2 * count,))],
        compiler_params=limit_for(sub, 8),
        name="pack_halo",
    )(table, edge, up)


def to_next_group(packed):
    count = len(packed)
    half = count // 2

    def send(mask):
        pairs = [(i, i ^ mask) for i in range(half, count)]
        if mask > half:
            pairs = [(i, j) for i, j in pairs if j > 0 and (i, j) != (half, 1)]
        if not pairs:
            return None
        return lax.ppermute(packed[mask], "col", pairs)

    got = [packed[0]] + [send(mask) for mask in range(1, count)]
    forwarded = lax.ppermute(got[half], "col", [(0, 1)])
    direct = got[half + 1]
    if direct is not None:
        forwarded = jnp.where(lax.axis_index("col") == 1, forwarded, direct)
    got[half + 1] = forwarded
    return got


def pick_for_cols(table, pieces, masks):
    count = len(pieces)

    def body(*refs):
        sc = refs[0]
        ins = refs[1 : 1 + count]
        outs = refs[1 + count : -1]
        sems = refs[-1]
        for i, mask in enumerate(masks):
            start_chosen(turn_of(sc, mask, count), ins, outs[i], sems.at[i])
        for i in range(len(masks)):
            pltpu.make_async_copy(ins[0], outs[i], sems.at[i]).wait()

    return pl.pallas_call(
        body,
        in_specs=[SMEM] + [ANY] * count,
        out_specs=[VMEM] * len(masks),
        out_shape=[f32(*pieces[0].shape)] * len(masks),
        scratch_shapes=[pltpu.SemaphoreType.DMA((len(masks),))],
        compiler_params=limit_for(BLK, 16),
        name="pick_for_cols",
    )(table, *pieces)


def place_rows(table, homes, edge, deal):
    count = len(homes)
    size, width = homes[0].shape
    rows = HALF * BLK

    def body(*refs):
        sc = refs[0]
        home_refs = refs[1 : 1 + count]
        edge_ref = refs[1 + count]
        outs = refs[2 + count : 2 + 2 * count]
        window, placed, sems = refs[2 + 2 * count :]
        main = window.at[pl.ds(EDGE, size)]
        start_chosen(sc[COL], home_refs, main, sems.at[0])
        copy = pltpu.make_async_copy(edge_ref, window.at[pl.ds(0, EDGE)], sems.at[1])
        copy.start()
        copy.wait()
        pltpu.make_async_copy(home_refs[0], main, sems.at[0]).wait()
        for which, half in ((0, sc[SIB]), (1, 1 - sc[SIB])):
            for slot in range(HALF):
                place = sc[OWN_ROWS + half * HALF + slot]
                block = window[span(jnp.maximum(place, 0), BLK), :]
                lines = slice(slot * BLK, (slot + 1) * BLK)
                placed[which, lines, :] = jnp.where(place >= 0, block, 0.0)
        for m, out in enumerate(outs):
            for which in range(2):
                out[which] = placed[which, span(sc[COL] ^ m, deal), :]

    return pl.pallas_call(
        body,
        in_specs=[SMEM] + [ANY] * (count + 1),
        out_specs=[VMEM] * count,
        out_shape=[f32(2, deal, width)] * count,
        scratch_shapes=[
            pltpu.VMEM((size + EDGE, width), jnp.float32),
            pltpu.VMEM((2, rows, width), jnp.float32),
            pltpu.SemaphoreType.DMA((2,)),
        ],
        compiler_params=limit_for(width, 8),
        name="place_rows",
    )(table, *homes, edge)


def factor_slice(table, small, small_other, dealt, pivot_inverse):
    count = len(small)
    _, rows, sub = small[0].shape

    def body(*refs):
        sc = refs[0]
        pieces = refs[1 : 1 + count]
        other_refs = refs[1 + count : 1 + 2 * count]
        deal_refs = refs[1 + 2 * count : 1 + 3 * count]
        inverse_ref, out, order, child, sums, sems = refs[1 + 3 * count :]
        start_chosen(sc[COL], deal_refs, sums, sems.at[2 * count])
        copies = []
        for k in range(count):
            place = order.at[sc[COL] ^ k]
            copies += [
                pltpu.make_async_copy(pieces[k].at[0], place.at[0], sems.at[2 * k]),
                pltpu.make_async_copy(other_refs[k].at[1], place.at[1], sems.at[2 * k + 1]),
            ]
        run_copies(copies)
        for j in range(count):
            block, lane = divmod(j * sub, BLK)
            for sibling in range(2):
                child[sibling, block, :, lane : lane + sub] = order[j, sibling]
        pltpu.make_async_copy(deal_refs[0], sums, sems.at[2 * count]).wait()
        for p in range(PIV):
            lanes = slice(p * BLK, (p + 1) * BLK)
            added = sums[:, lanes]
            for sibling, base in ((0, OWN_PIVOT), (1, OTHER_PIVOT)):
                place = sc[base + p]
                block = child[sibling, jnp.maximum(place - HB, 0)]
                added += jnp.where(place >= HB, block, 0.0)
            sums[:, lanes] = added
        out[...] = times_transpose(halves(sums[...]), halves(inverse_ref[...]))

    return pl.pallas_call(
        body,
        in_specs=[SMEM] + [ANY] * (3 * count) + [VMEM],
        out_specs=VMEM,
        out_shape=f32(rows, PANEL),
        scratch_shapes=[
            pltpu.VMEM((count, 2, rows, sub), jnp.float32),
            pltpu.VMEM((2, PIV, rows, BLK), jnp.float32),
            pltpu.VMEM((rows, PANEL), jnp.float32),
            pltpu.SemaphoreType.DMA((2 * count + 1,)),
        ],
        compiler_params=limit_for(sub, 16),
        name="factor_slice",
    )(table, *small, *small_other, *dealt, pivot_inverse)


def lay_rows(table, pieces):
    count = len(pieces)
    piece_rows, width = pieces[0].shape
    rows = count * piece_rows

    def body(*refs):
        sc = refs[0]
        ins = refs[1 : 1 + count]
        out, high, low, sems = refs[1 + count :]
        run_copies(gather_copies(sc, ins, out, sems, piece_rows))
        high[...], low[...] = halves(out[...])

    part = jax.ShapeDtypeStruct((rows, width), jnp.bfloat16)
    return pl.pallas_call(
        body,
        in_specs=[SMEM] + [ANY] * count,
        out_specs=[VMEM] * 3,
        out_shape=[f32(rows, width), part, part],
        scratch_shapes=[pltpu.SemaphoreType.DMA((count,))],
        compiler_params=limit_for(BLK, 8),
        name="lay_rows",
    )(table, *pieces)


def assemble(table, parent, own, other, row_factor):
    count = len(own) // 3
    rows, width = parent.shape
    size, sub = own[0].shape
    half = count // 2
    split = BLK // sub

    def body(*refs):
        sc, parent_ref = refs[:2]
        own_refs, other_refs = refs[2 : 2 + 3 * count], refs[2 + 3 * count : 2 + 6 * count]
        factor_ref, out, own_win, other_win, sems = refs[2 + 6 * count :]
        low, high = pl.ds(0, EDGE), pl.ds(EDGE, size)
        always, edges = [], []
        at = 0
        for refs_in, window in ((own_refs, own_win), (other_refs, other_win)):
            for m in range(count):
                home, above, before = (refs_in[i * count + m] for i in range(3))
                piece = sc[COL] ^ m
                main = half + piece
                side = jnp.maximum(piece - half, 0)
                always += [
                    pltpu.make_async_copy(home, window.at[main, high], sems.at[at]),
                    pltpu.make_async_copy(
                        above.at[low], window.at[main, low], sems.at[at + 1]
                    ),
                ]
                edges += [
                    (
                        piece,
                        pltpu.make_async_copy(before, window.at[side, high], sems.at[at + 2]),
                        pltpu.make_async_copy(
                            above.at[pl.ds(EDGE, EDGE)], window.at[side, low], sems.at[at + 3]
                        ),
                    )
                ]
                at += 4
        for copy in always:
            copy.start()
        for piece, first, second in edges:

            @pl.when(piece >= half)
            def _():
                first.start()
                second.start()

        for copy in always:
            copy.wait()
        for piece, first, second in edges:

            @pl.when(piece >= half)
            def _():
                first.wait()
                second.wait()

        for q in range(PBD):
            cols = slice(q * BLK, (q + 1) * BLK)
            for p in range(HALF):
                lines = slice(p * BLK, (p + 1) * BLK)
                total = parent_ref[lines, cols]
                for window, row_base, col_base in (
                    (own_win, OWN_ROWS, OWN_COLS),
                    (other_win, OTHER_ROWS, OTHER_COLS),
                ):
                    down = sc[row_base + sc[SIB] * HALF + p]
                    across = sc[col_base + q]
                    start = jnp.maximum(across, 0) * split
                    pieces = [
                        window[start + i, span(jnp.maximum(down, 0), BLK), :] for i in range(split)
                    ]
                    block = pieces[0] if split == 1 else jnp.concatenate(pieces, axis=1)
                    total += jnp.where((down >= 0) & (across >= 0), block, 0.0)
                if q < PIV:
                    total = jnp.where(sc[COL] == 0, factor_ref[lines, cols], total)
                out[lines, cols] = total

    return pl.pallas_call(
        body,
        in_specs=[SMEM, VMEM] + [ANY] * (6 * count) + [VMEM],
        out_specs=VMEM,
        out_shape=f32(rows, width),
        scratch_shapes=[
            pltpu.VMEM((half + count, size + EDGE, sub), jnp.float32),
            pltpu.VMEM((half + count, size + EDGE, sub), jnp.float32),
            pltpu.SemaphoreType.DMA((8 * count,)),
        ],
        compiler_params=limit_for(sub, 14),
        name="assemble",
    )(table, parent, *own, *other, row_factor)


def finish(table, assembled, row_high, row_low, col_own, col_other):
    count = len(col_own)
    rows, width = assembled.shape
    piece_rows = col_own[0].shape[0]

    def body(*refs):
        sc = refs[0]
        own_refs = refs[1 : 1 + count]
        other_refs = refs[1 + count : 1 + 2 * count]
        base_ref, high_ref, low_ref, out, col_factor, result, sems = refs[1 + 2 * count :]
        own = gather_copies(sc, own_refs, col_factor.at[0], sems, piece_rows)
        other = gather_copies(sc, other_refs, col_factor.at[1], sems, piece_rows, count)
        for copy in own + other:
            copy.start()
        left = high_ref[...], low_ref[...]
        first_row = (sc[ROW] * 2 + sc[SIB]) * HALF
        first_col = sc[COL] * PBD
        writes = []
        for which, copies in ((0, own), (1, other)):
            for copy in copies:
                copy.wait()
            side = jnp.abs(sc[SIB] - which)
            lanes = span(side, rows)
            product = times_transpose(left, halves(col_factor[which]))
            for p in range(HALF):
                lines = slice(p * BLK, (p + 1) * BLK)
                for i in range(HALF):
                    cols = slice(i * BLK, (i + 1) * BLK)
                    here = span(side * HALF + i, BLK)
                    total = base_ref[lines, here]
                    inside = (first_col + side * HALF + i >= PIV) & (first_row + p >= PIV)
                    reduced = total - product[lines, cols]
                    result[which, lines, cols] = jnp.where(inside, reduced, total)
            write = pltpu.make_async_copy(
                result.at[which], out.at[:, lanes], sems.at[2 * count + which]
            )
            write.start()
            writes.append(write)
        for write in writes:
            write.wait()

    return pl.pallas_call(
        body,
        in_specs=[SMEM] + [ANY] * (2 * count) + [VMEM] * 3,
        out_specs=ANY,
        out_shape=f32(rows, width),
        scratch_shapes=[
            pltpu.VMEM((2, rows, PANEL), jnp.float32),
            pltpu.VMEM((2, rows, rows), jnp.float32),
            pltpu.SemaphoreType.DMA((2 * count + 2,)),
        ],
        compiler_params=limit_for(BLK, 16),
        name="finish",
    )(table, *col_own, *col_other, assembled, row_high, row_low)


def shards(child_front, child_panel, block_map, parent_front, pivot_inverse):
    count = lax.axis_size("col")
    front = child_front[0]
    panel = child_panel[0]
    sub = panel.shape[0]
    parent_rows, parent_cols = parent_front.shape
    parent_span = parent_cols // BLK
    deal = parent_rows // count

    table = lookup_table(block_map, parent_span)

    def over_col(values):
        got = []
        for k, value in zip(range(1, count), values):
            got.append(swapped(value, "col", k))
        return got

    def over_row(value):
        got = [value]
        for d in range(1, count):
            got.append(rotated(value, "row", d))
        return got

    def to_sibling(value):
        return swapped(value, "sib", 1)

    around = around_row(panel)
    rows = [panel] + over_col([panel] * (count - 1))
    slices, deals = cut_slices(table, front, parent_front, deal, sub)
    fronts = [slices[0]] + over_col(slices[1:])

    dealt = []
    for j in range(count):
        value = deals[j]
        dealt.append(lax.ppermute(value, "col", [(0, j)]) if j else value)

    *slices, edge, up = slice_products(table, rows, around, fronts)
    homes, sides = slices[:count], slices[count:]
    edge = shifted(edge, "row")
    up = shifted(up, "row")
    own = [homes[0]] + over_col(homes[1:])

    small = place_rows(table, homes, edge, deal)
    small = [small[0]] + over_col(small[1:])
    small_other = [to_sibling(value) for value in small]
    above = pack_halo(table, edge, up)
    own = own + [above[0]] + over_col(above[1:]) + to_next_group(sides)
    factor = factor_slice(table, small, small_other, dealt, pivot_inverse)
    factors = over_row(factor)
    row_pieces = [factor] + over_col([factor] * (count - 1))

    row_factor, high, low = lay_rows(table, row_pieces)

    picked = pick_for_cols(table, factors, range(count))
    col_own = [picked[0]] + over_col(picked[1:])
    col_other = [to_sibling(value) for value in col_own]

    other = [to_sibling(value) for value in own]
    assembled = assemble(table, parent_front, own, other, row_factor)
    return finish(table, assembled, high, low, col_own, col_other)


def solution(mesh):
    in_specs = (
        P("sib", "row", "col"),
        P("sib", ("row", "col"), None),
        P(),
        P(("row", "sib"), "col"),
        P(),
    )
    out_specs = P(("row", "sib"), "col")

    return jax.shard_map(shards, mesh=mesh, in_specs=in_specs, out_specs=out_specs, check_vma=False)
```
